32 devices in a mesh: dp: 2 (over core), expert: 4 (over y, x), shard: 4 (over z).
Axes of the slice: x: 2, y: 2, z: 4, core: 2. Of those that a mesh axis runs over, the one named last changes fastest.
Arguments:
- tokens: bfloat16 [2, 32, 64, 2048], P(None, ('dp', 'expert', 'shard')), may hold values from -6 to 6
- cotangent: bfloat16 [2, 32, 64, 2048], P(None, ('dp', 'expert', 'shard')), may hold values from -6 to 6
- lengths: int32 [2, 32], P(None, ('dp', 'expert', 'shard')), may hold values from 16 to 64, as said below
- routes: int32 [2, 32, 64, 8], P(None, ('dp', 'expert', 'shard')), may hold values from 0 to 15, all different within a row; in each aligned block of 64 rows (0 to 63, 64 to 127, ..., all dimensions but the last counted through in order) at most 64 rows name the same one
- w_query: bfloat16 [2048, 2048], P('shard'), may hold values from -0.125 to 0.125
- w_key: bfloat16 [2048, 2048], P('shard'), may hold values from -0.125 to 0.125
- w_value: bfloat16 [2048, 2048], P('shard'), may hold values from -0.125 to 0.125
- w_out: bfloat16 [2048, 2048], P('shard'), may hold values from -0.5 to 0.5
- w_router: bfloat16 [2048, 16], P('shard'), may hold values from -0.0625 to 0.0625
- g_attn: bfloat16 [2048], P('shard'), may hold values from 0.25 to 1.75
- g_ffn: bfloat16 [2048], P('shard'), may hold values from 0.25 to 1.75
- g_query: bfloat16 [2048], P('shard'), may hold values from 0.25 to 1.75
- g_key: bfloat16 [2048], P('shard'), may hold values from 0.25 to 1.75
- w_gate: bfloat16 [16, 2048, 1024], P(('expert', 'shard'), None, 'dp'), may hold values from -0.125 to 0.125
- w_up: bfloat16 [16, 2048, 1024], P(('expert', 'shard'), None, 'dp'), may hold values from -0.125 to 0.125
- w_down: bfloat16 [16, 1024, 2048], P(('expert', 'shard'), 'dp'), may hold values from -1.5 to 1.5
Outputs:
- mixed_out: bfloat16 [2, 32, 64, 2048], P(None, ('dp', 'expert', 'shard'))
- grad_tokens: float32 [2, 32, 64, 2048], P(None, ('dp', 'expert', 'shard'))
- grad_w_query: float32 [2048, 2048], P('shard')
- grad_w_key: float32 [2048, 2048], P('shard')
- grad_w_value: float32 [2048, 2048], P('shard')
- grad_w_out: float32 [2048, 2048], P('shard')
- grad_w_router: float32 [2048, 16], P('shard')
- grad_g_attn: float32 [2048], P('shard')
- grad_g_ffn: float32 [2048], P('shard')
- grad_g_query: float32 [2048], P('shard')
- grad_g_key: float32 [2048], P('shard')
- grad_w_gate: float32 [16, 2048, 1024], P(('expert', 'shard'), None, 'dp')
- grad_w_up: float32 [16, 2048, 1024], P(('expert', 'shard'), None, 'dp')
- grad_w_down: float32 [16, 1024, 2048], P(('expert', 'shard'), 'dp')
The draws below stay inside these ranges and needn't reach their ends.
Inputs may be any that keep to these rules, and one draw needn't show every extreme that they name: `routes`: each row names 8 different experts. Among the 64 rows of one sequence no expert is named more than 64 times, and in some sequences an expert is named exactly 64 times. `lengths`: in every micro-batch at least one sequence has the full length 64.
All inputs are finite; a program needn't handle non-finite values.
Results may differ from the reference program's by a relative error of at most 0.022.
Values may be sent and summed in bfloat16 or wider, within the bound.
A program may use at most 320 MiB of HBM per device.

```python
import math
import jax
import jax.numpy as jnp
import numpy as np
from jax import lax

D = 2048
HEADS = 16
HDIM = 128
F = 1024
TOP = 8
SEQ = 64
MICRO = 2
EXPERTS = 16
SEQS = 32
CAP = 64


def draw_lengths(key, part):
    first_key, second_key = jax.random.split(jax.random.fold_in(key, 17))
    drawn = jax.random.randint(first_key, (MICRO, SEQS), SEQ // 4, SEQ + 1)
    picked = jax.random.randint(second_key, (MICRO, 1), 0, SEQS)
    full_row = jnp.arange(SEQS)[None, :] == picked
    return jnp.where(full_row, SEQ, drawn).astype(jnp.int32)


def block_scale(own_key, extent, cuts, low, largest):
    level = 1.0
    for axis_at, parts in cuts:
        heights = jax.random.uniform(jax.random.fold_in(jax.random.fold_in(own_key, 6), axis_at), (parts,), jnp.float32, low / len(cuts), largest / len(cuts))
        level = level * jnp.repeat(jnp.exp(heights), extent[axis_at] // parts).reshape((-1,) + (1,) * (len(extent) - 1 - axis_at))
    return level


def deal_out(stream_key, own, number, rows, count, top, most, lean):
    order = jax.random.permutation(stream_key, count)
    packed, usual = portions_of(count, rows * top, most, lean, True), portions_of(count, rows * top, most, lean, False)
    places = jnp.arange(count)

    def named(tallies, rotation):
        used = int((tallies > 0).sum())
        fixed = max(1, used // 4)
        moved = fixed + (places - fixed + rotation * (used - fixed)) % max(1, count - fixed)
        return jnp.zeros((count,), jnp.int32).at[order[jnp.where(places < fixed, places, moved)]].set(jnp.asarray(tallies, jnp.int32))

    tallies = jnp.where(number % 4 == 0, named(packed, number // 4), named(usual, number - number // 4 - 1))
    mixed = jax.random.permutation(jax.random.fold_in(own, 3), count)
    giver, receiver = mixed[0:count // 2 * 2:2], mixed[1:count // 2 * 2:2]
    slack = jnp.minimum(tallies[giver] - 1, most - tallies[receiver]) // 2
    slack = jnp.where((giver == order[0]) | (receiver == order[0]) | (tallies[receiver] == 0), 0, jnp.maximum(slack, 0))
    moved = jax.random.randint(jax.random.fold_in(own, 4), (count // 2,), 0, 1 << 20) % (slack + 1)
    tallies = tallies.at[giver].add(-moved).at[receiver].add(moved)
    labels = jnp.searchsorted(jnp.cumsum(tallies), jnp.arange(rows * top), side="right").astype(jnp.int32)
    grid = labels.reshape(top, rows).T
    grid = grid[jax.random.permutation(jax.random.fold_in(own, 1), rows)]
    rotation = jax.random.randint(jax.random.fold_in(own, 2), (rows, 1), 0, top)
    return jnp.take_along_axis(grid, (jnp.arange(top)[None, :] + rotation) % top, axis=1)


def portions_of(amount, total, limit, lean, full):
    portions = [(1 << 20) // math.isqrt(standing ** lean) + 1 for standing in range(1, amount + 1)]
    largest = limit if full else min(limit, max(-(-total // amount), total * portions[0] // sum(portions)))
    least = 1 if total - largest >= amount - 1 else 0
    given, spare = [largest] + [least] * (amount - 1), total - largest - least * (amount - 1)
    while spare > 0:
        movable = [i for i in range(1, amount) if given[i] < largest] or [i for i in range(1, amount) if given[i] < limit]
        whole, remaining = sum([portions[i] for i in movable]), spare
        for i in movable:
            more = min(limit - given[i], max(1, remaining * portions[i] // whole), spare)
            given[i] = given[i] + more
            spare = spare - more
    return np.array(given)


def normal_values(rng, extent, spread, bound, pieces=(), held_as=jnp.bfloat16):
    values = spread * jax.random.normal(rng, extent, jnp.float32)
    if pieces:
        values = values * block_scale(rng, extent, pieces, -0.22, 0.18)
    return jnp.clip(values, -bound, bound).astype(held_as)


def setup_inputs(seed: int = 0) -> dict:
    arg_keys = jax.random.split(jax.random.key(seed), 17)
    tokens = normal_values(arg_keys[0], (MICRO, SEQS, SEQ, D), 1.0, 6.0, ((1, 32),))
    cotangent = normal_values(arg_keys[1], (MICRO, SEQS, SEQ, D), 1.0, 6.0, ((1, 32),))
    lengths = draw_lengths(jax.random.fold_in(arg_keys[16], 71), 0)
    routes_keys = jax.random.split(jax.random.fold_in(arg_keys[3], 1), MICRO * SEQS * SEQ // SEQ)
    routes_turns = jax.random.permutation(jax.random.fold_in(arg_keys[3], 3), MICRO * SEQS * SEQ // SEQ)
    routes = jax.vmap(lambda own, number: deal_out(jax.random.fold_in(arg_keys[3], 2), own, number, SEQ, EXPERTS, TOP, CAP, 2))(routes_keys, routes_turns).reshape((MICRO, SEQS, SEQ, TOP))
    w_query = normal_values(arg_keys[4], (D, D), D ** -0.5, 0.125, ((0, 4),))
    w_key = normal_values(arg_keys[5], (D, D), D ** -0.5, 0.125, ((0, 4),))
    w_value = normal_values(arg_keys[6], (D, D), D ** -0.5, 0.125, ((0, 4),))
    w_out = normal_values(arg_keys[7], (D, D), (D // 16) ** -0.5, 0.5, ((0, 4),))
    w_router = normal_values(arg_keys[8], (D, EXPERTS), (4 * D) ** -0.5, 0.0625, ((0, 4),))
    g_attn = jnp.clip(1.0 + 0.15 * jax.random.normal(arg_keys[9], (D,), jnp.float32), 0.25, 1.75).astype(jnp.bfloat16)
    g_ffn = jnp.clip(1.0 + 0.15 * jax.random.normal(arg_keys[10], (D,), jnp.float32), 0.25, 1.75).astype(jnp.bfloat16)
    g_query = jnp.clip(1.0 + 0.15 * jax.random.normal(arg_keys[11], (D,), jnp.float32), 0.25, 1.75).astype(jnp.bfloat16)
    g_key = jnp.clip(1.0 + 0.15 * jax.random.normal(arg_keys[12], (D,), jnp.float32), 0.25, 1.75).astype(jnp.bfloat16)
    w_gate = normal_values(arg_keys[13], (EXPERTS, D, F), D ** -0.5, 0.125, ((0, 16), (2, 2)))
    w_up = normal_values(arg_keys[14], (EXPERTS, D, F), D ** -0.5, 0.125, ((0, 16), (2, 2)))
    w_down = normal_values(arg_keys[15], (EXPERTS, F, D), (max(1, 4 * F // (EXPERTS * EXPERTS))) ** -0.5, 1.5, ((0, 16), (1, 2)))
    return dict(tokens=tokens, cotangent=cotangent, lengths=lengths, routes=routes, w_query=w_query, w_key=w_key, w_value=w_value, w_out=w_out, w_router=w_router, g_attn=g_attn, g_ffn=g_ffn, g_query=g_query, g_key=g_key, w_gate=w_gate, w_up=w_up, w_down=w_down)


EPSILON = 1e-05
HIGHEST = lax.Precision.HIGHEST

@jax.custom_vjp
def low(v):
    return lax.optimization_barrier(v.astype(jnp.bfloat16)).astype(jnp.float32)

@jax.custom_vjp
def low_back(v):
    return v

def low_keep(v):
    return (low(v), None)

def low_pass(kept, grad):
    return (grad,)

def back_keep(v):
    return (v, None)

def back_low(kept, grad):
    return (low(grad),)
low.defvjp(low_keep, low_pass)
low_back.defvjp(back_keep, back_low)

def rms_norm(values, gain_vec):
    factor = lax.rsqrt(lax.optimization_barrier(jnp.mean(values * values, axis=-1, keepdims=True)) + EPSILON)
    return values * factor * gain_vec

def rope_tables(seq_count, head_size):
    half_dim = head_size // 2
    freqs = 10000.0 ** (-2.0 * jnp.arange(half_dim).astype(jnp.float32) / head_size)
    angles = jnp.arange(seq_count).astype(jnp.float32)[:, None] * freqs[None, :]
    cosine_table = jnp.concatenate([jnp.cos(angles), jnp.cos(angles)], axis=-1)
    sine_table = jnp.concatenate([jnp.sin(angles), jnp.sin(angles)], axis=-1)
    return (cosine_table, sine_table)

def rotate(head_rows, cosine_table, sine_table):
    half_dim = head_rows.shape[-1] // 2
    turned = jnp.concatenate([-head_rows[..., half_dim:], head_rows[..., :half_dim]], axis=-1)
    return head_rows * cosine_table[:, None, :] + turned * sine_table[:, None, :]

def softmax_rows(scores):
    shifted = jnp.exp(scores - lax.optimization_barrier(jnp.max(scores, axis=-1, keepdims=True)))
    return shifted / lax.optimization_barrier(jnp.sum(shifted, axis=-1, keepdims=True))

def sequence(inputs, length, route_ids, params):
    w_query, w_key, w_value, w_out, w_router, g_attn, g_ffn, g_query, g_key, w_gate, w_up, w_down = params
    seq_count = inputs.shape[0]
    normed = low(rms_norm(inputs, g_attn))
    query_raw = low_back(jnp.dot(normed, w_query, precision=HIGHEST))
    key_raw = low_back(jnp.dot(normed, w_key, precision=HIGHEST))
    value_low = low(low_back(jnp.dot(normed, w_value, precision=HIGHEST))).reshape(seq_count, HEADS, HDIM)
    cosine_table, sine_table = rope_tables(seq_count, HDIM)
    query_low = low(rotate(rms_norm(query_raw, g_query).reshape(seq_count, HEADS, HDIM), cosine_table, sine_table))
    key_low = low(rotate(rms_norm(key_raw, g_key).reshape(seq_count, HEADS, HDIM), cosine_table, sine_table))
    places = jnp.arange(seq_count)
    allowed = (places[None, :] <= places[:, None]) & (places[None, :] < length)
    scores = low_back(jnp.einsum('qhd,khd->hqk', query_low, key_low, precision=HIGHEST) * HDIM ** (-0.5))
    attn_probs = softmax_rows(jnp.where(allowed[None], scores, -1e+30))
    mixed_low = jnp.einsum('hqk,khd->qhd', low(attn_probs), value_low, precision=HIGHEST).reshape(seq_count, D)
    mixed_low = low(low_back(mixed_low))
    hidden_state = inputs + low_back(jnp.dot(mixed_low, w_out, precision=HIGHEST))
    ffn_in = low(rms_norm(hidden_state, g_ffn))
    router = softmax_rows(low_back(jnp.dot(ffn_in, w_router, precision=HIGHEST)))
    chosen = route_ids[:, :, None] == jnp.arange(EXPERTS)[None, None, :]
    combine = lax.optimization_barrier(jnp.sum(jnp.where(chosen, router[:, None, :], 0.0), axis=1))
    expert_token_rows = low_back(jnp.broadcast_to(ffn_in[None], (EXPERTS, seq_count, D)))
    gate_pre = low_back(jnp.einsum('etd,edf->etf', expert_token_rows, w_gate, precision=HIGHEST))
    up_value = low_back(jnp.einsum('etd,edf->etf', expert_token_rows, w_up, precision=HIGHEST))
    inner_activation = low(gate_pre * jax.nn.sigmoid(gate_pre) * up_value)
    expert_out = low_back(low(jnp.einsum('etf,efd->etd', inner_activation, w_down, precision=HIGHEST)))
    return hidden_state + jnp.einsum('te,etd->td', combine, expert_out, precision=HIGHEST)

def reference(tokens, cotangent, lengths, routes, w_query, w_key, w_value, w_out, w_router, g_attn, g_ffn, g_query, g_key, w_gate, w_up, w_down):
    params = tuple((item.astype(jnp.float32) for item in (w_query, w_key, w_value, w_out, w_router, g_attn, g_ffn, g_query, g_key, w_gate, w_up, w_down)))
    flat_tokens = tokens.astype(jnp.float32).reshape(-1, SEQ, D)
    flat_lengths = lengths.reshape(-1).astype(jnp.int32)
    flat_routes = routes.reshape(-1, SEQ, TOP).astype(jnp.int32)
    checked = jax.checkpoint(sequence)

    def forward(inputs, weights):

        def step(carry, item):
            return (carry, checked(item[0], item[1], item[2], weights))
        return lax.scan(step, None, (inputs, flat_lengths, flat_routes))[1]
    outputs, pullback = jax.vjp(forward, flat_tokens, params)
    live_mask = (jnp.arange(SEQ)[None, :] < flat_lengths[:, None]).astype(jnp.float32)
    seeds = cotangent.astype(jnp.float32).reshape(-1, SEQ, D) * live_mask[:, :, None]
    grads_in, grads_w = pullback(seeds)
    full_shape = tokens.shape
    return (outputs.reshape(full_shape).astype(jnp.bfloat16), grads_in.reshape(full_shape), grads_w[0], grads_w[1], grads_w[2], grads_w[3], grads_w[4], grads_w[5], grads_w[6], grads_w[7], grads_w[8], grads_w[9], grads_w[10], grads_w[11])
```

```python
import functools

import jax
import jax.numpy as jnp
from jax import lax
from jax.experimental import pallas as pl
from jax.experimental.pallas import tpu as pltpu
from jax.sharding import PartitionSpec as P

HEADS = 16
HDIM = 128


EPSILON = 1e-05


def matmul(left, right):
    return jnp.dot(left, right, preferred_element_type=jnp.float32)


def times_transposed(left, right):
    return lax.dot_general(
        left, right, (((1,), (1,)), ((), ())), preferred_element_type=jnp.float32
    )


def transposed_times(left, right):
    return lax.dot_general(
        left, right, (((0,), (0,)), ((), ())), preferred_element_type=jnp.float32
    )


def rms_norm(values, gain_vec):
    factor = lax.rsqrt(jnp.mean(values * values, axis=-1, keepdims=True) + EPSILON)
    return values * factor * gain_vec


def norm_back(values, gain_vec, incoming):
    factor = lax.rsqrt(jnp.mean(values * values, axis=-1, keepdims=True) + EPSILON)
    unit_rows = values * factor
    weighted = incoming * gain_vec
    d_values = factor * (
        weighted - unit_rows * jnp.mean(weighted * unit_rows, axis=-1, keepdims=True)
    )
    return (d_values, jnp.sum(incoming * unit_rows, axis=0))


def rope_tables(seq_count, head_size):
    half_dim = head_size // 2
    freqs = 10000.0 ** (-2.0 * jnp.arange(half_dim).astype(jnp.float32) / head_size)
    angles = jnp.arange(seq_count).astype(jnp.float32)[:, None] * freqs[None, :]
    cosine_table = jnp.concatenate([jnp.cos(angles), jnp.cos(angles)], axis=-1)
    sine_table = jnp.concatenate([jnp.sin(angles), jnp.sin(angles)], axis=-1)
    return (cosine_table, sine_table)


def rotate(head_rows, cosine_table, sine_table):
    half_dim = head_rows.shape[-1] // 2
    turned = jnp.concatenate([-head_rows[..., half_dim:], head_rows[..., :half_dim]], axis=-1)
    return head_rows * cosine_table[:, None, :] + turned * sine_table[:, None, :]


def rotate_back(incoming, cosine_table, sine_table):
    half_dim = incoming.shape[-1] // 2
    moved_part = incoming * sine_table[:, None, :]
    turned = jnp.concatenate([moved_part[..., half_dim:], -moved_part[..., :half_dim]], axis=-1)
    return incoming * cosine_table[:, None, :] + turned


def softmax_rows(scores):
    shifted = jnp.exp(scores - jnp.max(scores, axis=-1, keepdims=True))
    return shifted / jnp.sum(shifted, axis=-1, keepdims=True)


MESH_ID = pl.DeviceIdType.MESH
EXTRA = 128
ANY = pl.BlockSpec(memory_space=pl.ANY)


def place():
    return lax.axis_index("dp"), lax.axis_index("expert"), lax.axis_index("shard")


def x_of(e):
    return e + 1 - 2 * lax.rem(e, 2)


def y_of(e):
    return lax.rem(e + 2, 4)


def greet(peers):
    barrier = pltpu.get_barrier_semaphore()
    for peer in peers:
        pl.semaphore_signal(barrier, inc=1, device_id=peer, device_id_type=MESH_ID)
    pl.semaphore_wait(barrier, len(peers))


class Copies:
    def __init__(self):
        self.started = []

    def send(self, src, dst, send_sem, recv_sem, device, when=None):
        copy = pltpu.make_async_remote_copy(
            src_ref=src,
            dst_ref=dst,
            send_sem=send_sem,
            recv_sem=recv_sem,
            device_id=device,
            device_id_type=MESH_ID,
        )
        if when is None:
            copy.start()
        else:
            pl.when(when)(copy.start)
        self.started.append((copy, when))

    def drain(self):
        for copy, when in self.started:
            if when is None:
                copy.wait_send()
            else:
                pl.when(when)(copy.wait_send)


def arrived(ref, sem, other):
    pltpu.make_async_remote_copy(
        src_ref=ref,
        dst_ref=ref,
        send_sem=sem,
        recv_sem=sem,
        device_id=other,
        device_id_type=MESH_ID,
    ).wait_recv()


class SemPool:
    def __init__(self, ref):
        self.ref = ref
        self.used = 0

    def take(self):
        self.used += 1
        assert self.used <= self.ref.shape[0]
        return self.ref.at[self.used - 1]


class Item:
    def __init__(self, own, dst, recv, skip=False, cross=None, cross_recv=None):
        self.own, self.dst, self.recv = own, dst, recv
        self.skip, self.cross, self.cross_recv = skip, cross, cross_recv


def gather_items(items, copies, pool):
    dp, e, z = place()
    px, py = x_of(e), y_of(e)
    firsts, seconds = (px, py), (py, px)
    diag = x_of(y_of(e))

    def onward(item, h, ee, zz, targets, when):
        ref = item.dst(zz, ee, h)
        sem = item.recv.at[h, ee * 4 + zz]
        for target, cond in targets:
            copies.send(ref, ref, pool.take(), sem, target, cond)
        if item.cross is not None:
            copies.send(ref, ref, pool.take(), item.cross_recv.at[h, ee * 4 + zz], (1 - dp, e, z), when)

    def wait_for(item, h, ee, zz, when):
        def body():
            arrived(item.dst(zz, ee, h), item.recv.at[h, ee * 4 + zz], (dp, e, z))
        if when is None:
            body()
        else:
            pl.when(when)(body)

    def own_stage(k):
        for sign in (-1, 1):
            zz = z + sign * k
            valid = (zz >= 0) & (zz <= 3)
            nxt = z - sign
            on = valid & (nxt >= 0) & (nxt <= 3)
            for h in (0, 1):
                for item in items:
                    wait_for(item, h, e, zz, valid)
                    onward(item, h, e, zz,
                           [((dp, e, nxt), on), ((dp, firsts[h], z), valid), ((dp, seconds[h], z), valid)],
                           valid)

    def relay_stage(k):
        for sign in (-1, 1) if k else (1,):
            zz = z + sign * k
            valid = (zz >= 0) & (zz <= 3) if k else None
            for h in (0, 1):
                for item in items:
                    if k == 0 and item.skip:
                        continue
                    wait_for(item, h, firsts[h], zz, valid)
                    onward(item, h, firsts[h], zz, [((dp, seconds[h], z), valid)], valid)

    def last_stage(k):
        for sign in (-1, 1) if k else (1,):
            zz = z + sign * k
            valid = (zz >= 0) & (zz <= 3) if k else None
            for h in (0, 1):
                for item in items:
                    if k == 0 and item.skip:
                        continue
                    for ee in (seconds[h], diag):
                        wait_for(item, h, ee, zz, valid)
                        onward(item, h, ee, zz, [], valid)

    for h in (0, 1):
        for item in items:
            own, dst, sem = item.own(h), item.dst(z, e, h), item.recv.at[h, e * 4 + z]
            for sign in (-1, 1):
                nxt = z + sign
                copies.send(own, dst, pool.take(), sem, (dp, e, nxt), (nxt >= 0) & (nxt <= 3))
            if not item.skip:
                for target in (firsts[h], seconds[h]):
                    copies.send(own, dst, pool.take(), sem, (dp, target, z))
    own_stage(1)
    relay_stage(0)
    own_stage(2)
    relay_stage(1)
    own_stage(3)
    relay_stage(2)
    relay_stage(3)
    for k in range(4):
        last_stage(k)
    for item in items:
        if item.cross is not None:
            for sign in (-1, 1):
                for k in (1, 2, 3):
                    zz = z + sign * k

                    @pl.when((zz >= 0) & (zz <= 3))
                    def _(item=item, zz=zz):
                        for ee in range(4):
                            for h in (0, 1):
                                arrived(item.cross(zz, ee, h), item.cross_recv.at[h, ee * 4 + zz], (dp, e, z))


def collect_kernel(
    wq, wk, wv, wo, small, wg, wu, wd, dy,
    full, small_all, wg_far, wu_far, wd_far, dy_all,
    own4, load_sem, store_sem, recv_w, recv_x, recv_dy, recv_small, recv_far, send_sems,
):
    dp, e, z = place()
    px, py = x_of(e), y_of(e)
    loads = []
    for m, ref in enumerate((wq, wk, wv, wo)):
        load = pltpu.make_async_copy(ref, own4.at[m], load_sem.at[m])
        load.start()
        loads.append(load)
    peers = [(dp, e, lax.rem(z + d, 4)) for d in (1, 2, 3)]
    peers += [(dp, px, z), (dp, py, z), (1 - dp, e, z)]
    greet(peers)
    copies, pool = Copies(), SemPool(send_sems)
    for load in loads:
        load.wait()

    def row(zz, ee, d, h):
        return zz * 512 + ee * 128 + d * 64 + h * 32

    def own_w(h):
        return own4.at[:, pl.ds(pl.multiple_of(e * 128 + dp * 64 + h * 32, 32), 32), :]

    def dst_w(d):
        return lambda zz, ee, h: full.at[:, pl.ds(pl.multiple_of(row(zz, ee, d, h), 32), 32), :]

    items = [
        Item(own_w, dst_w(dp), recv_w, skip=True, cross=dst_w(1 - dp), cross_recv=recv_x),
        Item(lambda h: dy.at[h], lambda zz, ee, h: dy_all.at[ee * 4 + zz, h], recv_dy),
    ]
    stores = [
        pltpu.make_async_copy(own4, full.at[:, pl.ds(pl.multiple_of(z * 512, 512), 512), :], store_sem.at[0]),
        pltpu.make_async_copy(dy, dy_all.at[e * 4 + z], store_sem.at[1]),
        pltpu.make_async_copy(small, small_all.at[z], store_sem.at[2]),
    ]
    for store in stores:
        store.start()
    for d in (1, 2, 3):
        copies.send(small, small_all.at[z], pool.take(), recv_small.at[z], (dp, e, lax.rem(z + d, 4)))
    for i, (src, dst) in enumerate(((wg, wg_far), (wu, wu_far), (wd, wd_far))):
        copies.send(src, dst, pool.take(), recv_far.at[i], (1 - dp, e, z))
    gather_items(items, copies, pool)
    for d in (1, 2, 3):
        zz = lax.rem(z + d, 4)
        arrived(small_all.at[zz], recv_small.at[zz], (dp, e, z))
    for i, dst in enumerate((wg_far, wu_far, wd_far)):
        arrived(dst, recv_far.at[i], (dp, e, z))
    copies.drain()
    for store in stores:
        store.wait()


def collect(wq, wk, wv, wo, small, wg, wu, wd, dy):
    bf = jnp.bfloat16
    dma = pltpu.SemaphoreType.DMA
    return pl.pallas_call(
        collect_kernel,
        out_shape=(
            jax.ShapeDtypeStruct((4, 2048, 2048), bf),
            jax.ShapeDtypeStruct((4,) + small.shape, bf),
            jax.ShapeDtypeStruct(wg.shape, bf),
            jax.ShapeDtypeStruct(wu.shape, bf),
            jax.ShapeDtypeStruct(wd.shape, bf),
            jax.ShapeDtypeStruct((16,) + dy.shape, bf),
        ),
        in_specs=[ANY] * 8 + [pl.BlockSpec(memory_space=pltpu.VMEM)],
        out_specs=(ANY,) * 6,
        scratch_shapes=[
            pltpu.VMEM((4, 512, 2048), bf),
            dma((4,)),
            dma((3,)),
            dma((2, 16)),
            dma((2, 16)),
            dma((2, 16)),
            dma((4,)),
            dma((3,)),
            dma((192,)),
        ],
        compiler_params=pltpu.CompilerParams(collective_id=0, has_side_effects=True, vmem_limit_bytes=24 * 2**20),
        name="collect_weights",
    )(wq, wk, wv, wo, small, wg, wu, wd, dy)


def spread_kernel(rows, rows_all, store_sem, recv, send_sems):
    dp, e, z = place()
    px, py = x_of(e), y_of(e)
    peers = [(dp, e, lax.rem(z + d, 4)) for d in (1, 2, 3)] + [(dp, px, z), (dp, py, z)]
    greet(peers)
    copies, pool = Copies(), SemPool(send_sems)
    store = pltpu.make_async_copy(rows, rows_all.at[e * 4 + z], store_sem)
    store.start()
    gather_items([Item(lambda h: rows.at[h], lambda zz, ee, h: rows_all.at[ee * 4 + zz, h], recv)], copies, pool)
    copies.drain()
    store.wait()


def spread(rows):
    dma = pltpu.SemaphoreType.DMA
    return pl.pallas_call(
        spread_kernel,
        out_shape=jax.ShapeDtypeStruct((16,) + rows.shape, rows.dtype),
        in_specs=[pl.BlockSpec(memory_space=pltpu.VMEM)],
        out_specs=ANY,
        scratch_shapes=[dma(()), dma((2, 16)), dma((96,))],
        compiler_params=pltpu.CompilerParams(collective_id=1, has_side_effects=True),
        name="spread_rows",
    )(rows)


def combine_kernel(y_in, d_in, y_out, d_out, y_loc, d_loc, y_a, d_a, y_b, d_b, y_c, d_c,
                   load_sem, a_sem, b_sem, c_sem, a_send, b_send, c_send):
    dp, e, z = place()
    px, py = x_of(e), y_of(e)
    diag = x_of(y_of(e))
    me = (dp, e, z)
    loads = []
    for i, (src, loc) in enumerate(((y_in, y_loc), (d_in, d_loc))):
        load = pltpu.make_async_copy(src, loc, load_sem.at[i])
        load.start()
        loads.append(load)
    greet([(dp, e, lax.rem(z + d, 4)) for d in (1, 2, 3)] + [(dp, px, z), (dp, py, z)])
    firsts, seconds = (py, px), (px, py)
    sets = ((0, y_in, y_loc, y_a, y_b, y_c, y_out), (1, d_in, d_loc, d_a, d_b, d_c, d_out))

    def copy(src, dst, send_sem, recv_sem, device):
        return pltpu.make_async_remote_copy(
            src_ref=src, dst_ref=dst, send_sem=send_sem, recv_sem=recv_sem,
            device_id=device, device_id_type=MESH_ID)

    def a_copy(s, h, g, zz):
        i, src, loc, a, b, c, out = s
        ee = (diag, firsts[h])[g]
        return copy(src.at[ee * 4 + zz, h], a.at[h, g, zz], a_send.at[i, h, g, zz], a_sem.at[i, h, g, zz],
                    (dp, firsts[h], z))

    def b_copy(s, h, zz):
        i, src, loc, a, b, c, out = s
        return copy(a.at[h, 0, zz], b.at[h, zz], b_send.at[i, h, zz], b_sem.at[i, h, zz], (dp, seconds[h], z))

    def c_copy(s, h, zz):
        i, src, loc, a, b, c, out = s
        return copy(a.at[h, 1, zz], c.at[h, z], c_send.at[i, h, zz], c_sem.at[i, h, z], (dp, e, zz))

    for g in (0, 1):
        for s in sets:
            for h in (0, 1):
                def start_a(d, _, s=s, h=h, g=g):
                    a_copy(s, h, g, lax.rem(z + d, 4)).start()
                    return 0
                lax.fori_loop(1, 5, start_a, 0)
    for load in loads:
        load.wait()

    for s in sets:
        i, src, loc, a, b, c, out = s
        for h in (0, 1):
            def relay(d, _, s=s, h=h, loc=loc, a=a):
                zz = lax.rem(z + d, 4)
                a_copy(s, h, 0, zz).wait_recv()
                total = a[h, 0, zz].astype(jnp.float32) + loc[seconds[h] * 4 + zz, h].astype(jnp.float32)
                a[h, 0, zz] = total.astype(a.dtype)
                b_copy(s, h, zz).start()
                return 0
            lax.fori_loop(1, 5, relay, 0)
    for s in sets:
        i, src, loc, a, b, c, out = s
        for h in (0, 1):
            def finish(d, _, s=s, h=h, loc=loc, a=a, b=b):
                zz = lax.rem(z + d, 4)
                a_copy(s, h, 1, zz).wait_recv()
                b_copy(s, h, zz).wait_recv()
                total = (a[h, 1, zz].astype(jnp.float32) + loc[e * 4 + zz, h].astype(jnp.float32)
                         + b[h, zz].astype(jnp.float32))
                a[h, 1, zz] = total.astype(a.dtype)
                c_copy(s, h, zz).start()
                return 0
            lax.fori_loop(1, 4, finish, 0)
    for s in sets:
        i, src, loc, a, b, c, out = s
        for h in (0, 1):
            a_copy(s, h, 1, z).wait_recv()
            b_copy(s, h, z).wait_recv()
            out[h] = (a[h, 1, z].astype(jnp.float32) + loc[e * 4 + z, h].astype(jnp.float32)
                      + b[h, z].astype(jnp.float32))
            for d in (1, 2, 3):
                zz = lax.rem(z + d, 4)
                arrived(c.at[h, zz], c_sem.at[i, h, zz], me)
                out[h] += c[h, zz].astype(jnp.float32)
    for s in sets:
        for h in (0, 1):
            def drain(d, _, s=s, h=h):
                zz = lax.rem(z + d, 4)
                a_copy(s, h, 0, zz).wait_send()
                a_copy(s, h, 1, zz).wait_send()
                b_copy(s, h, zz).wait_send()
                return 0
            lax.fori_loop(1, 5, drain, 0)

            def drain_c(d, _, s=s, h=h):
                c_copy(s, h, lax.rem(z + d, 4)).wait_send()
                return 0
            lax.fori_loop(1, 4, drain_c, 0)


def combine(y_part, d_part):
    dma = pltpu.SemaphoreType.DMA
    bf = jnp.bfloat16
    wide, narrow = y_part.shape[3], d_part.shape[3]
    rows = y_part.shape[2]
    vmem = pl.BlockSpec(memory_space=pltpu.VMEM)
    return pl.pallas_call(
        combine_kernel,
        out_shape=(
            jax.ShapeDtypeStruct((2, rows, wide), jnp.float32),
            jax.ShapeDtypeStruct((2, rows, narrow), jnp.float32),
        ),
        in_specs=[ANY, ANY],
        out_specs=(vmem, vmem),
        scratch_shapes=[
            pltpu.VMEM(y_part.shape, bf),
            pltpu.VMEM(d_part.shape, bf),
            pltpu.VMEM((2, 2, 4, rows, wide), bf),
            pltpu.VMEM((2, 2, 4, rows, narrow), bf),
            pltpu.VMEM((2, 4, rows, wide), bf),
            pltpu.VMEM((2, 4, rows, narrow), bf),
            pltpu.VMEM((2, 4, rows, wide), bf),
            pltpu.VMEM((2, 4, rows, narrow), bf),
            dma((2,)),
            dma((2, 2, 2, 4)),
            dma((2, 2, 4)),
            dma((2, 2, 4)),
            dma((2, 2, 2, 4)),
            dma((2, 2, 4)),
            dma((2, 2, 4)),
        ],
        compiler_params=pltpu.CompilerParams(collective_id=2, has_side_effects=True, vmem_limit_bytes=56 * 2**20),
        name="combine_rows",
    )(y_part, d_part)


def total_kernel(gq, gk, gv, go, small, eg, eu, ed,
                 out, small_out, eg_far, eu_far, ed_far,
                 far, a, b, c, mine, work, s_z, s_all,
                 work_sem, far_sem, a_sem, b_sem, c_sem, e_sem, sz_sem, sa_sem, g_sem,
                 far_send, a_send, b_send, c_send, e_send, sz_send, sa_send, g_send, out_sem):
    dp, e, z = place()
    px, py = x_of(e), y_of(e)
    diag = x_of(y_of(e))
    firsts, seconds = (py, px), (px, py)
    grads = (gq, gk, gv, go)
    zs = [lax.rem(z + d, 4) for d in range(4)]
    mates = [(lax.rem(dp + d // 4, 2), lax.rem(e + d % 4, 4), z) for d in range(1, 8)]
    greet([(dp, e, zz) for zz in zs[1:]] + mates)

    def copy(src, dst, send_sem, recv_sem, device):
        return pltpu.make_async_remote_copy(
            src_ref=src, dst_ref=dst, send_sem=send_sem, recv_sem=recv_sem,
            device_id=device, device_id_type=MESH_ID)

    def rows_of(ee, zz, d, h):
        return pl.ds(pl.multiple_of(zz * 512 + ee * 128 + d * 64 + h * 32, 32), 32)

    def far_copy(m, ee, zz, h):
        return copy(grads[m].at[rows_of(ee, zz, 1 - dp, h)], far.at[h, ee, zz, m],
                    far_send.at[h, ee, zz, m], far_sem.at[h, ee, zz, m], (1 - dp, e, z))

    def load(m, ee, zz, h, slot):
        return pltpu.make_async_copy(grads[m].at[rows_of(ee, zz, dp, h)], work.at[slot, m], work_sem.at[slot, m])

    def groups(h):
        return (diag, firsts[h], seconds[h], e)

    def e_copy(i):
        src, dst = ((eg, eg_far), (eu, eu_far), (ed, ed_far))[i]
        return copy(src, dst, e_send.at[i], e_sem.at[i], (1 - dp, e, z))

    def sz_copy(d):
        return copy(small.at[zs[d]], s_z.at[z], sz_send.at[d - 1], sz_sem.at[z], (dp, e, zs[d]))

    for d in (1, 2, 3):
        sz_copy(d).start()
    for g in range(4):
        for h in (0, 1):
            def start_far(zz, _, g=g, h=h):
                for m in range(4):
                    far_copy(m, groups(h)[g], zz, h).start()
                return 0
            lax.fori_loop(0, 4, start_far, 0)
    for i in range(3):
        e_copy(i).start()

    def a_copy(h, g, zz):
        return copy(far.at[h, groups(h)[g], zz], a.at[h, g, zz], a_send.at[h, g, zz], a_sem.at[h, g, zz],
                    (dp, firsts[h], z))

    def b_copy(h, zz):
        return copy(far.at[h, seconds[h], zz], b.at[h, zz], b_send.at[h, zz], b_sem.at[h, zz], (dp, seconds[h], z))

    def c_copy(h, zz):
        return copy(far.at[h, e, zz], c.at[h, z], c_send.at[h, zz], c_sem.at[h, z], (dp, e, zz))

    def load_step(n, slot):
        g, h, zz = n // 8, lax.rem(n // 4, 2), lax.rem(n, 4)
        ee = pick(g, h)
        for m in range(4):
            load(m, ee, zz, h, slot).start()

    def pick(g, h):
        first = jnp.where(h == 0, py, px)
        second = jnp.where(h == 0, px, py)
        return jnp.where(g == 0, diag, jnp.where(g == 1, first, jnp.where(g == 2, second, e)))

    load_step(0, 0)

    def near(n, _):
        slot = lax.rem(n, 2)

        @pl.when(n + 1 < 32)
        def _():
            load_step(n + 1, 1 - slot)

        g, h, zz = n // 8, lax.rem(n // 4, 2), lax.rem(n, 4)
        ee = pick(g, h)
        for m in range(4):
            load(m, ee, zz, h, slot).wait()
            arrived(far.at[h, ee, zz, m], far_sem.at[h, ee, zz, m], (dp, e, z))
        far[h, ee, zz] = (far[h, ee, zz].astype(jnp.float32) + work[slot].astype(jnp.float32)).astype(far.dtype)

        @pl.when(g < 2)
        def _():
            first = jnp.where(h == 0, py, px)
            copy(far.at[h, ee, zz], a.at[h, g, zz], a_send.at[h, g, zz], a_sem.at[h, g, zz], (dp, first, z)).start()
        return 0

    lax.fori_loop(0, 32, near, 0)

    for h in (0, 1):
        def relay(d, _, h=h):
            zz = lax.rem(z + d, 4)
            arrived(a.at[h, 0, zz], a_sem.at[h, 0, zz], (dp, e, z))
            far[h, seconds[h], zz] = (far[h, seconds[h], zz].astype(jnp.float32)
                                      + a[h, 0, zz].astype(jnp.float32)).astype(far.dtype)
            b_copy(h, zz).start()
            return 0
        lax.fori_loop(1, 5, relay, 0)
    for h in (0, 1):
        def finish(d, _, h=h):
            zz = lax.rem(z + d, 4)
            arrived(a.at[h, 1, zz], a_sem.at[h, 1, zz], (dp, e, z))
            arrived(b.at[h, zz], b_sem.at[h, zz], (dp, e, z))
            far[h, e, zz] = (far[h, e, zz].astype(jnp.float32) + a[h, 1, zz].astype(jnp.float32)
                             + b[h, zz].astype(jnp.float32)).astype(far.dtype)

            @pl.when(d < 4)
            def _():
                c_copy(h, zz).start()
            return 0
        lax.fori_loop(1, 5, finish, 0)

    def sa_copy(d):
        return copy(mine_small, s_all.at[dp * 4 + e], sa_send.at[d - 1], sa_sem.at[dp * 4 + e], mates[d - 1])

    slot_me = dp * 4 + e
    for d in (1, 2, 3):
        arrived(s_z.at[zs[d]], sz_sem.at[zs[d]], (dp, e, z))
    s_all[slot_me] = (small[z] + s_z[zs[1]]) + (s_z[zs[2]] + s_z[zs[3]])
    mine_small = s_all.at[slot_me]
    for d in range(1, 8):
        sa_copy(d).start()

    def mine_at(d, ee):
        return pl.ds(pl.multiple_of(ee * 128 + d * 64, 64), 64)

    def g_copy(h, n):
        return copy(mine.at[:, pl.ds(h * 32, 32)],
                    out.at[:, pl.ds(pl.multiple_of(e * 128 + dp * 64 + h * 32, 32), 32)],
                    g_send.at[h, n], g_sem.at[h, slot_me], mates[n])

    locals_out = []
    for h in (0, 1):
        def last(m, _, h=h):
            mine[m, pl.ds(h * 32, 32)] = (
                (far[h, e, z, m].astype(jnp.float32) + c[h, zs[1], m].astype(jnp.float32))
                + (c[h, zs[2], m].astype(jnp.float32) + c[h, zs[3], m].astype(jnp.float32))
            ).astype(mine.dtype)
            return 0
        for d in (1, 2, 3):
            arrived(c.at[h, zs[d]], c_sem.at[h, zs[d]], (dp, e, z))
        lax.fori_loop(0, 4, last, 0)
        for n in range(7):
            g_copy(h, n).start()
        keep = pltpu.make_async_copy(
            mine.at[:, pl.ds(h * 32, 32)],
            out.at[:, pl.ds(pl.multiple_of(e * 128 + dp * 64 + h * 32, 32), 32)],
            out_sem.at[h])
        keep.start()
        locals_out.append(keep)
    total = s_all[slot_me]
    for d in range(1, 8):
        other = lax.rem(dp + d // 4, 2) * 4 + lax.rem(e + d % 4, 4)
        arrived(s_all.at[other], sa_sem.at[other], (dp, e, z))
    small_out[...] = (((s_all[0] + s_all[1]) + (s_all[2] + s_all[3]))
                      + ((s_all[4] + s_all[5]) + (s_all[6] + s_all[7])))
    for h in (0, 1):
        for d in range(1, 8):
            od, oe = lax.rem(dp + d // 4, 2), lax.rem(e + d % 4, 4)
            arrived(out.at[:, pl.ds(pl.multiple_of(oe * 128 + od * 64 + h * 32, 32), 32)],
                    g_sem.at[h, od * 4 + oe], (dp, e, z))
    for i in range(3):
        e_copy(i).wait()
    for d in (1, 2, 3):
        sz_copy(d).wait_send()
    for d in range(1, 8):
        sa_copy(d).wait_send()
    for h in (0, 1):
        for n in range(7):
            g_copy(h, n).wait_send()
        locals_out[h].wait()
        for g in range(4):
            def drain_far(zz, _, g=g, h=h):
                for m in range(4):
                    far_copy(m, groups(h)[g], zz, h).wait_send()
                return 0
            lax.fori_loop(0, 4, drain_far, 0)

        def drain(d, _, h=h):
            zz = lax.rem(z + d, 4)
            a_copy(h, 0, zz).wait_send()
            a_copy(h, 1, zz).wait_send()
            b_copy(h, zz).wait_send()

            @pl.when(d < 4)
            def _():
                c_copy(h, zz).wait_send()
            return 0
        lax.fori_loop(1, 5, drain, 0)


def total(gq, gk, gv, go, small, eg, eu, ed):
    dma = pltpu.SemaphoreType.DMA
    bf, f32 = jnp.bfloat16, jnp.float32
    vmem = pl.BlockSpec(memory_space=pltpu.VMEM)
    return pl.pallas_call(
        total_kernel,
        out_shape=(
            jax.ShapeDtypeStruct((4, 512, 2048), bf),
            jax.ShapeDtypeStruct(small.shape[1:], f32),
            jax.ShapeDtypeStruct(eg.shape, bf),
            jax.ShapeDtypeStruct(eu.shape, bf),
            jax.ShapeDtypeStruct(ed.shape, bf),
        ),
        in_specs=[ANY] * 4 + [vmem] + [ANY] * 3,
        out_specs=(ANY, vmem, ANY, ANY, ANY),
        scratch_shapes=[
            pltpu.VMEM((2, 4, 4, 4, 32, 2048), bf),
            pltpu.VMEM((2, 2, 4, 4, 32, 2048), bf),
            pltpu.VMEM((2, 4, 4, 32, 2048), bf),
            pltpu.VMEM((2, 4, 4, 32, 2048), bf),
            pltpu.VMEM((4, 64, 2048), bf),
            pltpu.VMEM((2, 4, 32, 2048), bf),
            pltpu.VMEM(small.shape, f32),
            pltpu.VMEM((8,) + small.shape[1:], f32),
            dma((2, 4)),
            dma((2, 4, 4, 4)),
            dma((2, 2, 4)),
            dma((2, 4)),
            dma((2, 4)),
            dma((3,)),
            dma((4,)),
            dma((8,)),
            dma((2, 8)),
            dma((2, 4, 4, 4)),
            dma((2, 2, 4)),
            dma((2, 4)),
            dma((2, 4)),
            dma((3,)),
            dma((3,)),
            dma((7,)),
            dma((2, 7)),
            dma((2,)),
        ],
        compiler_params=pltpu.CompilerParams(collective_id=3, has_side_effects=True, vmem_limit_bytes=52 * 2**20),
        name="total_grads",
    )(gq, gk, gv, go, small, eg, eu, ed)


def gathered(
    tokens,
    cotangent,
    lengths,
    routes,
    w_query,
    w_key,
    w_value,
    w_out,
    w_router,
    g_attn,
    g_ffn,
    g_query,
    g_key,
    w_gate,
    w_up,
    w_down,
):
    micro_count, _, seq_len, model_width = tokens.shape
    expert_count = w_router.shape[1]
    f32, bf = jnp.float32, jnp.bfloat16
    places = jnp.arange(seq_len)
    score_scale = HDIM ** (-0.5)
    length = lengths[:, 0]
    live = places[None, :] < length[:, None]
    dy = jnp.where(live[:, :, None], cotangent[:, 0], jnp.zeros((), bf))
    small = jnp.concatenate(
        [w_router.T, g_attn[None], g_ffn[None], g_query[None], g_key[None],
         jnp.zeros((32 - expert_count - 4, w_router.shape[0]), bf)], axis=0)
    full, small_all, gate_far, up_far, down_far, dy_all = collect(
        w_query, w_key, w_value, w_out, small, w_gate[0], w_up[0], w_down[0], dy)
    query_full, key_full, value_full, out_full = full[0], full[1], full[2], full[3]
    small_rows = jnp.swapaxes(small_all, 0, 1).reshape(32, model_width)
    route_full = small_rows[:expert_count].T
    gain_attn, gain_ffn, gain_query, gain_key = (
        small_rows[expert_count + i].astype(f32) for i in range(4))

    rows = micro_count * seq_len
    cosine_one, sine_one = rope_tables(seq_len, HDIM)
    cosine_table, sine_table = jnp.tile(cosine_one, (micro_count, 1)), jnp.tile(sine_one, (micro_count, 1))
    inputs = tokens[:, 0].reshape(rows, model_width).astype(f32)
    route_ids = routes[:, 0].reshape(rows, -1)
    normed = rms_norm(inputs, gain_attn).astype(bf)
    query_raw = matmul(normed, query_full)
    key_raw = matmul(normed, key_full)
    value_raw = matmul(normed, value_full)

    def per_head(values):
        return values.reshape(micro_count, seq_len, HEADS, HDIM)

    value_low = per_head(value_raw.astype(bf))
    query_low = per_head(rotate(
        rms_norm(query_raw, gain_query).reshape(rows, HEADS, HDIM), cosine_table, sine_table).astype(bf))
    key_low = per_head(rotate(
        rms_norm(key_raw, gain_key).reshape(rows, HEADS, HDIM), cosine_table, sine_table).astype(bf))
    allowed = (places[None, None, :] <= places[None, :, None]) & live[:, None, :]
    scores = jnp.einsum("mqhd,mkhd->mhqk", query_low, key_low, preferred_element_type=f32) * score_scale
    attn_probs = softmax_rows(jnp.where(allowed[:, None], scores, -1e30))
    probs_low = attn_probs.astype(bf)
    mixed_low = jnp.einsum("mhqk,mkhd->mqhd", probs_low, value_low, preferred_element_type=f32)
    mixed_low = mixed_low.reshape(rows, model_width).astype(bf)
    hidden_state = inputs + matmul(mixed_low, out_full)
    ffn_in = rms_norm(hidden_state, gain_ffn).astype(bf)
    router = softmax_rows(matmul(ffn_in, route_full))
    expert_ids = jnp.arange(expert_count)
    chosen = jnp.any(route_ids[:, :, None] == expert_ids[None, None, :], axis=1)
    gates = jnp.where(chosen, router, 0.0)
    gates_high = gates.astype(bf)
    gates_low = (gates - gates_high.astype(f32)).astype(bf)
    sent = jnp.concatenate(
        [ffn_in, gates_high, gates_low, jnp.zeros((rows, EXTRA - 2 * expert_count), bf)], axis=1)
    spread_rows = spread(sent.reshape(micro_count, seq_len, -1))

    every = 16 * rows
    wide_rows = spread_rows.reshape(every, -1)
    dy_rows = dy_all.reshape(every, model_width)
    expert_rows = wide_rows[:, :model_width]
    mine = lax.axis_index("expert") * 4 + lax.axis_index("shard")
    lane = jnp.arange(EXTRA)
    pick = (lane == mine) | (lane == mine + expert_count)
    gate_own = jnp.sum(jnp.where(pick[None], wide_rows[:, model_width:].astype(f32), 0.0), axis=1, keepdims=True)
    dy_route = (gate_own * dy_rows.astype(f32)).astype(bf)
    halves = ((w_gate[0], w_up[0], w_down[0]), (gate_far, up_far, down_far))
    y_sum, d_sum, grads = 0.0, 0.0, []
    for gate_w, up_w, down_w in halves:
        gate_pre = matmul(expert_rows, gate_w)
        up_value = matmul(expert_rows, up_w)
        sigmoid_gate = jax.nn.sigmoid(gate_pre)
        activated = gate_pre * sigmoid_gate
        inner = (activated * up_value).astype(bf)
        y_sum = y_sum + matmul(inner, down_w)
        d_inner = times_transposed(dy_route, down_w)
        d_gate = (d_inner * up_value * (sigmoid_gate + gate_pre * sigmoid_gate * (1.0 - sigmoid_gate))).astype(bf)
        d_up = (d_inner * activated).astype(bf)
        d_sum = d_sum + times_transposed(d_gate, gate_w) + times_transposed(d_up, up_w)
        grads.append((transposed_times(expert_rows, d_gate), transposed_times(expert_rows, d_up),
                      transposed_times(inner, dy_route)))
    y_low = y_sum.astype(bf).astype(f32)
    d_gate_own = jnp.sum(y_low * dy_rows.astype(f32), axis=1, keepdims=True)
    dg_high = d_gate_own.astype(bf).astype(f32)
    dg_low = d_gate_own - dg_high
    extra = jnp.where(lane[None] == mine, dg_high, 0.0) + jnp.where(lane[None] == mine + expert_count, dg_low, 0.0)
    y_part = jnp.concatenate([(gate_own * y_low).astype(bf), extra.astype(bf)], axis=1)
    y_all, d_all = combine(y_part.reshape(16, micro_count, seq_len, -1),
                           d_sum.astype(bf).reshape(16, micro_count, seq_len, -1))
    y_all = y_all.reshape(rows, -1)
    d_ffn_in = d_all.reshape(rows, -1)
    mixed_out = (hidden_state + y_all[:, :model_width]).astype(bf)
    d_gates = y_all[:, model_width:model_width + expert_count] + y_all[
        :, model_width + expert_count:model_width + 2 * expert_count]
    d_router = jnp.where(chosen, d_gates, 0.0)
    d_output = dy.reshape(rows, model_width).astype(f32)
    d_logits = (router * (d_router - jnp.sum(router * d_router, axis=1, keepdims=True))).astype(bf)
    grad_router = transposed_times(d_logits, ffn_in)
    d_ffn_in = d_ffn_in + times_transposed(d_logits, route_full)
    d_hidden_norm, d_gain_ffn = norm_back(hidden_state, gain_ffn, d_ffn_in)
    d_hidden = d_output + d_hidden_norm
    d_attn_low = d_hidden.astype(bf)
    grad_out = transposed_times(mixed_low, d_attn_low).astype(bf)
    d_mixed = per_head(times_transposed(d_attn_low, out_full).astype(bf))
    d_probs = jnp.einsum("mqhd,mkhd->mhqk", d_mixed, value_low, preferred_element_type=f32)
    d_value = jnp.einsum("mhqk,mqhd->mkhd", probs_low, d_mixed, preferred_element_type=f32)
    d_value = d_value.reshape(rows, model_width).astype(bf)
    d_scores = (attn_probs * (d_probs - jnp.sum(attn_probs * d_probs, axis=-1, keepdims=True))).astype(bf)
    d_query = jnp.einsum("mhqk,mkhd->mqhd", d_scores, key_low, preferred_element_type=f32) * score_scale
    d_key = jnp.einsum("mhqk,mqhd->mkhd", d_scores, query_low, preferred_element_type=f32) * score_scale

    def raw_back(raw, gain_vec, d_heads):
        turned = rotate_back(d_heads.reshape(rows, HEADS, HDIM), cosine_table, sine_table)
        return norm_back(raw, gain_vec, turned.reshape(rows, model_width))

    d_query_raw, d_gain_query = raw_back(query_raw, gain_query, d_query)
    d_key_raw, d_gain_key = raw_back(key_raw, gain_key, d_key)
    d_query_low, d_key_low = d_query_raw.astype(bf), d_key_raw.astype(bf)
    grad_query = transposed_times(normed, d_query_low).astype(bf)
    grad_key = transposed_times(normed, d_key_low).astype(bf)
    grad_value = transposed_times(normed, d_value).astype(bf)
    d_normed = (times_transposed(d_query_low, query_full) + times_transposed(d_key_low, key_full)
                + times_transposed(d_value, value_full))
    d_input_norm, d_gain_attn = norm_back(inputs, gain_attn, d_normed)
    grad_tokens = (d_hidden + d_input_norm).reshape(micro_count, 1, seq_len, model_width)

    small_grads = jnp.concatenate(
        [grad_router, d_gain_attn[None], d_gain_ffn[None], d_gain_query[None], d_gain_key[None],
         jnp.zeros((24 - expert_count - 4, model_width), f32)], axis=0)
    small_grads = jnp.swapaxes(small_grads.reshape(24, 4, model_width // 4), 0, 1)
    near, away = grads
    sums, small_sums, eg, eu, ed = total(
        grad_query, grad_key, grad_value, grad_out, small_grads, *(g.astype(bf) for g in away))
    expert_totals = [(g + other.astype(f32))[None] for g, other in zip(near, (eg, eu, ed))]
    return (
        mixed_out.reshape(micro_count, 1, seq_len, model_width),
        grad_tokens,
        sums[0].astype(f32),
        sums[1].astype(f32),
        sums[2].astype(f32),
        sums[3].astype(f32),
        small_sums[:expert_count].T,
        small_sums[expert_count],
        small_sums[expert_count + 1],
        small_sums[expert_count + 2],
        small_sums[expert_count + 3],
        *expert_totals,
    )


def dispatch_rows(buffer):
    return lax.all_to_all(buffer, ("expert", "shard"), split_axis=0, concat_axis=0, tiled=True)


def collect_rows(buffer):
    return lax.all_to_all(buffer, ("expert", "shard"), split_axis=0, concat_axis=0, tiled=True)


def dispatch_grads(buffer):
    return lax.all_to_all(buffer, ("expert", "shard"), split_axis=0, concat_axis=0, tiled=True)


def collect_grads(buffer):
    return lax.all_to_all(buffer, ("expert", "shard"), split_axis=0, concat_axis=0, tiled=True)


def to_experts(arrived, local_experts, capacity):
    sources = arrived.shape[0]
    model_width = arrived.shape[2]
    split_rows = arrived.reshape(sources, local_experts, capacity, model_width)
    return jnp.swapaxes(split_rows, 0, 1).reshape(local_experts, sources * capacity, model_width)


def from_experts(expert_token_rows, owners, capacity):
    local_experts = expert_token_rows.shape[0]
    model_width = expert_token_rows.shape[2]
    split_rows = expert_token_rows.reshape(local_experts, owners, capacity, model_width)
    return jnp.swapaxes(split_rows, 0, 1).reshape(owners, local_experts * capacity, model_width)


def exchanged(
    tokens,
    cotangent,
    lengths,
    routes,
    w_query,
    w_key,
    w_value,
    w_out,
    w_router,
    g_attn,
    g_ffn,
    g_query,
    g_key,
    w_gate,
    w_up,
    w_down,
):
    micro_count = tokens.shape[0]
    seq_len = tokens.shape[2]
    model_width = tokens.shape[3]
    top_count = routes.shape[3]
    expert_count = w_router.shape[1]
    local_experts = w_gate.shape[0]
    owners = expert_count // local_experts
    capacity = min(seq_len, max(2, 2 * seq_len * top_count // expert_count))
    slot_total = expert_count * capacity
    gate_weight_complete, up_weight_complete, down_weight_complete = (
        lax.all_gather(w_gate, "dp", axis=2, tiled=True),
        lax.all_gather(w_up, "dp", axis=2, tiled=True),
        lax.all_gather(w_down, "dp", axis=1, tiled=True),
    )
    cosine_table, sine_table = rope_tables(seq_len, HDIM)
    places = jnp.arange(seq_len)
    slot_ids = jnp.arange(slot_total)
    expert_ids = jnp.arange(expert_count)
    score_scale = HDIM ** (-0.5)
    grad_query = jnp.zeros((model_width, model_width), jnp.float32)
    grad_key = jnp.zeros((model_width, model_width), jnp.float32)
    grad_value = jnp.zeros((model_width, model_width), jnp.float32)
    grad_out = jnp.zeros((model_width, model_width), jnp.float32)
    grad_router = jnp.zeros((model_width, expert_count), jnp.float32)
    grad_gain_attn = jnp.zeros((model_width,), jnp.float32)
    grad_gain_ffn = jnp.zeros((model_width,), jnp.float32)
    grad_gain_query = jnp.zeros((model_width,), jnp.float32)
    grad_gain_key = jnp.zeros((model_width,), jnp.float32)
    grad_gate = jnp.zeros(gate_weight_complete.shape, jnp.float32)
    grad_up = jnp.zeros(up_weight_complete.shape, jnp.float32)
    grad_down = jnp.zeros(down_weight_complete.shape, jnp.float32)
    outs_mixed = []
    outs_grad = []
    for micro_step in range(micro_count):
        layer_set = (
            lax.all_gather(w_query, "shard", axis=0, tiled=True),
            lax.all_gather(w_key, "shard", axis=0, tiled=True),
            lax.all_gather(w_value, "shard", axis=0, tiled=True),
            lax.all_gather(w_out, "shard", axis=0, tiled=True),
            lax.all_gather(w_router, "shard", axis=0, tiled=True),
            lax.all_gather(g_attn, "shard", axis=0, tiled=True),
            lax.all_gather(g_ffn, "shard", axis=0, tiled=True),
            lax.all_gather(g_query, "shard", axis=0, tiled=True),
            lax.all_gather(g_key, "shard", axis=0, tiled=True),
        )
        query_full, key_full, value_full, out_full, route_full = (
            layer_set[0],
            layer_set[1],
            layer_set[2],
            layer_set[3],
            layer_set[4],
        )
        gain_attn = layer_set[5].astype(jnp.float32)
        gain_ffn = layer_set[6].astype(jnp.float32)
        gain_query = layer_set[7].astype(jnp.float32)
        gain_key = layer_set[8].astype(jnp.float32)
        inputs = tokens[micro_step, 0].astype(jnp.float32)
        length = lengths[micro_step, 0]
        route_ids = routes[micro_step, 0]
        normed = rms_norm(inputs, gain_attn).astype(jnp.bfloat16)
        query_raw = matmul(normed, query_full)
        key_raw = matmul(normed, key_full)
        value_raw = matmul(normed, value_full)
        value_low = value_raw.astype(jnp.bfloat16).reshape(seq_len, HEADS, HDIM)
        query_low = rotate(
            rms_norm(query_raw, gain_query).reshape(seq_len, HEADS, HDIM), cosine_table, sine_table
        ).astype(jnp.bfloat16)
        key_low = rotate(
            rms_norm(key_raw, gain_key).reshape(seq_len, HEADS, HDIM), cosine_table, sine_table
        ).astype(jnp.bfloat16)
        allowed = (places[None, :] <= places[:, None]) & (places[None, :] < length)
        scores = (
            jnp.einsum("qhd,khd->hqk", query_low, key_low, preferred_element_type=jnp.float32)
            * score_scale
        )
        attn_probs = softmax_rows(jnp.where(allowed[None], scores, -1e30))
        probs_low = attn_probs.astype(jnp.bfloat16)
        mixed_low = (
            jnp.einsum("hqk,khd->qhd", probs_low, value_low, preferred_element_type=jnp.float32)
            .reshape(seq_len, model_width)
            .astype(jnp.bfloat16)
        )
        attn_part = matmul(mixed_low, out_full)
        hidden_state = inputs + attn_part
        ffn_in = rms_norm(hidden_state, gain_ffn).astype(jnp.bfloat16)
        logits = matmul(ffn_in, route_full)
        router = softmax_rows(logits)
        chosen = route_ids[:, :, None] == expert_ids[None, None, :]
        gate_vals = jnp.sum(jnp.where(chosen, router[:, None, :], 0.0), axis=2)
        flat_chosen = chosen.reshape(seq_len * top_count, expert_count).astype(jnp.int32)
        before = jnp.cumsum(flat_chosen, axis=0) - flat_chosen
        slot_rank = jnp.sum(before * flat_chosen, axis=1)
        target = route_ids.reshape(-1) * capacity + slot_rank
        placing = (slot_ids[:, None] == target[None, :]).astype(jnp.bfloat16)
        token_placing = jnp.sum(placing.reshape(slot_total, seq_len, top_count), axis=2)
        outgoing = matmul(token_placing, ffn_in).astype(jnp.bfloat16)
        arrived = dispatch_rows(outgoing.reshape(owners, local_experts * capacity, model_width))
        expert_token_rows = to_experts(arrived, local_experts, capacity)
        gate_pre = jnp.einsum(
            "qjs,qsy->qjy",
            expert_token_rows,
            gate_weight_complete,
            preferred_element_type=jnp.float32,
        )
        up_value = jnp.einsum(
            "qjs,qsy->qjy",
            expert_token_rows,
            up_weight_complete,
            preferred_element_type=jnp.float32,
        )
        sigmoid_gate = jax.nn.sigmoid(gate_pre)
        activated = gate_pre * sigmoid_gate
        inner_activation = (activated * up_value).astype(jnp.bfloat16)
        expert_out = jnp.einsum(
            "aqc,aco->aqo",
            inner_activation,
            down_weight_complete,
            preferred_element_type=jnp.float32,
        ).astype(jnp.bfloat16)
        returned = collect_rows(from_experts(expert_out, owners, capacity)).reshape(
            slot_total, model_width
        )
        picked = (
            jnp.take(returned, target, axis=0)
            .astype(jnp.float32)
            .reshape(seq_len, top_count, model_width)
        )
        expert_sum = jnp.sum(picked * gate_vals[:, :, None], axis=1)
        outs_mixed.append((hidden_state + expert_sum).astype(jnp.bfloat16))
        live_mask = (places < length).astype(jnp.float32)
        d_output = cotangent[micro_step, 0].astype(jnp.float32) * live_mask[:, None]
        d_gates = jnp.sum(picked * d_output[:, None, :], axis=2)
        d_slots = (
            (gate_vals[:, :, None] * d_output[:, None, :])
            .astype(jnp.bfloat16)
            .reshape(seq_len * top_count, model_width)
        )
        d_outgoing = matmul(placing, d_slots).astype(jnp.bfloat16)
        d_arrived = dispatch_grads(
            d_outgoing.reshape(owners, local_experts * capacity, model_width)
        )
        expert_output_gradient = to_experts(d_arrived, local_experts, capacity)
        d_inner = jnp.einsum(
            "azy,ajy->azj",
            expert_output_gradient,
            down_weight_complete,
            preferred_element_type=jnp.float32,
        )
        grad_down = grad_down + jnp.einsum(
            "qti,qtj->qij",
            inner_activation,
            expert_output_gradient,
            preferred_element_type=jnp.float32,
        )
        gate_preactivation_gradient = (
            d_inner * up_value * (sigmoid_gate + gate_pre * sigmoid_gate * (1.0 - sigmoid_gate))
        ).astype(jnp.bfloat16)
        up_projection_value_gradient = (d_inner * activated).astype(jnp.bfloat16)
        grad_gate = grad_gate + jnp.einsum(
            "hzo,hzg->hog",
            expert_token_rows,
            gate_preactivation_gradient,
            preferred_element_type=jnp.float32,
        )
        grad_up = grad_up + jnp.einsum(
            "hzo,hzg->hog",
            expert_token_rows,
            up_projection_value_gradient,
            preferred_element_type=jnp.float32,
        )
        d_rows = jnp.einsum(
            "ing,itg->int",
            gate_preactivation_gradient,
            gate_weight_complete,
            preferred_element_type=jnp.float32,
        )
        d_rows = (
            d_rows
            + jnp.einsum(
                "ing,itg->int",
                up_projection_value_gradient,
                up_weight_complete,
                preferred_element_type=jnp.float32,
            )
        ).astype(jnp.bfloat16)
        d_returned = collect_grads(from_experts(d_rows, owners, capacity)).reshape(
            slot_total, model_width
        )
        d_ffn_in = jnp.sum(
            jnp.take(d_returned, target, axis=0)
            .astype(jnp.float32)
            .reshape(seq_len, top_count, model_width),
            axis=1,
        )
        d_router = jnp.sum(jnp.where(chosen, d_gates[:, :, None], 0.0), axis=1)
        d_logits = (router * (d_router - jnp.sum(router * d_router, axis=1, keepdims=True))).astype(
            jnp.bfloat16
        )
        grad_router = grad_router + transposed_times(ffn_in, d_logits)
        d_ffn_in = d_ffn_in + times_transposed(d_logits, route_full)
        d_hidden_norm, d_gain_ffn = norm_back(hidden_state, gain_ffn, d_ffn_in)
        grad_gain_ffn = grad_gain_ffn + d_gain_ffn
        d_hidden = d_output + d_hidden_norm
        d_attn_low = d_hidden.astype(jnp.bfloat16)
        grad_out = grad_out + transposed_times(mixed_low, d_attn_low)
        d_mixed_wide = times_transposed(d_attn_low, out_full)
        d_mixed = d_mixed_wide.astype(jnp.bfloat16).reshape(seq_len, HEADS, HDIM)
        d_probs = jnp.einsum("qhd,khd->hqk", d_mixed, value_low, preferred_element_type=jnp.float32)
        d_value = (
            jnp.einsum("hqk,qhd->khd", probs_low, d_mixed, preferred_element_type=jnp.float32)
            .reshape(seq_len, model_width)
            .astype(jnp.bfloat16)
        )
        d_scores = (
            attn_probs * (d_probs - jnp.sum(attn_probs * d_probs, axis=-1, keepdims=True))
        ).astype(jnp.bfloat16)
        d_query = (
            jnp.einsum("hqk,khd->qhd", d_scores, key_low, preferred_element_type=jnp.float32)
            * score_scale
        )
        d_key = (
            jnp.einsum("hqk,qhd->khd", d_scores, query_low, preferred_element_type=jnp.float32)
            * score_scale
        )
        d_query_raw, d_gain_query = norm_back(
            query_raw,
            gain_query,
            rotate_back(d_query, cosine_table, sine_table).reshape(seq_len, model_width),
        )
        d_key_raw, d_gain_key = norm_back(
            key_raw,
            gain_key,
            rotate_back(d_key, cosine_table, sine_table).reshape(seq_len, model_width),
        )
        grad_gain_query = grad_gain_query + d_gain_query
        grad_gain_key = grad_gain_key + d_gain_key
        d_query_low = d_query_raw.astype(jnp.bfloat16)
        d_key_low = d_key_raw.astype(jnp.bfloat16)
        grad_query = grad_query + transposed_times(normed, d_query_low)
        grad_key = grad_key + transposed_times(normed, d_key_low)
        grad_value = grad_value + transposed_times(normed, d_value)
        d_normed = (
            times_transposed(d_query_low, query_full)
            + times_transposed(d_key_low, key_full)
            + times_transposed(d_value, value_full)
        )
        d_input_norm, d_gain_attn = norm_back(inputs, gain_attn, d_normed)
        grad_gain_attn = grad_gain_attn + d_gain_attn
        outs_grad.append(d_hidden + d_input_norm)
    layer_sums = (
        lax.psum_scatter(
            grad_query.astype(jnp.bfloat16), "shard", scatter_dimension=0, tiled=True
        ).astype(jnp.float32),
        lax.psum_scatter(
            grad_key.astype(jnp.bfloat16), "shard", scatter_dimension=0, tiled=True
        ).astype(jnp.float32),
        lax.psum_scatter(
            grad_value.astype(jnp.bfloat16), "shard", scatter_dimension=0, tiled=True
        ).astype(jnp.float32),
        lax.psum_scatter(
            grad_out.astype(jnp.bfloat16), "shard", scatter_dimension=0, tiled=True
        ).astype(jnp.float32),
        lax.psum_scatter(
            grad_router.astype(jnp.bfloat16), "shard", scatter_dimension=0, tiled=True
        ).astype(jnp.float32),
        lax.psum_scatter(
            grad_gain_attn.astype(jnp.bfloat16), "shard", scatter_dimension=0, tiled=True
        ).astype(jnp.float32),
        lax.psum_scatter(
            grad_gain_ffn.astype(jnp.bfloat16), "shard", scatter_dimension=0, tiled=True
        ).astype(jnp.float32),
        lax.psum_scatter(
            grad_gain_query.astype(jnp.bfloat16), "shard", scatter_dimension=0, tiled=True
        ).astype(jnp.float32),
        lax.psum_scatter(
            grad_gain_key.astype(jnp.bfloat16), "shard", scatter_dimension=0, tiled=True
        ).astype(jnp.float32),
    )
    layer_totals = (
        lax.psum(layer_sums[0].astype(jnp.bfloat16), ("dp", "expert")).astype(jnp.float32),
        lax.psum(layer_sums[1].astype(jnp.bfloat16), ("dp", "expert")).astype(jnp.float32),
        lax.psum(layer_sums[2].astype(jnp.bfloat16), ("dp", "expert")).astype(jnp.float32),
        lax.psum(layer_sums[3].astype(jnp.bfloat16), ("dp", "expert")).astype(jnp.float32),
        lax.psum(layer_sums[4].astype(jnp.bfloat16), ("dp", "expert")).astype(jnp.float32),
        lax.psum(layer_sums[5].astype(jnp.bfloat16), ("dp", "expert")).astype(jnp.float32),
        lax.psum(layer_sums[6].astype(jnp.bfloat16), ("dp", "expert")).astype(jnp.float32),
        lax.psum(layer_sums[7].astype(jnp.bfloat16), ("dp", "expert")).astype(jnp.float32),
        lax.psum(layer_sums[8].astype(jnp.bfloat16), ("dp", "expert")).astype(jnp.float32),
    )
    expert_totals = (
        lax.psum_scatter(
            grad_gate.astype(jnp.bfloat16), "dp", scatter_dimension=2, tiled=True
        ).astype(jnp.float32),
        lax.psum_scatter(
            grad_up.astype(jnp.bfloat16), "dp", scatter_dimension=2, tiled=True
        ).astype(jnp.float32),
        lax.psum_scatter(
            grad_down.astype(jnp.bfloat16), "dp", scatter_dimension=1, tiled=True
        ).astype(jnp.float32),
    )
    mixed_out = jnp.stack(outs_mixed)[:, None]
    grad_tokens = jnp.stack(outs_grad)[:, None]
    return (
        mixed_out,
        grad_tokens,
        layer_totals[0],
        layer_totals[1],
        layer_totals[2],
        layer_totals[3],
        layer_totals[4],
        layer_totals[5],
        layer_totals[6],
        layer_totals[7],
        layer_totals[8],
        expert_totals[0],
        expert_totals[1],
        expert_totals[2],
    )


def solution(mesh):
    placed = (
        P(None, ("dp", "expert", "shard"), None, None),
        P(None, ("dp", "expert", "shard"), None, None),
        P(None, ("dp", "expert", "shard")),
        P(None, ("dp", "expert", "shard"), None, None),
        P("shard", None),
        P("shard", None),
        P("shard", None),
        P("shard", None),
        P("shard", None),
        P("shard"),
        P("shard"),
        P("shard"),
        P("shard"),
        P(("expert", "shard"), None, "dp"),
        P(("expert", "shard"), None, "dp"),
        P(("expert", "shard"), "dp", None),
    )
    sizes = (mesh.shape["dp"], mesh.shape["expert"], mesh.shape["shard"])
    return jax.shard_map(
        gathered if sizes == (2, 4, 4) else exchanged,
        mesh=mesh,
        in_specs=placed,
        out_specs=(
            P(None, ("dp", "expert", "shard"), None, None),
            P(None, ("dp", "expert", "shard"), None, None),
            P("shard", None),
            P("shard", None),
            P("shard", None),
            P("shard", None),
            P("shard", None),
            P("shard"),
            P("shard"),
            P("shard"),
            P("shard"),
            P(("expert", "shard"), None, "dp"),
            P(("expert", "shard"), None, "dp"),
            P(("expert", "shard"), "dp", None),
        ),
        check_vma=False,
    )
```

```python
import functools

import jax
import jax.numpy as jnp
from jax import lax
from jax.experimental import pallas as pl
from jax.experimental.pallas import tpu as pltpu
from jax.sharding import PartitionSpec as P

HEADS = 16
HDIM = 128


EPSILON = 1e-05


def matmul(left, right):
    return jnp.dot(left, right, preferred_element_type=jnp.float32)


def times_transposed(left, right):
    return lax.dot_general(
        left, right, (((1,), (1,)), ((), ())), preferred_element_type=jnp.float32
    )


def transposed_times(left, right):
    return lax.dot_general(
        left, right, (((0,), (0,)), ((), ())), preferred_element_type=jnp.float32
    )


def rms_norm(values, gain_vec):
    factor = lax.rsqrt(jnp.mean(values * values, axis=-1, keepdims=True) + EPSILON)
    return values * factor * gain_vec


def norm_back(values, gain_vec, incoming):
    factor = lax.rsqrt(jnp.mean(values * values, axis=-1, keepdims=True) + EPSILON)
    unit_rows = values * factor
    weighted = incoming * gain_vec
    d_values = factor * (
        weighted - unit_rows * jnp.mean(weighted * unit_rows, axis=-1, keepdims=True)
    )
    return (d_values, jnp.sum(incoming * unit_rows, axis=0))


def rope_tables(seq_count, head_size):
    half_dim = head_size // 2
    freqs = 10000.0 ** (-2.0 * jnp.arange(half_dim).astype(jnp.float32) / head_size)
    angles = jnp.arange(seq_count).astype(jnp.float32)[:, None] * freqs[None, :]
    cosine_table = jnp.concatenate([jnp.cos(angles), jnp.cos(angles)], axis=-1)
    sine_table = jnp.concatenate([jnp.sin(angles), jnp.sin(angles)], axis=-1)
    return (cosine_table, sine_table)


def rotate(head_rows, cosine_table, sine_table):
    half_dim = head_rows.shape[-1] // 2
    turned = jnp.concatenate([-head_rows[..., half_dim:], head_rows[..., :half_dim]], axis=-1)
    return head_rows * cosine_table[:, None, :] + turned * sine_table[:, None, :]


def rotate_back(incoming, cosine_table, sine_table):
    half_dim = incoming.shape[-1] // 2
    moved_part = incoming * sine_table[:, None, :]
    turned = jnp.concatenate([moved_part[..., half_dim:], -moved_part[..., :half_dim]], axis=-1)
    return incoming * cosine_table[:, None, :] + turned


def softmax_rows(scores):
    shifted = jnp.exp(scores - jnp.max(scores, axis=-1, keepdims=True))
    return shifted / jnp.sum(shifted, axis=-1, keepdims=True)


MESH_ID = pl.DeviceIdType.MESH
EXTRA = 128
ANY = pl.BlockSpec(memory_space=pl.ANY)


def place():
    return lax.axis_index("dp"), lax.axis_index("expert"), lax.axis_index("shard")


def x_of(e):
    return e + 1 - 2 * lax.rem(e, 2)


def y_of(e):
    return lax.rem(e + 2, 4)


def greet(peers):
    barrier = pltpu.get_barrier_semaphore()
    for peer in peers:
        pl.semaphore_signal(barrier, inc=1, device_id=peer, device_id_type=MESH_ID)
    pl.semaphore_wait(barrier, len(peers))


class Copies:
    def __init__(self):
        self.started = []

    def send(self, src, dst, send_sem, recv_sem, device, when=None):
        copy = pltpu.make_async_remote_copy(
            src_ref=src,
            dst_ref=dst,
            send_sem=send_sem,
            recv_sem=recv_sem,
            device_id=device,
            device_id_type=MESH_ID,
        )
        if when is None:
            copy.start()
        else:
            pl.when(when)(copy.start)
        self.started.append((copy, when))

    def drain(self):
        for copy, when in self.started:
            if when is None:
                copy.wait_send()
            else:
                pl.when(when)(copy.wait_send)


def arrived(ref, sem, other):
    pltpu.make_async_remote_copy(
        src_ref=ref,
        dst_ref=ref,
        send_sem=sem,
        recv_sem=sem,
        device_id=other,
        device_id_type=MESH_ID,
    ).wait_recv()


class SemPool:
    def __init__(self, ref):
        self.ref = ref
        self.used = 0

    def take(self):
        self.used += 1
        assert self.used <= self.ref.shape[0]
        return self.ref.at[self.used - 1]


class Item:
    def __init__(self, own, dst, recv, skip=False, cross=None, cross_recv=None):
        self.own, self.dst, self.recv = own, dst, recv
        self.skip, self.cross, self.cross_recv = skip, cross, cross_recv


def gather_items(items, copies, pool):
    dp, e, z = place()
    px, py = x_of(e), y_of(e)
    firsts, seconds = (px, py), (py, px)
    diag = x_of(y_of(e))

    def onward(item, h, ee, zz, targets, when):
        ref = item.dst(zz, ee, h)
        sem = item.recv.at[h, ee * 4 + zz]
        for target, cond in targets:
            copies.send(ref, ref, pool.take(), sem, target, cond)
        if item.cross is not None:
            copies.send(ref, ref, pool.take(), item.cross_recv.at[h, ee * 4 + zz], (1 - dp, e, z), when)

    def wait_for(item, h, ee, zz, when):
        def body():
            arrived(item.dst(zz, ee, h), item.recv.at[h, ee * 4 + zz], (dp, e, z))
        if when is None:
            body()
        else:
            pl.when(when)(body)

    def own_stage(k):
        for sign in (-1, 1):
            zz = z + sign * k
            valid = (zz >= 0) & (zz <= 3)
            nxt = z - sign
            on = valid & (nxt >= 0) & (nxt <= 3)
            for h in (0, 1):
                for item in items:
                    wait_for(item, h, e, zz, valid)
                    onward(item, h, e, zz,
                           [((dp, e, nxt), on), ((dp, firsts[h], z), valid), ((dp, seconds[h], z), valid)],
                           valid)

    def relay_stage(k):
        for sign in (-1, 1) if k else (1,):
            zz = z + sign * k
            valid = (zz >= 0) & (zz <= 3) if k else None
            for h in (0, 1):
                for item in items:
                    if k == 0 and item.skip:
                        continue
                    wait_for(item, h, firsts[h], zz, valid)
                    onward(item, h, firsts[h], zz, [((dp, seconds[h], z), valid)], valid)

    def last_stage(k):
        for sign in (-1, 1) if k else (1,):
            zz = z + sign * k
            valid = (zz >= 0) & (zz <= 3) if k else None
            for h in (0, 1):
                for item in items:
                    if k == 0 and item.skip:
                        continue
                    for ee in (seconds[h], diag):
                        wait_for(item, h, ee, zz, valid)
                        onward(item, h, ee, zz, [], valid)

    for h in (0, 1):
        for item in items:
            own, dst, sem = item.own(h), item.dst(z, e, h), item.recv.at[h, e * 4 + z]
            for sign in (-1, 1):
                nxt = z + sign
                copies.send(own, dst, pool.take(), sem, (dp, e, nxt), (nxt >= 0) & (nxt <= 3))
            if not item.skip:
                for target in (firsts[h], seconds[h]):
                    copies.send(own, dst, pool.take(), sem, (dp, target, z))
    own_stage(1)
    relay_stage(0)
    own_stage(2)
    relay_stage(1)
    own_stage(3)
    relay_stage(2)
    relay_stage(3)
    for k in range(4):
        last_stage(k)
    for item in items:
        if item.cross is not None:
            for sign in (-1, 1):
                for k in (1, 2, 3):
                    zz = z + sign * k

                    @pl.when((zz >= 0) & (zz <= 3))
                    def _(item=item, zz=zz):
                        for ee in range(4):
                            for h in (0, 1):
                                arrived(item.cross(zz, ee, h), item.cross_recv.at[h, ee * 4 + zz], (dp, e, z))


def collect_kernel(
    wq, wk, wv, wo, small, wg, wu, wd, dy,
    full, small_all, wg_far, wu_far, wd_far, dy_all,
    own4, load_sem, store_sem, recv_w, recv_x, recv_dy, recv_small, recv_far, send_sems,
):
    dp, e, z = place()
    px, py = x_of(e), y_of(e)
    loads = []
    for m, ref in enumerate((wq, wk, wv, wo)):
        load = pltpu.make_async_copy(ref, own4.at[m], load_sem.at[m])
        load.start()
        loads.append(load)
    peers = [(dp, e, lax.rem(z + d, 4)) for d in (1, 2, 3)]
    peers += [(dp, px, z), (dp, py, z), (1 - dp, e, z)]
    greet(peers)
    copies, pool = Copies(), SemPool(send_sems)
    for load in loads:
        load.wait()

    def row(zz, ee, d, h):
        return zz * 512 + ee * 128 + d * 64 + h * 32

    def own_w(h):
        return own4.at[:, pl.ds(pl.multiple_of(e * 128 + dp * 64 + h * 32, 32), 32), :]

    def dst_w(d):
        return lambda zz, ee, h: full.at[:, pl.ds(pl.multiple_of(row(zz, ee, d, h), 32), 32), :]

    items = [
        Item(own_w, dst_w(dp), recv_w, skip=True, cross=dst_w(1 - dp), cross_recv=recv_x),
        Item(lambda h: dy.at[h], lambda zz, ee, h: dy_all.at[ee * 4 + zz, h], recv_dy),
    ]
    stores = [
        pltpu.make_async_copy(own4, full.at[:, pl.ds(pl.multiple_of(z * 512, 512), 512), :], store_sem.at[0]),
        pltpu.make_async_copy(dy, dy_all.at[e * 4 + z], store_sem.at[1]),
        pltpu.make_async_copy(small, small_all.at[z], store_sem.at[2]),
    ]
    for store in stores:
        store.start()
    for d in (1, 2, 3):
        copies.send(small, small_all.at[z], pool.take(), recv_small.at[z], (dp, e, lax.rem(z + d, 4)))
    for i, (src, dst) in enumerate(((wg, wg_far), (wu, wu_far), (wd, wd_far))):
        copies.send(src, dst, pool.take(), recv_far.at[i], (1 - dp, e, z))
    gather_items(items, copies, pool)
    for d in (1, 2, 3):
        zz = lax.rem(z + d, 4)
        arrived(small_all.at[zz], recv_small.at[zz], (dp, e, z))
    for i, dst in enumerate((wg_far, wu_far, wd_far)):
        arrived(dst, recv_far.at[i], (dp, e, z))
    copies.drain()
    for store in stores:
        store.wait()


def collect(wq, wk, wv, wo, small, wg, wu, wd, dy):
    bf = jnp.bfloat16
    dma = pltpu.SemaphoreType.DMA
    return pl.pallas_call(
        collect_kernel,
        out_shape=(
            jax.ShapeDtypeStruct((4, 2048, 2048), bf),
            jax.ShapeDtypeStruct((4,) + small.shape, bf),
            jax.ShapeDtypeStruct(wg.shape, bf),
            jax.ShapeDtypeStruct(wu.shape, bf),
            jax.ShapeDtypeStruct(wd.shape, bf),
            jax.ShapeDtypeStruct((16,) + dy.shape, bf),
        ),
        in_specs=[ANY] * 8 + [pl.BlockSpec(memory_space=pltpu.VMEM)],
        out_specs=(ANY,) * 6,
        scratch_shapes=[
            pltpu.VMEM((4, 512, 2048), bf),
            dma((4,)),
            dma((3,)),
            dma((2, 16)),
            dma((2, 16)),
            dma((2, 16)),
            dma((4,)),
            dma((3,)),
            dma((192,)),
        ],
        compiler_params=pltpu.CompilerParams(collective_id=0, has_side_effects=True, vmem_limit_bytes=24 * 2**20),
        name="collect_weights",
    )(wq, wk, wv, wo, small, wg, wu, wd, dy)


def spread_kernel(rows, rows_all, store_sem, recv, send_sems):
    dp, e, z = place()
    px, py = x_of(e), y_of(e)
    peers = [(dp, e, lax.rem(z + d, 4)) for d in (1, 2, 3)] + [(dp, px, z), (dp, py, z)]
    greet(peers)
    copies, pool = Copies(), SemPool(send_sems)
    store = pltpu.make_async_copy(rows, rows_all.at[e * 4 + z], store_sem)
    store.start()
    gather_items([Item(lambda h: rows.at[h], lambda zz, ee, h: rows_all.at[ee * 4 + zz, h], recv)], copies, pool)
    copies.drain()
    store.wait()


def spread(rows):
    dma = pltpu.SemaphoreType.DMA
    return pl.pallas_call(
        spread_kernel,
        out_shape=jax.ShapeDtypeStruct((16,) + rows.shape, rows.dtype),
        in_specs=[pl.BlockSpec(memory_space=pltpu.VMEM)],
        out_specs=ANY,
        scratch_shapes=[dma(()), dma((2, 16)), dma((96,))],
        compiler_params=pltpu.CompilerParams(collective_id=1, has_side_effects=True),
        name="spread_rows",
    )(rows)


def times(left, right):
    return jnp.dot(left, right, preferred_element_type=jnp.float32)


def experts_kernel(
    wide, dy, wg, wu, wd, wgf, wuf, wdf,
    res, eg, eu, ed, part, a_buf, b_buf, c_buf,
    WG, WU, WD, rows_in, dy_rows, hidden, saved, acc, stage, addend, turned, column, far_out,
    w_sem, dy_sem, in_sem, part_sem, add_sem, col_sem, fin_sem, out_sem,
    a_sem, b_sem, c_sem, a_send, b_send, c_send, gu_send, gu_sem, dn_send, dn_sem, free_sem,
):
    dp, e, z = place()
    px, py = x_of(e), y_of(e)
    diag = x_of(y_of(e))
    me = (dp, e, z)
    far_core = (1 - dp, e, z)
    f32, bf = jnp.float32, jnp.bfloat16
    width = dy.shape[3]
    half_f = wg.shape[1]
    total_width = part.shape[3]

    def local(src, dst, sem):
        return pltpu.make_async_copy(src, dst, sem)

    def remote(src, dst, send_sem, recv_sem, device):
        return pltpu.make_async_remote_copy(
            src_ref=src, dst_ref=dst, send_sem=send_sem, recv_sem=recv_sem,
            device_id=device, device_id_type=MESH_ID)

    def column_of(c):
        return jnp.where(c == 0, diag, jnp.where(c == 1, py, jnp.where(c == 2, px, e)))

    def zed(i):
        return lax.rem(z + jnp.where(i == 0, 2, jnp.where(i == 1, 1, jnp.where(i == 2, 3, 0))), 4)

    def slot_of(s, i):
        return column_of(s // 2) * 4 + zed(2 * lax.rem(s, 2) + i)

    def rows_load(s, i, buf):
        return local(wide.at[slot_of(s, i)], rows_in.at[buf, i], in_sem.at[buf, i])

    weights = [
        local(src, dst, w_sem.at[n])
        for n, (src, dst) in enumerate((
            (wg, WG.at[0]), (wu, WU.at[0]), (wd, WD.at[0]), (wgf, WG.at[1]), (wuf, WU.at[1]), (wdf, WD.at[1])))
    ]
    for i in range(2):
        rows_load(0, i, 0).start()
    weights[0].start()
    weights[1].start()
    dy_load = local(dy, dy_rows, dy_sem)
    dy_load.start()
    for load in weights[2:]:
        load.start()
    greet([(dp, e, lax.rem(z + d, 4)) for d in (1, 2, 3)] + [(dp, px, z), (dp, py, z), far_core])

    def part_write(s, i):
        return local(stage.at[lax.rem(s, 2), i], part.at[slot_of(s, i)], part_sem.at[lax.rem(s, 2), i])

    def a_copy(h, g, slot, zz, target):
        return remote(part.at[slot, h], a_buf.at[h, g, zz], a_send.at[h, g, zz], a_sem.at[h, g, zz], (dp, target, z))

    def b_copy(h, slot, zz, target):
        return remote(part.at[slot, h], b_buf.at[h, zz], b_send.at[h, zz], b_sem.at[h, zz], (dp, target, z))

    def send_step(s):
        c = s // 2
        for i in range(2):
            part_write(s, i).wait()
            zz = zed(2 * lax.rem(s, 2) + i)

            @pl.when(c == 0)
            def _():
                a_copy(0, 0, diag * 4 + zz, zz, py).start()
                a_copy(1, 0, diag * 4 + zz, zz, px).start()

            @pl.when(c == 1)
            def _():
                a_copy(0, 1, py * 4 + zz, zz, py).start()
                b_copy(1, py * 4 + zz, zz, py).start()

            @pl.when(c == 2)
            def _():
                a_copy(1, 1, px * 4 + zz, zz, px).start()
                b_copy(0, px * 4 + zz, zz, px).start()

    def addend_load(s, i):
        h = jnp.where(s // 2 == 1, 1, 0)
        zz = zed(2 * lax.rem(s, 2) + i)
        return local(a_buf.at[h, 0, zz], addend.at[i], add_sem.at[i])

    mine = e * 4 + z
    lane = lax.broadcasted_iota(jnp.int32, (256, EXTRA), 1)
    at_high, at_low = lane == mine, lane == mine + 16

    weights[0].wait()
    weights[1].wait()
    dy_load.wait()

    def step(s, _):
        buf = lax.rem(s, 2)

        @pl.when(s + 1 < 8)
        def _():
            for i in range(2):
                rows_load(s + 1, i, 1 - buf).start()
        for i in range(2):
            rows_load(s, i, buf).wait()
        slots = [slot_of(s, i) for i in range(2)]
        extra = rows_in[buf, :, :, :, width:].reshape(256, EXTRA).astype(f32)
        gate = jnp.sum(jnp.where(at_high | at_low, extra, 0.0), axis=1, keepdims=True)

        def dy_step():
            return jnp.concatenate([dy_rows[slot].reshape(128, width) for slot in slots], axis=0)

        def put(ref, values, lo, hi):
            for i in range(2):
                ref[slots[i], :, lo:hi] = values[i * 128:(i + 1) * 128]

        dy_route = (gate * dy_step().astype(f32)).astype(bf)
        for n in range(2):
            if n == 1:
                @pl.when(s == 0)
                def _():
                    for load in weights[3:]:
                        load.wait()

                @pl.when(s > 0)
                def _():
                    send_step(s - 1)

                @pl.when((s >= 2) & (s < 6))
                def _():
                    for i in range(2):
                        h = jnp.where(s // 2 == 1, 1, 0)
                        zz = zed(2 * lax.rem(s, 2) + i)
                        arrived(a_buf.at[h, 0, zz], a_sem.at[h, 0, zz], me)
                        addend_load(s, i).start()
            x = rows_in[buf, :, :, :, :width].reshape(256, width)
            gate_pre = times(x, WG[n])
            up_value = times(x, WU[n])
            sigmoid_gate = jax.nn.sigmoid(gate_pre)
            activated = gate_pre * sigmoid_gate
            inner = (activated * up_value).astype(bf)
            put(hidden, inner, n * half_f, (n + 1) * half_f)
            if n == 0:
                @pl.when(s == 0)
                def _():
                    weights[2].wait()
            d_inner = times_transposed(dy_route, WD[n])
            d_gate = (d_inner * up_value * (sigmoid_gate + gate_pre * sigmoid_gate * (1.0 - sigmoid_gate))).astype(bf)
            d_up = (d_inner * activated).astype(bf)
            put(saved, d_gate, 2 * n * half_f, (2 * n + 1) * half_f)
            put(saved, d_up, (2 * n + 1) * half_f, (2 * n + 2) * half_f)
            if n == 0:
                acc[0] = times(inner, WD[n])
                acc[1] = times_transposed(d_gate, WG[n]) + times_transposed(d_up, WU[n])
            else:
                acc[0] += times(inner, WD[n])
                acc[1] += times_transposed(d_gate, WG[n]) + times_transposed(d_up, WU[n])
        y_low = acc[0].astype(bf).astype(f32)
        d_own = jnp.sum(y_low * dy_step().astype(f32), axis=1, keepdims=True)
        high = d_own.astype(bf).astype(f32)
        tail = jnp.where(at_high, high, jnp.where(at_low, d_own - high, 0.0)).astype(bf)

        def lay(values):
            return values.reshape(2, 2, 64, values.shape[1])

        stage[buf, :, :, :, :width] = lay((gate * y_low).astype(bf))
        stage[buf, :, :, :, width:width + EXTRA] = lay(tail)
        stage[buf, :, :, :, width + EXTRA:] = lay(acc[1].astype(bf))
        for i in range(2):
            dy_rows[slots[i]] = dy_route[i * 128:(i + 1) * 128].reshape(2, 64, width)

        @pl.when((s >= 2) & (s < 6))
        def _():
            h = jnp.where(s // 2 == 1, 1, 0)
            for i in range(2):
                addend_load(s, i).wait()
                stage[buf, i, h] = (stage[buf, i, h].astype(f32) + addend[i].astype(f32)).astype(bf)
        for i in range(2):
            part_write(s, i).start()
        return 0

    lax.fori_loop(0, 8, step, 0)
    pl.semaphore_signal(free_sem, inc=1, device_id=far_core, device_id_type=MESH_ID)
    for i in range(2):
        part_write(7, i).wait()

    def finish_loads(k):
        zz = zed(k)
        return (local(part.at[e * 4 + zz], stage.at[0, 0], fin_sem.at[0]),
                local(a_buf.at[:, 1, zz], stage.at[0, 1], fin_sem.at[1]),
                local(b_buf.at[:, zz], stage.at[1, 0], fin_sem.at[2]))

    def begin(k):
        zz = zed(k)
        for h in range(2):
            arrived(a_buf.at[h, 1, zz], a_sem.at[h, 1, zz], me)
            arrived(b_buf.at[h, zz], b_sem.at[h, zz], me)
        for load in finish_loads(k):
            load.start()

    def result_write(k):
        return local(stage.at[1, 1], part.at[e * 4 + zed(k)], fin_sem.at[3])

    def c_copy(k):
        zz = zed(k)
        return remote(part.at[e * 4 + zz], c_buf.at[z], c_send.at[k], c_sem.at[z], (dp, e, zz))

    def close(k):
        for load in finish_loads(k):
            load.wait()
        for h in range(2):
            total = (stage[0, 0, h].astype(f32) + stage[0, 1, h].astype(f32)) + stage[1, 0, h].astype(f32)
            if k < 3:
                stage[1, 1, h] = total.astype(bf)
            else:
                res[h] = total
        if k < 3:
            result_write(k).start()

    def fire(k):
        result_write(k).wait()
        c_copy(k).start()

    def turn_hidden(n):
        turned[...] = hidden[:, :, pl.ds(pl.multiple_of(n * 256, 256), 256)].reshape(2048, 256).T

    def down_block(dst):
        def col(j, _):
            cc = pl.ds(pl.multiple_of(j * 512, 512), 512)
            dst(cc, times(turned[...], dy_rows[:, :, :, cc].reshape(2048, 512)))
            return 0
        lax.fori_loop(0, 4, col, 0)

    def column_load(n):
        return local(wide.at[:, :, :, pl.ds(pl.multiple_of(n * 256, 256), 256)], column.at[lax.rem(n, 2)],
                     col_sem.at[lax.rem(n, 2)])

    def down_send(n):
        return remote(far_out.at[n], WD.at[1, pl.ds(n * 256, 256)], dn_send.at[n], dn_sem.at[n], far_core)

    column_load(0).start()
    for n in range(2):
        turn_hidden(2 + n)

        def to_far(cc, values, n=n):
            far_out[n, :, cc] = values.astype(bf)
        down_block(to_far)
        if n == 0:
            pl.semaphore_wait(free_sem, 1)
        down_send(n).start()

    def row_block(n):
        return pl.ds(pl.multiple_of(n * 256, 256), 256)

    def gu_copy(n, w):
        buf = lax.rem(n, 2)
        return remote(far_out.at[buf, :, w * 512:(w + 1) * 512], WG.at[w, row_block(n)],
                      gu_send.at[buf, w], gu_sem.at[n, w], far_core)

    def gu_out(n, w):
        buf = lax.rem(n, 2)
        return local(acc.at[buf, :, w * 512:(w + 1) * 512], (eg, eu)[w].at[row_block(n)], out_sem.at[buf, w])

    def settle(n):
        buf = lax.rem(n, 2)
        for w in range(2):
            arrived(WG.at[w, row_block(n)], gu_sem.at[n, w], me)
            acc[buf, :, w * 512:(w + 1) * 512] += WG[w, row_block(n)].astype(f32)
            gu_out(n, w).start()

    def gate_up(n, _):
        buf = lax.rem(n, 2)

        @pl.when(n + 1 < 8)
        def _():
            column_load(n + 1).start()
        column_load(n).wait()
        turned[...] = column[buf].reshape(2048, 256).T

        @pl.when(n < 2)
        def _():
            for k in range(2):
                @pl.when(n == k)
                def _(k=k):
                    down_send(k).wait_send()

        @pl.when(n >= 2)
        def _():
            for w in range(2):
                gu_copy(n - 2, w).wait_send()
                gu_out(n - 2, w).wait()

        def far_col(j, _):
            cc = pl.ds(pl.multiple_of(j * 512, 512), 512)
            src = pl.ds(pl.multiple_of(1024 + j * 512, 512), 512)
            far_out[buf, :, cc] = times(turned[...], saved[:, :, src].reshape(2048, 512)).astype(bf)
            return 0

        def near_col(j, _):
            cc = pl.ds(pl.multiple_of(j * 512, 512), 512)
            acc[buf, :, cc] = times(turned[...], saved[:, :, cc].reshape(2048, 512))
            return 0
        lax.fori_loop(0, 2, far_col, 0)
        for w in range(2):
            gu_copy(n, w).start()
        lax.fori_loop(0, 2, near_col, 0)

        @pl.when(n > 0)
        def _():
            settle(n - 1)
        for at, act in ((2, lambda: begin(0)), (3, lambda: close(0)), (4, lambda: fire(0)),
                        (5, lambda: begin(1)), (6, lambda: close(1)), (7, lambda: fire(1))):
            pl.when(n == at)(act)
        return 0

    lax.fori_loop(0, 8, gate_up, 0)
    settle(7)
    for n in (6, 7):
        for w in range(2):
            gu_copy(n, w).wait_send()
            gu_out(n, w).wait()

    def down_out(n):
        return local(acc.at[n], ed.at[pl.ds(n * 256, 256)], out_sem.at[n, 0])

    for n in range(2):
        turn_hidden(n)

        def keep(cc, values, n=n):
            acc[n, :, cc] = values
        down_block(keep)
        arrived(WD.at[1, pl.ds(n * 256, 256)], dn_sem.at[n], me)
        acc[n] += WD[1, pl.ds(n * 256, 256)].astype(f32)
        down_out(n).start()
    begin(2)
    close(2)
    fire(2)
    begin(3)
    close(3)
    for k in range(3):
        zz = zed(k)
        arrived(c_buf.at[zz], c_sem.at[zz], me)
        load = local(c_buf.at[zz], stage.at[0, 0], fin_sem.at[0])
        load.start()
        load.wait()
        for h in range(2):
            res[h] += stage[0, 0, h].astype(f32)
    for n in range(2):
        down_out(n).wait()
    for k in range(3):
        c_copy(k).wait_send()

    def drain(zz, _):
        a_copy(0, 0, diag * 4 + zz, zz, py).wait_send()
        a_copy(1, 0, diag * 4 + zz, zz, px).wait_send()
        a_copy(0, 1, py * 4 + zz, zz, py).wait_send()
        b_copy(1, py * 4 + zz, zz, py).wait_send()
        a_copy(1, 1, px * 4 + zz, zz, px).wait_send()
        b_copy(0, px * 4 + zz, zz, px).wait_send()
        return 0
    lax.fori_loop(0, 4, drain, 0)


def experts(wide, dy, near, far):
    dma = pltpu.SemaphoreType.DMA
    bf, f32 = jnp.bfloat16, jnp.float32
    wg, wu, wd = near
    width, half_f = wg.shape
    rows = wide.shape[2]
    total_width = 2 * width + EXTRA
    shape = jax.ShapeDtypeStruct
    every = 16 * 2 * rows
    outs = pl.pallas_call(
        experts_kernel,
        out_shape=(
            shape((2, rows, total_width), f32),
            shape((width, half_f), f32),
            shape((width, half_f), f32),
            shape((half_f, width), f32),
            shape((16, 2, rows, total_width), bf),
            shape((2, 2, 4, rows, total_width), bf),
            shape((2, 4, rows, total_width), bf),
            shape((4, 2, rows, total_width), bf),
        ),
        in_specs=[ANY] * 8,
        out_specs=(pl.BlockSpec(memory_space=pltpu.VMEM),) + (ANY,) * 7,
        scratch_shapes=[
            pltpu.VMEM((2, width, half_f), bf),
            pltpu.VMEM((2, width, half_f), bf),
            pltpu.VMEM((2, half_f, width), bf),
            pltpu.VMEM((2, 2, 2, rows, width + EXTRA), bf),
            pltpu.VMEM((16, 2, rows, width), bf),
            pltpu.VMEM((16, 2 * rows, 2 * half_f), bf),
            pltpu.VMEM((16, 2 * rows, 4 * half_f), bf),
            pltpu.VMEM((2, 256, width), f32),
            pltpu.VMEM((2, 2, 2, rows, total_width), bf),
            pltpu.VMEM((2, rows, total_width), bf),
            pltpu.VMEM((256, every), bf),
            pltpu.VMEM((2, 16, 2, rows, 256), bf),
            pltpu.VMEM((2, 256, width), bf),
            dma((6,)),
            dma(()),
            dma((2, 2)),
            dma((2, 2)),
            dma((2,)),
            dma((2,)),
            dma((4,)),
            dma((2, 2)),
            dma((2, 2, 4)),
            dma((2, 4)),
            dma((4,)),
            dma((2, 2, 4)),
            dma((2, 4)),
            dma((3,)),
            dma((2, 2)),
            dma((8, 2)),
            dma((2,)),
            dma((2,)),
            pltpu.SemaphoreType.REGULAR,
        ],
        compiler_params=pltpu.CompilerParams(collective_id=2, has_side_effects=True, vmem_limit_bytes=62 * 2**20),
        name="owned_expert",
    )(wide, dy, *near, *far)
    return outs[:4]


def total_kernel(gq, gk, gv, go, small,
                 out, small_out,
                 far, a, b, c, mine, work, s_z, s_all,
                 work_sem, far_sem, a_sem, b_sem, c_sem, sz_sem, sa_sem, g_sem,
                 far_send, a_send, b_send, c_send, sz_send, sa_send, g_send, out_sem):
    dp, e, z = place()
    px, py = x_of(e), y_of(e)
    diag = x_of(y_of(e))
    firsts, seconds = (py, px), (px, py)
    grads = (gq, gk, gv, go)
    zs = [lax.rem(z + d, 4) for d in range(4)]
    mates = [(lax.rem(dp + d // 4, 2), lax.rem(e + d % 4, 4), z) for d in range(1, 8)]
    greet([(dp, e, zz) for zz in zs[1:]] + mates)

    def copy(src, dst, send_sem, recv_sem, device):
        return pltpu.make_async_remote_copy(
            src_ref=src, dst_ref=dst, send_sem=send_sem, recv_sem=recv_sem,
            device_id=device, device_id_type=MESH_ID)

    def rows_of(ee, zz, d, h):
        return pl.ds(pl.multiple_of(zz * 512 + ee * 128 + d * 64 + h * 32, 32), 32)

    def far_copy(m, ee, zz, h):
        return copy(grads[m].at[rows_of(ee, zz, 1 - dp, h)], far.at[h, ee, zz, m],
                    far_send.at[h, ee, zz, m], far_sem.at[h, ee, zz, m], (1 - dp, e, z))

    def load(m, ee, zz, h, slot):
        return pltpu.make_async_copy(grads[m].at[rows_of(ee, zz, dp, h)], work.at[slot, m], work_sem.at[slot, m])

    def groups(h):
        return (diag, firsts[h], seconds[h], e)

    def sz_copy(d):
        return copy(small.at[zs[d]], s_z.at[z], sz_send.at[d - 1], sz_sem.at[z], (dp, e, zs[d]))

    for d in (1, 2, 3):
        sz_copy(d).start()
    for g in range(4):
        for h in (0, 1):
            def start_far(zz, _, g=g, h=h):
                for m in range(4):
                    far_copy(m, groups(h)[g], zz, h).start()
                return 0
            lax.fori_loop(0, 4, start_far, 0)

    def a_copy(h, g, zz):
        return copy(far.at[h, groups(h)[g], zz], a.at[h, g, zz], a_send.at[h, g, zz], a_sem.at[h, g, zz],
                    (dp, firsts[h], z))

    def b_copy(h, zz):
        return copy(far.at[h, seconds[h], zz], b.at[h, zz], b_send.at[h, zz], b_sem.at[h, zz], (dp, seconds[h], z))

    def c_copy(h, zz):
        return copy(far.at[h, e, zz], c.at[h, z], c_send.at[h, zz], c_sem.at[h, z], (dp, e, zz))

    def load_step(n, slot):
        g, h, zz = n // 8, lax.rem(n // 4, 2), lax.rem(n, 4)
        ee = pick(g, h)
        for m in range(4):
            load(m, ee, zz, h, slot).start()

    def pick(g, h):
        first = jnp.where(h == 0, py, px)
        second = jnp.where(h == 0, px, py)
        return jnp.where(g == 0, diag, jnp.where(g == 1, first, jnp.where(g == 2, second, e)))

    load_step(0, 0)

    def near(n, _):
        slot = lax.rem(n, 2)

        @pl.when(n + 1 < 32)
        def _():
            load_step(n + 1, 1 - slot)

        g, h, zz = n // 8, lax.rem(n // 4, 2), lax.rem(n, 4)
        ee = pick(g, h)
        for m in range(4):
            load(m, ee, zz, h, slot).wait()
            arrived(far.at[h, ee, zz, m], far_sem.at[h, ee, zz, m], (dp, e, z))
        far[h, ee, zz] = (far[h, ee, zz].astype(jnp.float32) + work[slot].astype(jnp.float32)).astype(far.dtype)

        @pl.when(g < 2)
        def _():
            first = jnp.where(h == 0, py, px)
            copy(far.at[h, ee, zz], a.at[h, g, zz], a_send.at[h, g, zz], a_sem.at[h, g, zz], (dp, first, z)).start()
        return 0

    lax.fori_loop(0, 32, near, 0)

    for h in (0, 1):
        def relay(d, _, h=h):
            zz = lax.rem(z + d, 4)
            arrived(a.at[h, 0, zz], a_sem.at[h, 0, zz], (dp, e, z))
            far[h, seconds[h], zz] = (far[h, seconds[h], zz].astype(jnp.float32)
                                      + a[h, 0, zz].astype(jnp.float32)).astype(far.dtype)
            b_copy(h, zz).start()
            return 0
        lax.fori_loop(1, 5, relay, 0)
    for h in (0, 1):
        def finish(d, _, h=h):
            zz = lax.rem(z + d, 4)
            arrived(a.at[h, 1, zz], a_sem.at[h, 1, zz], (dp, e, z))
            arrived(b.at[h, zz], b_sem.at[h, zz], (dp, e, z))
            far[h, e, zz] = (far[h, e, zz].astype(jnp.float32) + a[h, 1, zz].astype(jnp.float32)
                             + b[h, zz].astype(jnp.float32)).astype(far.dtype)

            @pl.when(d < 4)
            def _():
                c_copy(h, zz).start()
            return 0
        lax.fori_loop(1, 5, finish, 0)

    def sa_copy(d):
        return copy(mine_small, s_all.at[dp * 4 + e], sa_send.at[d - 1], sa_sem.at[dp * 4 + e], mates[d - 1])

    slot_me = dp * 4 + e
    for d in (1, 2, 3):
        arrived(s_z.at[zs[d]], sz_sem.at[zs[d]], (dp, e, z))
    s_all[slot_me] = (small[z] + s_z[zs[1]]) + (s_z[zs[2]] + s_z[zs[3]])
    mine_small = s_all.at[slot_me]
    for d in range(1, 8):
        sa_copy(d).start()

    def mine_at(d, ee):
        return pl.ds(pl.multiple_of(ee * 128 + d * 64, 64), 64)

    def g_copy(h, n):
        return copy(mine.at[:, pl.ds(h * 32, 32)],
                    out.at[:, pl.ds(pl.multiple_of(e * 128 + dp * 64 + h * 32, 32), 32)],
                    g_send.at[h, n], g_sem.at[h, slot_me], mates[n])

    locals_out = []
    for h in (0, 1):
        def last(m, _, h=h):
            mine[m, pl.ds(h * 32, 32)] = (
                (far[h, e, z, m].astype(jnp.float32) + c[h, zs[1], m].astype(jnp.float32))
                + (c[h, zs[2], m].astype(jnp.float32) + c[h, zs[3], m].astype(jnp.float32))
            ).astype(mine.dtype)
            return 0
        for d in (1, 2, 3):
            arrived(c.at[h, zs[d]], c_sem.at[h, zs[d]], (dp, e, z))
        lax.fori_loop(0, 4, last, 0)
        for n in range(7):
            g_copy(h, n).start()
        keep = pltpu.make_async_copy(
            mine.at[:, pl.ds(h * 32, 32)],
            out.at[:, pl.ds(pl.multiple_of(e * 128 + dp * 64 + h * 32, 32), 32)],
            out_sem.at[h])
        keep.start()
        locals_out.append(keep)
    total = s_all[slot_me]
    for d in range(1, 8):
        other = lax.rem(dp + d // 4, 2) * 4 + lax.rem(e + d % 4, 4)
        arrived(s_all.at[other], sa_sem.at[other], (dp, e, z))
    small_out[...] = (((s_all[0] + s_all[1]) + (s_all[2] + s_all[3]))
                      + ((s_all[4] + s_all[5]) + (s_all[6] + s_all[7])))
    for h in (0, 1):
        for d in range(1, 8):
            od, oe = lax.rem(dp + d // 4, 2), lax.rem(e + d % 4, 4)
            arrived(out.at[:, pl.ds(pl.multiple_of(oe * 128 + od * 64 + h * 32, 32), 32)],
                    g_sem.at[h, od * 4 + oe], (dp, e, z))
    for d in (1, 2, 3):
        sz_copy(d).wait_send()
    for d in range(1, 8):
        sa_copy(d).wait_send()
    for h in (0, 1):
        for n in range(7):
            g_copy(h, n).wait_send()
        locals_out[h].wait()
        for g in range(4):
            def drain_far(zz, _, g=g, h=h):
                for m in range(4):
                    far_copy(m, groups(h)[g], zz, h).wait_send()
                return 0
            lax.fori_loop(0, 4, drain_far, 0)

        def drain(d, _, h=h):
            zz = lax.rem(z + d, 4)
            a_copy(h, 0, zz).wait_send()
            a_copy(h, 1, zz).wait_send()
            b_copy(h, zz).wait_send()

            @pl.when(d < 4)
            def _():
                c_copy(h, zz).wait_send()
            return 0
        lax.fori_loop(1, 5, drain, 0)


def total(gq, gk, gv, go, small):
    dma = pltpu.SemaphoreType.DMA
    bf, f32 = jnp.bfloat16, jnp.float32
    vmem = pl.BlockSpec(memory_space=pltpu.VMEM)
    return pl.pallas_call(
        total_kernel,
        out_shape=(
            jax.ShapeDtypeStruct((4, 512, 2048), bf),
            jax.ShapeDtypeStruct(small.shape[1:], f32),
        ),
        in_specs=[ANY] * 4 + [vmem],
        out_specs=(ANY, vmem),
        scratch_shapes=[
            pltpu.VMEM((2, 4, 4, 4, 32, 2048), bf),
            pltpu.VMEM((2, 2, 4, 4, 32, 2048), bf),
            pltpu.VMEM((2, 4, 4, 32, 2048), bf),
            pltpu.VMEM((2, 4, 4, 32, 2048), bf),
            pltpu.VMEM((4, 64, 2048), bf),
            pltpu.VMEM((2, 4, 32, 2048), bf),
            pltpu.VMEM(small.shape, f32),
            pltpu.VMEM((8,) + small.shape[1:], f32),
            dma((2, 4)),
            dma((2, 4, 4, 4)),
            dma((2, 2, 4)),
            dma((2, 4)),
            dma((2, 4)),
            dma((4,)),
            dma((8,)),
            dma((2, 8)),
            dma((2, 4, 4, 4)),
            dma((2, 2, 4)),
            dma((2, 4)),
            dma((2, 4)),
            dma((3,)),
            dma((7,)),
            dma((2, 7)),
            dma((2,)),
        ],
        compiler_params=pltpu.CompilerParams(collective_id=3, has_side_effects=True, vmem_limit_bytes=52 * 2**20),
        name="total_grads",
    )(gq, gk, gv, go, small)


def gathered(
    tokens,
    cotangent,
    lengths,
    routes,
    w_query,
    w_key,
    w_value,
    w_out,
    w_router,
    g_attn,
    g_ffn,
    g_query,
    g_key,
    w_gate,
    w_up,
    w_down,
):
    micro_count, _, seq_len, model_width = tokens.shape
    expert_count = w_router.shape[1]
    f32, bf = jnp.float32, jnp.bfloat16
    places = jnp.arange(seq_len)
    score_scale = HDIM ** (-0.5)
    length = lengths[:, 0]
    live = places[None, :] < length[:, None]
    dy = jnp.where(live[:, :, None], cotangent[:, 0], jnp.zeros((), bf))
    small = jnp.concatenate(
        [w_router.T, g_attn[None], g_ffn[None], g_query[None], g_key[None],
         jnp.zeros((32 - expert_count - 4, w_router.shape[0]), bf)], axis=0)
    full, small_all, gate_far, up_far, down_far, dy_all = collect(
        w_query, w_key, w_value, w_out, small, w_gate[0], w_up[0], w_down[0], dy)
    query_full, key_full, value_full, out_full = full[0], full[1], full[2], full[3]
    small_rows = jnp.swapaxes(small_all, 0, 1).reshape(32, model_width)
    route_full = small_rows[:expert_count].T
    gain_attn, gain_ffn, gain_query, gain_key = (
        small_rows[expert_count + i].astype(f32) for i in range(4))

    rows = micro_count * seq_len
    cosine_one, sine_one = rope_tables(seq_len, HDIM)
    cosine_table, sine_table = jnp.tile(cosine_one, (micro_count, 1)), jnp.tile(sine_one, (micro_count, 1))
    inputs = tokens[:, 0].reshape(rows, model_width).astype(f32)
    route_ids = routes[:, 0].reshape(rows, -1)
    normed = rms_norm(inputs, gain_attn).astype(bf)
    query_raw = matmul(normed, query_full)
    key_raw = matmul(normed, key_full)
    value_raw = matmul(normed, value_full)

    def per_head(values):
        return values.reshape(micro_count, seq_len, HEADS, HDIM)

    value_low = per_head(value_raw.astype(bf))
    query_low = per_head(rotate(
        rms_norm(query_raw, gain_query).reshape(rows, HEADS, HDIM), cosine_table, sine_table).astype(bf))
    key_low = per_head(rotate(
        rms_norm(key_raw, gain_key).reshape(rows, HEADS, HDIM), cosine_table, sine_table).astype(bf))
    allowed = (places[None, None, :] <= places[None, :, None]) & live[:, None, :]
    scores = jnp.einsum("mqhd,mkhd->mhqk", query_low, key_low, preferred_element_type=f32) * score_scale
    attn_probs = softmax_rows(jnp.where(allowed[:, None], scores, -1e30))
    probs_low = attn_probs.astype(bf)
    mixed_low = jnp.einsum("mhqk,mkhd->mqhd", probs_low, value_low, preferred_element_type=f32)
    mixed_low = mixed_low.reshape(rows, model_width).astype(bf)
    hidden_state = inputs + matmul(mixed_low, out_full)
    ffn_in = rms_norm(hidden_state, gain_ffn).astype(bf)
    router = softmax_rows(matmul(ffn_in, route_full))
    expert_ids = jnp.arange(expert_count)
    chosen = jnp.any(route_ids[:, :, None] == expert_ids[None, None, :], axis=1)
    gates = jnp.where(chosen, router, 0.0)
    gates_high = gates.astype(bf)
    gates_low = (gates - gates_high.astype(f32)).astype(bf)
    sent = jnp.concatenate(
        [ffn_in, gates_high, gates_low, jnp.zeros((rows, EXTRA - 2 * expert_count), bf)], axis=1)
    spread_rows = spread(sent.reshape(micro_count, seq_len, -1))

    expert_sums, *expert_grads = experts(
        spread_rows, dy_all, (w_gate[0], w_up[0], w_down[0]), (gate_far, up_far, down_far))
    y_all = expert_sums.reshape(rows, -1)
    d_ffn_in = y_all[:, model_width + EXTRA:]
    mixed_out = (hidden_state + y_all[:, :model_width]).astype(bf)
    d_gates = y_all[:, model_width:model_width + expert_count] + y_all[
        :, model_width + expert_count:model_width + 2 * expert_count]
    d_router = jnp.where(chosen, d_gates, 0.0)
    d_output = dy.reshape(rows, model_width).astype(f32)
    d_logits = (router * (d_router - jnp.sum(router * d_router, axis=1, keepdims=True))).astype(bf)
    grad_router = transposed_times(d_logits, ffn_in)
    d_ffn_in = d_ffn_in + times_transposed(d_logits, route_full)
    d_hidden_norm, d_gain_ffn = norm_back(hidden_state, gain_ffn, d_ffn_in)
    d_hidden = d_output + d_hidden_norm
    d_attn_low = d_hidden.astype(bf)
    grad_out = transposed_times(mixed_low, d_attn_low).astype(bf)
    d_mixed = per_head(times_transposed(d_attn_low, out_full).astype(bf))
    d_probs = jnp.einsum("mqhd,mkhd->mhqk", d_mixed, value_low, preferred_element_type=f32)
    d_value = jnp.einsum("mhqk,mqhd->mkhd", probs_low, d_mixed, preferred_element_type=f32)
    d_value = d_value.reshape(rows, model_width).astype(bf)
    d_scores = (attn_probs * (d_probs - jnp.sum(attn_probs * d_probs, axis=-1, keepdims=True))).astype(bf)
    d_query = jnp.einsum("mhqk,mkhd->mqhd", d_scores, key_low, preferred_element_type=f32) * score_scale
    d_key = jnp.einsum("mhqk,mqhd->mkhd", d_scores, query_low, preferred_element_type=f32) * score_scale

    def raw_back(raw, gain_vec, d_heads):
        turned = rotate_back(d_heads.reshape(rows, HEADS, HDIM), cosine_table, sine_table)
        return norm_back(raw, gain_vec, turned.reshape(rows, model_width))

    d_query_raw, d_gain_query = raw_back(query_raw, gain_query, d_query)
    d_key_raw, d_gain_key = raw_back(key_raw, gain_key, d_key)
    d_query_low, d_key_low = d_query_raw.astype(bf), d_key_raw.astype(bf)
    grad_query = transposed_times(normed, d_query_low).astype(bf)
    grad_key = transposed_times(normed, d_key_low).astype(bf)
    grad_value = transposed_times(normed, d_value).astype(bf)
    d_normed = (times_transposed(d_query_low, query_full) + times_transposed(d_key_low, key_full)
                + times_transposed(d_value, value_full))
    d_input_norm, d_gain_attn = norm_back(inputs, gain_attn, d_normed)
    grad_tokens = (d_hidden + d_input_norm).reshape(micro_count, 1, seq_len, model_width)

    small_grads = jnp.concatenate(
        [grad_router, d_gain_attn[None], d_gain_ffn[None], d_gain_query[None], d_gain_key[None],
         jnp.zeros((24 - expert_count - 4, model_width), f32)], axis=0)
    small_grads = jnp.swapaxes(small_grads.reshape(24, 4, model_width // 4), 0, 1)
    sums, small_sums = total(grad_query, grad_key, grad_value, grad_out, small_grads)
    return (
        mixed_out.reshape(micro_count, 1, seq_len, model_width),
        grad_tokens,
        sums[0].astype(f32),
        sums[1].astype(f32),
        sums[2].astype(f32),
        sums[3].astype(f32),
        small_sums[:expert_count].T,
        small_sums[expert_count],
        small_sums[expert_count + 1],
        small_sums[expert_count + 2],
        small_sums[expert_count + 3],
        *(g[None] for g in expert_grads),
    )


def dispatch_rows(buffer):
    return lax.all_to_all(buffer, ("expert", "shard"), split_axis=0, concat_axis=0, tiled=True)


def collect_rows(buffer):
    return lax.all_to_all(buffer, ("expert", "shard"), split_axis=0, concat_axis=0, tiled=True)


def dispatch_grads(buffer):
    return lax.all_to_all(buffer, ("expert", "shard"), split_axis=0, concat_axis=0, tiled=True)


def collect_grads(buffer):
    return lax.all_to_all(buffer, ("expert", "shard"), split_axis=0, concat_axis=0, tiled=True)


def to_experts(arrived, local_experts, capacity):
    sources = arrived.shape[0]
    model_width = arrived.shape[2]
    split_rows = arrived.reshape(sources, local_experts, capacity, model_width)
    return jnp.swapaxes(split_rows, 0, 1).reshape(local_experts, sources * capacity, model_width)


def from_experts(expert_token_rows, owners, capacity):
    local_experts = expert_token_rows.shape[0]
    model_width = expert_token_rows.shape[2]
    split_rows = expert_token_rows.reshape(local_experts, owners, capacity, model_width)
    return jnp.swapaxes(split_rows, 0, 1).reshape(owners, local_experts * capacity, model_width)


def exchanged(
    tokens,
    cotangent,
    lengths,
    routes,
    w_query,
    w_key,
    w_value,
    w_out,
    w_router,
    g_attn,
    g_ffn,
    g_query,
    g_key,
    w_gate,
    w_up,
    w_down,
):
    micro_count = tokens.shape[0]
    seq_len = tokens.shape[2]
    model_width = tokens.shape[3]
    top_count = routes.shape[3]
    expert_count = w_router.shape[1]
    local_experts = w_gate.shape[0]
    owners = expert_count // local_experts
    capacity = min(seq_len, max(2, 2 * seq_len * top_count // expert_count))
    slot_total = expert_count * capacity
    gate_weight_complete, up_weight_complete, down_weight_complete = (
        lax.all_gather(w_gate, "dp", axis=2, tiled=True),
        lax.all_gather(w_up, "dp", axis=2, tiled=True),
        lax.all_gather(w_down, "dp", axis=1, tiled=True),
    )
    cosine_table, sine_table = rope_tables(seq_len, HDIM)
    places = jnp.arange(seq_len)
    slot_ids = jnp.arange(slot_total)
    expert_ids = jnp.arange(expert_count)
    score_scale = HDIM ** (-0.5)
    grad_query = jnp.zeros((model_width, model_width), jnp.float32)
    grad_key = jnp.zeros((model_width, model_width), jnp.float32)
    grad_value = jnp.zeros((model_width, model_width), jnp.float32)
    grad_out = jnp.zeros((model_width, model_width), jnp.float32)
    grad_router = jnp.zeros((model_width, expert_count), jnp.float32)
    grad_gain_attn = jnp.zeros((model_width,), jnp.float32)
    grad_gain_ffn = jnp.zeros((model_width,), jnp.float32)
    grad_gain_query = jnp.zeros((model_width,), jnp.float32)
    grad_gain_key = jnp.zeros((model_width,), jnp.float32)
    grad_gate = jnp.zeros(gate_weight_complete.shape, jnp.float32)
    grad_up = jnp.zeros(up_weight_complete.shape, jnp.float32)
    grad_down = jnp.zeros(down_weight_complete.shape, jnp.float32)
    outs_mixed = []
    outs_grad = []
    for micro_step in range(micro_count):
        layer_set = (
            lax.all_gather(w_query, "shard", axis=0, tiled=True),
            lax.all_gather(w_key, "shard", axis=0, tiled=True),
            lax.all_gather(w_value, "shard", axis=0, tiled=True),
            lax.all_gather(w_out, "shard", axis=0, tiled=True),
            lax.all_gather(w_router, "shard", axis=0, tiled=True),
            lax.all_gather(g_attn, "shard", axis=0, tiled=True),
            lax.all_gather(g_ffn, "shard", axis=0, tiled=True),
            lax.all_gather(g_query, "shard", axis=0, tiled=True),
            lax.all_gather(g_key, "shard", axis=0, tiled=True),
        )
        query_full, key_full, value_full, out_full, route_full = (
            layer_set[0],
            layer_set[1],
            layer_set[2],
            layer_set[3],
            layer_set[4],
        )
        gain_attn = layer_set[5].astype(jnp.float32)
        gain_ffn = layer_set[6].astype(jnp.float32)
        gain_query = layer_set[7].astype(jnp.float32)
        gain_key = layer_set[8].astype(jnp.float32)
        inputs = tokens[micro_step, 0].astype(jnp.float32)
        length = lengths[micro_step, 0]
        route_ids = routes[micro_step, 0]
        normed = rms_norm(inputs, gain_attn).astype(jnp.bfloat16)
        query_raw = matmul(normed, query_full)
        key_raw = matmul(normed, key_full)
        value_raw = matmul(normed, value_full)
        value_low = value_raw.astype(jnp.bfloat16).reshape(seq_len, HEADS, HDIM)
        query_low = rotate(
            rms_norm(query_raw, gain_query).reshape(seq_len, HEADS, HDIM), cosine_table, sine_table
        ).astype(jnp.bfloat16)
        key_low = rotate(
            rms_norm(key_raw, gain_key).reshape(seq_len, HEADS, HDIM), cosine_table, sine_table
        ).astype(jnp.bfloat16)
        allowed = (places[None, :] <= places[:, None]) & (places[None, :] < length)
        scores = (
            jnp.einsum("qhd,khd->hqk", query_low, key_low, preferred_element_type=jnp.float32)
            * score_scale
        )
        attn_probs = softmax_rows(jnp.where(allowed[None], scores, -1e30))
        probs_low = attn_probs.astype(jnp.bfloat16)
        mixed_low = (
            jnp.einsum("hqk,khd->qhd", probs_low, value_low, preferred_element_type=jnp.float32)
            .reshape(seq_len, model_width)
            .astype(jnp.bfloat16)
        )
        attn_part = matmul(mixed_low, out_full)
        hidden_state = inputs + attn_part
        ffn_in = rms_norm(hidden_state, gain_ffn).astype(jnp.bfloat16)
        logits = matmul(ffn_in, route_full)
        router = softmax_rows(logits)
        chosen = route_ids[:, :, None] == expert_ids[None, None, :]
        gate_vals = jnp.sum(jnp.where(chosen, router[:, None, :], 0.0), axis=2)
        flat_chosen = chosen.reshape(seq_len * top_count, expert_count).astype(jnp.int32)
        before = jnp.cumsum(flat_chosen, axis=0) - flat_chosen
        slot_rank = jnp.sum(before * flat_chosen, axis=1)
        target = route_ids.reshape(-1) * capacity + slot_rank
        placing = (slot_ids[:, None] == target[None, :]).astype(jnp.bfloat16)
        token_placing = jnp.sum(placing.reshape(slot_total, seq_len, top_count), axis=2)
        outgoing = matmul(token_placing, ffn_in).astype(jnp.bfloat16)
        arrived = dispatch_rows(outgoing.reshape(owners, local_experts * capacity, model_width))
        expert_token_rows = to_experts(arrived, local_experts, capacity)
        gate_pre = jnp.einsum(
            "qjs,qsy->qjy",
            expert_token_rows,
            gate_weight_complete,
            preferred_element_type=jnp.float32,
        )
        up_value = jnp.einsum(
            "qjs,qsy->qjy",
            expert_token_rows,
            up_weight_complete,
            preferred_element_type=jnp.float32,
        )
        sigmoid_gate = jax.nn.sigmoid(gate_pre)
        activated = gate_pre * sigmoid_gate
        inner_activation = (activated * up_value).astype(jnp.bfloat16)
        expert_out = jnp.einsum(
            "aqc,aco->aqo",
            inner_activation,
            down_weight_complete,
            preferred_element_type=jnp.float32,
        ).astype(jnp.bfloat16)
        returned = collect_rows(from_experts(expert_out, owners, capacity)).reshape(
            slot_total, model_width
        )
        picked = (
            jnp.take(returned, target, axis=0)
            .astype(jnp.float32)
            .reshape(seq_len, top_count, model_width)
        )
        expert_sum = jnp.sum(picked * gate_vals[:, :, None], axis=1)
        outs_mixed.append((hidden_state + expert_sum).astype(jnp.bfloat16))
        live_mask = (places < length).astype(jnp.float32)
        d_output = cotangent[micro_step, 0].astype(jnp.float32) * live_mask[:, None]
        d_gates = jnp.sum(picked * d_output[:, None, :], axis=2)
        d_slots = (
            (gate_vals[:, :, None] * d_output[:, None, :])
            .astype(jnp.bfloat16)
            .reshape(seq_len * top_count, model_width)
        )
        d_outgoing = matmul(placing, d_slots).astype(jnp.bfloat16)
        d_arrived = dispatch_grads(
            d_outgoing.reshape(owners, local_experts * capacity, model_width)
        )
        expert_output_gradient = to_experts(d_arrived, local_experts, capacity)
        d_inner = jnp.einsum(
            "azy,ajy->azj",
            expert_output_gradient,
            down_weight_complete,
            preferred_element_type=jnp.float32,
        )
        grad_down = grad_down + jnp.einsum(
            "qti,qtj->qij",
            inner_activation,
            expert_output_gradient,
            preferred_element_type=jnp.float32,
        )
        gate_preactivation_gradient = (
            d_inner * up_value * (sigmoid_gate + gate_pre * sigmoid_gate * (1.0 - sigmoid_gate))
        ).astype(jnp.bfloat16)
        up_projection_value_gradient = (d_inner * activated).astype(jnp.bfloat16)
        grad_gate = grad_gate + jnp.einsum(
            "hzo,hzg->hog",
            expert_token_rows,
            gate_preactivation_gradient,
            preferred_element_type=jnp.float32,
        )
        grad_up = grad_up + jnp.einsum(
            "hzo,hzg->hog",
            expert_token_rows,
            up_projection_value_gradient,
            preferred_element_type=jnp.float32,
        )
        d_rows = jnp.einsum(
            "ing,itg->int",
            gate_preactivation_gradient,
            gate_weight_complete,
            preferred_element_type=jnp.float32,
        )
        d_rows = (
            d_rows
            + jnp.einsum(
                "ing,itg->int",
                up_projection_value_gradient,
                up_weight_complete,
                preferred_element_type=jnp.float32,
            )
        ).astype(jnp.bfloat16)
        d_returned = collect_grads(from_experts(d_rows, owners, capacity)).reshape(
            slot_total, model_width
        )
        d_ffn_in = jnp.sum(
            jnp.take(d_returned, target, axis=0)
            .astype(jnp.float32)
            .reshape(seq_len, top_count, model_width),
            axis=1,
        )
        d_router = jnp.sum(jnp.where(chosen, d_gates[:, :, None], 0.0), axis=1)
        d_logits = (router * (d_router - jnp.sum(router * d_router, axis=1, keepdims=True))).astype(
            jnp.bfloat16
        )
        grad_router = grad_router + transposed_times(ffn_in, d_logits)
        d_ffn_in = d_ffn_in + times_transposed(d_logits, route_full)
        d_hidden_norm, d_gain_ffn = norm_back(hidden_state, gain_ffn, d_ffn_in)
        grad_gain_ffn = grad_gain_ffn + d_gain_ffn
        d_hidden = d_output + d_hidden_norm
        d_attn_low = d_hidden.astype(jnp.bfloat16)
        grad_out = grad_out + transposed_times(mixed_low, d_attn_low)
        d_mixed_wide = times_transposed(d_attn_low, out_full)
        d_mixed = d_mixed_wide.astype(jnp.bfloat16).reshape(seq_len, HEADS, HDIM)
        d_probs = jnp.einsum("qhd,khd->hqk", d_mixed, value_low, preferred_element_type=jnp.float32)
        d_value = (
            jnp.einsum("hqk,qhd->khd", probs_low, d_mixed, preferred_element_type=jnp.float32)
            .reshape(seq_len, model_width)
            .astype(jnp.bfloat16)
        )
        d_scores = (
            attn_probs * (d_probs - jnp.sum(attn_probs * d_probs, axis=-1, keepdims=True))
        ).astype(jnp.bfloat16)
        d_query = (
            jnp.einsum("hqk,khd->qhd", d_scores, key_low, preferred_element_type=jnp.float32)
            * score_scale
        )
        d_key = (
            jnp.einsum("hqk,qhd->khd", d_scores, query_low, preferred_element_type=jnp.float32)
            * score_scale
        )
        d_query_raw, d_gain_query = norm_back(
            query_raw,
            gain_query,
            rotate_back(d_query, cosine_table, sine_table).reshape(seq_len, model_width),
        )
        d_key_raw, d_gain_key = norm_back(
            key_raw,
            gain_key,
            rotate_back(d_key, cosine_table, sine_table).reshape(seq_len, model_width),
        )
        grad_gain_query = grad_gain_query + d_gain_query
        grad_gain_key = grad_gain_key + d_gain_key
        d_query_low = d_query_raw.astype(jnp.bfloat16)
        d_key_low = d_key_raw.astype(jnp.bfloat16)
        grad_query = grad_query + transposed_times(normed, d_query_low)
        grad_key = grad_key + transposed_times(normed, d_key_low)
        grad_value = grad_value + transposed_times(normed, d_value)
        d_normed = (
            times_transposed(d_query_low, query_full)
            + times_transposed(d_key_low, key_full)
            + times_transposed(d_value, value_full)
        )
        d_input_norm, d_gain_attn = norm_back(inputs, gain_attn, d_normed)
        grad_gain_attn = grad_gain_attn + d_gain_attn
        outs_grad.append(d_hidden + d_input_norm)
    layer_sums = (
        lax.psum_scatter(
            grad_query.astype(jnp.bfloat16), "shard", scatter_dimension=0, tiled=True
        ).astype(jnp.float32),
        lax.psum_scatter(
            grad_key.astype(jnp.bfloat16), "shard", scatter_dimension=0, tiled=True
        ).astype(jnp.float32),
        lax.psum_scatter(
            grad_value.astype(jnp.bfloat16), "shard", scatter_dimension=0, tiled=True
        ).astype(jnp.float32),
        lax.psum_scatter(
            grad_out.astype(jnp.bfloat16), "shard", scatter_dimension=0, tiled=True
        ).astype(jnp.float32),
        lax.psum_scatter(
            grad_router.astype(jnp.bfloat16), "shard", scatter_dimension=0, tiled=True
        ).astype(jnp.float32),
        lax.psum_scatter(
            grad_gain_attn.astype(jnp.bfloat16), "shard", scatter_dimension=0, tiled=True
        ).astype(jnp.float32),
        lax.psum_scatter(
            grad_gain_ffn.astype(jnp.bfloat16), "shard", scatter_dimension=0, tiled=True
        ).astype(jnp.float32),
        lax.psum_scatter(
            grad_gain_query.astype(jnp.bfloat16), "shard", scatter_dimension=0, tiled=True
        ).astype(jnp.float32),
        lax.psum_scatter(
            grad_gain_key.astype(jnp.bfloat16), "shard", scatter_dimension=0, tiled=True
        ).astype(jnp.float32),
    )
    layer_totals = (
        lax.psum(layer_sums[0].astype(jnp.bfloat16), ("dp", "expert")).astype(jnp.float32),
        lax.psum(layer_sums[1].astype(jnp.bfloat16), ("dp", "expert")).astype(jnp.float32),
        lax.psum(layer_sums[2].astype(jnp.bfloat16), ("dp", "expert")).astype(jnp.float32),
        lax.psum(layer_sums[3].astype(jnp.bfloat16), ("dp", "expert")).astype(jnp.float32),
        lax.psum(layer_sums[4].astype(jnp.bfloat16), ("dp", "expert")).astype(jnp.float32),
        lax.psum(layer_sums[5].astype(jnp.bfloat16), ("dp", "expert")).astype(jnp.float32),
        lax.psum(layer_sums[6].astype(jnp.bfloat16), ("dp", "expert")).astype(jnp.float32),
        lax.psum(layer_sums[7].astype(jnp.bfloat16), ("dp", "expert")).astype(jnp.float32),
        lax.psum(layer_sums[8].astype(jnp.bfloat16), ("dp", "expert")).astype(jnp.float32),
    )
    expert_totals = (
        lax.psum_scatter(
            grad_gate.astype(jnp.bfloat16), "dp", scatter_dimension=2, tiled=True
        ).astype(jnp.float32),
        lax.psum_scatter(
            grad_up.astype(jnp.bfloat16), "dp", scatter_dimension=2, tiled=True
        ).astype(jnp.float32),
        lax.psum_scatter(
            grad_down.astype(jnp.bfloat16), "dp", scatter_dimension=1, tiled=True
        ).astype(jnp.float32),
    )
    mixed_out = jnp.stack(outs_mixed)[:, None]
    grad_tokens = jnp.stack(outs_grad)[:, None]
    return (
        mixed_out,
        grad_tokens,
        layer_totals[0],
        layer_totals[1],
        layer_totals[2],
        layer_totals[3],
        layer_totals[4],
        layer_totals[5],
        layer_totals[6],
        layer_totals[7],
        layer_totals[8],
        expert_totals[0],
        expert_totals[1],
        expert_totals[2],
    )


def solution(mesh):
    placed = (
        P(None, ("dp", "expert", "shard"), None, None),
        P(None, ("dp", "expert", "shard"), None, None),
        P(None, ("dp", "expert", "shard")),
        P(None, ("dp", "expert", "shard"), None, None),
        P("shard", None),
        P("shard", None),
        P("shard", None),
        P("shard", None),
        P("shard", None),
        P("shard"),
        P("shard"),
        P("shard"),
        P("shard"),
        P(("expert", "shard"), None, "dp"),
        P(("expert", "shard"), None, "dp"),
        P(("expert", "shard"), "dp", None),
    )
    sizes = (mesh.shape["dp"], mesh.shape["expert"], mesh.shape["shard"])
    return jax.shard_map(
        gathered if sizes == (2, 4, 4) else exchanged,
        mesh=mesh,
        in_specs=placed,
        out_specs=(
            P(None, ("dp", "expert", "shard"), None, None),
            P(None, ("dp", "expert", "shard"), None, None),
            P("shard", None),
            P("shard", None),
            P("shard", None),
            P("shard", None),
            P("shard", None),
            P("shard"),
            P("shard"),
            P("shard"),
            P("shard"),
            P(("expert", "shard"), None, "dp"),
            P(("expert", "shard"), None, "dp"),
            P(("expert", "shard"), "dp", None),
        ),
        check_vma=False,
    )
```

```python
import functools

import jax
import jax.numpy as jnp
import numpy as np
from jax import lax
from jax.experimental import pallas as pl
from jax.experimental.pallas import tpu as pltpu
from jax.sharding import PartitionSpec as P

HEADS = 16
HDIM = 128


EPSILON = 1e-05


def matmul(left, right):
    return jnp.dot(left, right, preferred_element_type=jnp.float32)


def times_transposed(left, right):
    return lax.dot_general(
        left, right, (((1,), (1,)), ((), ())), preferred_element_type=jnp.float32
    )


def transposed_times(left, right):
    return lax.dot_general(
        left, right, (((0,), (0,)), ((), ())), preferred_element_type=jnp.float32
    )


def rms_norm(values, gain_vec):
    factor = lax.rsqrt(jnp.mean(values * values, axis=-1, keepdims=True) + EPSILON)
    return values * factor * gain_vec


def norm_back(values, gain_vec, incoming):
    factor = lax.rsqrt(jnp.mean(values * values, axis=-1, keepdims=True) + EPSILON)
    unit_rows = values * factor
    weighted = incoming * gain_vec
    d_values = factor * (
        weighted - unit_rows * jnp.mean(weighted * unit_rows, axis=-1, keepdims=True)
    )
    return (d_values, jnp.sum(incoming * unit_rows, axis=0))


def rope_tables(seq_count, head_size):
    half_dim = head_size // 2
    freqs = 10000.0 ** (-2.0 * jnp.arange(half_dim).astype(jnp.float32) / head_size)
    angles = jnp.arange(seq_count).astype(jnp.float32)[:, None] * freqs[None, :]
    cosine_table = jnp.concatenate([jnp.cos(angles), jnp.cos(angles)], axis=-1)
    sine_table = jnp.concatenate([jnp.sin(angles), jnp.sin(angles)], axis=-1)
    return (cosine_table, sine_table)


def rotate(head_rows, cosine_table, sine_table):
    half_dim = head_rows.shape[-1] // 2
    turned = jnp.concatenate([-head_rows[..., half_dim:], head_rows[..., :half_dim]], axis=-1)
    return head_rows * cosine_table[:, None, :] + turned * sine_table[:, None, :]


def rotate_back(incoming, cosine_table, sine_table):
    half_dim = incoming.shape[-1] // 2
    moved_part = incoming * sine_table[:, None, :]
    turned = jnp.concatenate([moved_part[..., half_dim:], -moved_part[..., :half_dim]], axis=-1)
    return incoming * cosine_table[:, None, :] + turned


def softmax_rows(scores):
    shifted = jnp.exp(scores - jnp.max(scores, axis=-1, keepdims=True))
    return shifted / jnp.sum(shifted, axis=-1, keepdims=True)


MESH_ID = pl.DeviceIdType.MESH
EXTRA = 128
ANY = pl.BlockSpec(memory_space=pl.ANY)


def place():
    return lax.axis_index("dp"), lax.axis_index("expert"), lax.axis_index("shard")


def x_of(e):
    return e + 1 - 2 * lax.rem(e, 2)


def y_of(e):
    return lax.rem(e + 2, 4)


def greet(peers):
    barrier = pltpu.get_barrier_semaphore()
    for peer in peers:
        pl.semaphore_signal(barrier, inc=1, device_id=peer, device_id_type=MESH_ID)
    pl.semaphore_wait(barrier, len(peers))


class Copies:
    def __init__(self):
        self.started = []

    def send(self, src, dst, send_sem, recv_sem, device, when=None):
        copy = pltpu.make_async_remote_copy(
            src_ref=src,
            dst_ref=dst,
            send_sem=send_sem,
            recv_sem=recv_sem,
            device_id=device,
            device_id_type=MESH_ID,
        )
        if when is None:
            copy.start()
        else:
            pl.when(when)(copy.start)
        self.started.append((copy, when))

    def drain(self):
        for copy, when in self.started:
            if when is None:
                copy.wait_send()
            else:
                pl.when(when)(copy.wait_send)


def arrived(ref, sem, other):
    pltpu.make_async_remote_copy(
        src_ref=ref,
        dst_ref=ref,
        send_sem=sem,
        recv_sem=sem,
        device_id=other,
        device_id_type=MESH_ID,
    ).wait_recv()


class SemPool:
    def __init__(self, ref):
        self.ref = ref
        self.used = 0

    def take(self):
        self.used += 1
        assert self.used <= self.ref.shape[0]
        return self.ref.at[self.used - 1]


class Item:
    def __init__(self, own, dst, recv, skip=False, cross=None, cross_recv=None):
        self.own, self.dst, self.recv = own, dst, recv
        self.skip, self.cross, self.cross_recv = skip, cross, cross_recv


class Gather:
    def __init__(self, item, copies, pool):
        self.item, self.copies, self.pool = item, copies, pool
        self.dp, self.e, self.z = place()
        self.px, self.py = x_of(self.e), y_of(self.e)
        self.diag = x_of(self.py)
        self.firsts, self.seconds = (self.px, self.py), (self.py, self.px)

    def send(self, h, ee, zz, target, zt, when, own=False):
        item = self.item
        ref = item.dst(zz, ee, h)
        self.copies.send(item.own(h) if own else ref, ref, self.pool.take(), item.recv.at[h, ee * 4 + zz],
                         (self.dp, target, zt), when)

    def across(self, h, ee, zz, when):
        item = self.item
        if item.cross is not None:
            ref = item.dst(zz, ee, h)
            self.copies.send(ref, ref, self.pool.take(), item.cross_recv.at[h, ee * 4 + zz],
                             (1 - self.dp, self.e, self.z), when)

    def wait(self, h, ee, zz, when):
        def body():
            arrived(self.item.dst(zz, ee, h), self.item.recv.at[h, ee * 4 + zz], (self.dp, self.e, self.z))
        if when is None:
            body()
        else:
            pl.when(when)(body)

    def steps(self, k):
        if k == 0:
            return [(self.z, None, 1)]
        out = []
        for sign in (-1, 1):
            zz = self.z + sign * k
            out.append((zz, (zz >= 0) & (zz <= 3), sign))
        return out

    def begin_z(self):
        for h in (0, 1):
            for sign in (-1, 1):
                nxt = self.z + sign
                self.send(h, self.e, self.z, self.e, nxt, (nxt >= 0) & (nxt <= 3), own=True)

    def begin_plane(self):
        for h in (0, 1):
            for target in (self.firsts[h], self.seconds[h]):
                self.send(h, self.e, self.z, target, self.z, None, own=True)

    def own_stage(self, k):
        for zz, valid, sign in self.steps(k):
            nxt = self.z - sign
            for h in (0, 1):
                self.wait(h, self.e, zz, valid)
                self.send(h, self.e, zz, self.e, nxt, valid & (nxt >= 0) & (nxt <= 3))
                self.send(h, self.e, zz, self.firsts[h], self.z, valid)
                self.send(h, self.e, zz, self.seconds[h], self.z, valid)
                self.across(h, self.e, zz, valid)

    def relay_stage(self, k):
        if k == 0 and self.item.skip:
            return
        for zz, valid, _ in self.steps(k):
            for h in (0, 1):
                self.wait(h, self.firsts[h], zz, valid)
                self.send(h, self.firsts[h], zz, self.seconds[h], self.z, valid)
                self.across(h, self.firsts[h], zz, valid)

    def last_stage(self, k):
        if k == 0 and self.item.skip:
            return
        for zz, valid, _ in self.steps(k):
            for h in (0, 1):
                for ee in (self.seconds[h], self.diag):
                    self.wait(h, ee, zz, valid)
                    self.across(h, ee, zz, valid)

    def cross_stage(self):
        if self.item.cross is None:
            return
        for k in (1, 2, 3):
            for zz, valid, _ in self.steps(k):
                @pl.when(valid)
                def _(zz=zz):
                    for ee in range(4):
                        for h in (0, 1):
                            arrived(self.item.cross(zz, ee, h), self.item.cross_recv.at[h, ee * 4 + zz],
                                    (self.dp, self.e, self.z))

    def both_ways(self, h, ee, own=False):
        for sign in (-1, 1):
            nxt = self.z + sign
            self.send(h, ee, self.z, self.e, nxt, (nxt >= 0) & (nxt <= 3), own=own)

    def plane_relay(self):
        for h in (0, 1):
            self.wait(h, self.firsts[h], self.z, None)
            self.send(h, self.firsts[h], self.z, self.seconds[h], self.z, None)

    def line_begin(self, group):
        for h in (0, 1):
            if group == 0:
                self.both_ways(h, self.e, own=True)
                self.both_ways(h, self.firsts[h])
            else:
                for ee in (self.seconds[h], self.diag):
                    self.wait(h, ee, self.z, None)
                    self.both_ways(h, ee)

    def line_stage(self, k, group):
        for zz, valid, sign in self.steps(k):
            nxt = self.z - sign
            for h in (0, 1):
                for ee in ((self.e, self.firsts[h]), (self.seconds[h], self.diag))[group]:
                    self.wait(h, ee, zz, valid)
                    self.send(h, ee, zz, self.e, nxt, valid & (nxt >= 0) & (nxt <= 3))


class Plane:
    def __init__(self, own, all_rows, recv, send, relay, cross):
        self.own, self.all_rows, self.recv = own, all_rows, recv
        self.send, self.relay, self.cross = send, relay, cross
        self.dp, self.e, self.z = place()
        px, py = x_of(self.e), y_of(self.e)
        self.plane = (px, py, x_of(py))
        self.half = all_rows.shape[1] // 2

    def at(self, ref, h):
        return ref.at[pl.ds(h * self.half, self.half)]

    def copy(self, src, slot, h, send_sem, device):
        return pltpu.make_async_remote_copy(
            src_ref=src, dst_ref=self.at(self.all_rows.at[slot], h), send_sem=send_sem,
            recv_sem=self.recv.at[h, slot], device_id=device, device_id_type=MESH_ID)

    def first(self, n, h):
        target = (1 - self.dp, self.e, self.z) if n == 2 else (self.dp, self.plane[n], self.z)
        return self.copy(self.at(self.own, h), self.dp * 4 + self.e, h, self.send.at[n, h], target)

    def on(self, h):
        slot = self.dp * 4 + self.plane[h]
        return self.copy(self.at(self.all_rows.at[slot], h), slot, h, self.relay.at[h],
                         (self.dp, self.plane[1 - h], self.z))

    def over(self, n, h):
        slot = self.dp * 4 + self.plane[n]
        return self.copy(self.at(self.all_rows.at[slot], h), slot, h, self.cross.at[n, h],
                         (1 - self.dp, self.e, self.z))

    def wait(self, h, slot):
        arrived(self.at(self.all_rows.at[slot], h), self.recv.at[h, slot], (self.dp, self.e, self.z))

    def begin(self):
        for n in range(3):
            for h in (0, 1):
                self.first(n, h).start()

    def pass_on(self):
        for h in (0, 1):
            self.wait(h, self.dp * 4 + self.plane[h])
            self.on(h).start()
            self.over(h, h).start()

    def end(self):
        for h in (0, 1):
            self.wait(h, self.dp * 4 + self.plane[1 - h])
            self.over(1 - h, h).start()
        for h in (0, 1):
            self.wait(h, self.dp * 4 + self.plane[2])
            self.over(2, h).start()

    def end_cross(self):
        for ee in range(4):
            for h in (0, 1):
                self.wait(h, (1 - self.dp) * 4 + ee)

    def drain(self):
        for h in (0, 1):
            for n in range(3):
                self.first(n, h).wait_send()
                self.over(n, h).wait_send()
            self.on(h).wait_send()


def mates_of():
    dp, e, z = place()
    return [(lax.rem(dp + d // 4, 2), lax.rem(e + d % 4, 4), z) for d in range(1, 8)]


def columns_of(d, ee):
    return pl.ds(pl.multiple_of(ee * 512 + d * 256, 256), 256)


def as_column(row, count):
    return jnp.broadcast_to(row, (count, row.shape[1])).T


def as_row(column):
    return jnp.broadcast_to(column, (column.shape[0], 128)).T[0:1]


def chosen_experts(route_ids):
    lane = lax.broadcasted_iota(jnp.int32, (route_ids.shape[0], EXTRA), 1)
    found = route_ids[:, 0:1] == lane
    for r in range(1, route_ids.shape[1]):
        found = found | (route_ids[:, r:r + 1] == lane)
    return found


def allowed_keys(live_row):
    rows = live_row.shape[1]
    i = lax.broadcasted_iota(jnp.int32, (rows, rows), 0)
    j = lax.broadcasted_iota(jnp.int32, (rows, rows), 1)
    half = rows // 2
    return ((i < half) == (j < half)) & (j <= i) & (live_row > 0.5)


def front_kernel(
    tok, cot, live, route_ids, cosine, sine, route_in, gains_in, wq, wk, wv, wo, wg, wu, wd,
    q_raw, k_raw, q_low, k_low, v_low, squares, lives, mixed, hidden, ffn_in, router, small_rows, dy,
    rows_all, w_cols, w_out, wide_all, dy_all, wg_far, wu_far, wd_far,
    X, Wc, Wo, R, small, normed, mixed_cols, mixed_own, parts, sent, load_sem, store_sem, x_recv, x_send, x_relay, x_cross,
    recv_w, recv_o, cross_o, recv_a, recv_b, recv_r, recv_small, recv_far, recv_live, recv_sq, recv_mix,
    mate_send, send_sems,
):
    dp, e, z = place()
    px, py = x_of(e), y_of(e)
    me, far = (dp, e, z), (1 - dp, e, z)
    f32, bf = jnp.float32, jnp.bfloat16
    rows, width = tok.shape
    quarter = width // 4
    slot_z = e * 4 + z
    slot_me = dp * 4 + e
    mates = mates_of()
    own_cols = columns_of(dp, e)

    def local(src, dst, sem):
        return pltpu.make_async_copy(src, dst, sem)

    z_rows = pl.ds(pl.multiple_of(z * 512, 512), 512)
    loads = [local(ref.at[:, own_cols], Wc.at[m, z_rows], load_sem.at[m]) for m, ref in enumerate((wq, wk, wv))]
    loads.append(local(wo, Wo.at[z_rows], load_sem.at[3]))
    for load in loads:
        load.start()
    unit = (lax.broadcasted_iota(jnp.int32, (16, 16), 0) == lax.broadcasted_iota(jnp.int32, (16, 16), 1)).astype(bf)
    small[0:16] = times_transposed(unit, route_in[...]).astype(bf)
    small[16:] = gains_in[...]
    dy_live = jnp.where(as_column(live[0:1], rows)[:, :1] > 0.5, cot[...].astype(f32), 0.0)
    dy[...] = dy_live.astype(bf).reshape(dy.shape)
    greet([(dp, e, lax.rem(z + d, 4)) for d in (1, 2, 3)] + mates)
    copies, pool = Copies(), SemPool(send_sems)

    def to_mates(src, dst, recv_at, kind):
        for n, mate in enumerate(mates):
            copies.send(src(mate), dst, mate_send.at[kind, n], recv_at, mate)

    def cols_piece(zz, h):
        return Wc.at[:, pl.ds(pl.multiple_of(zz * 512 + h * 256, 256), 256), :]

    def cols_send(zz, h, sign, when):
        nxt = z + sign
        on = (nxt >= 0) & (nxt <= 3)
        copies.send(cols_piece(zz, h), cols_piece(zz, h), pool.take(), recv_w.at[h, zz], (dp, e, nxt),
                    on if when is None else on & when)

    def cols_stage(k):
        for sign in (-1, 1):
            zz = z + sign * k
            valid = (zz >= 0) & (zz <= 3)
            for h in (0, 1):
                @pl.when(valid)
                def _(zz=zz, h=h):
                    arrived(cols_piece(zz, h), recv_w.at[h, zz], me)
                cols_send(zz, h, -sign, valid)

    def out_piece(d):
        def at(zz, ee, h):
            return Wo.at[pl.ds(pl.multiple_of(zz * 512 + ee * 128 + d * 64 + h * 32, 32), 32), :]
        return at

    out_at = out_piece(dp)
    cuts = (32, 32)
    out_g = Gather(Item(lambda h: out_at(z, e, h), out_at, recv_o, skip=True, cross=out_piece(1 - dp),
                        cross_recv=cross_o), copies, pool)
    dy_a = Gather(Item(lambda h: dy.at[h, 0:cuts[h]], lambda zz, ee, h: dy_all.at[ee * 4 + zz, h, 0:cuts[h]], recv_a),
                  copies, pool)
    dy_b = Gather(Item(lambda h: dy.at[h, cuts[h]:64], lambda zz, ee, h: dy_all.at[ee * 4 + zz, h, cuts[h]:64], recv_b),
                  copies, pool)
    b_all = Gather(Item(lambda h: wide_all.at[slot_z, h], lambda zz, ee, h: wide_all.at[ee * 4 + zz, h], recv_r),
                   copies, pool)
    x_plane = Plane(normed, X, x_recv, x_send, x_relay, x_cross)

    for d in (1, 2, 3):
        copies.send(small, small_rows.at[z], pool.take(), recv_small.at[z], (dp, e, lax.rem(z + d, 4)))
    to_mates(lambda mate: live, lives.at[slot_me], recv_live.at[slot_me], 0)
    small_store = local(small, small_rows.at[z], store_sem.at[0])
    small_store.start()
    dy_store = local(dy, dy_all.at[slot_z], store_sem.at[1])
    dy_store.start()
    for load in loads:
        load.wait()
    for h in (0, 1):
        for sign in (-1, 1):
            cols_send(z, h, sign, None)
    small_store.wait()
    for d in (1, 2, 3):
        zz = lax.rem(z + d, 4)
        arrived(small_rows.at[zz], recv_small.at[zz], me)
    for zz in range(4):
        R[:, zz * quarter:(zz + 1) * quarter] = small_rows[zz]

    def gain(i):
        return R[16 + i:17 + i, :].astype(f32)

    def factor(values):
        return lax.rsqrt(jnp.mean(values * values, axis=1, keepdims=True) + EPSILON)

    x = tok[...].astype(f32)
    normed[...] = (x * factor(x) * gain(0)).astype(bf)
    x_plane.begin()
    x_keep = local(normed, X.at[slot_me], store_sem.at[2])
    x_keep.start()
    lives[slot_me] = live[...]
    dy_a.begin_plane()
    dy_b.begin_plane()
    cols_stage(1)
    out_g.begin_z()
    x_plane.pass_on()
    for i, (src, dst) in enumerate(((wg, wg_far), (wu, wu_far), (wd, wd_far))):
        copies.send(src, dst, pool.take(), recv_far.at[i], far)
    dy_a.relay_stage(0)
    dy_b.plane_relay()
    cols_stage(2)
    x_plane.end()
    out_g.own_stage(1)
    dy_a.begin_z()
    x_plane.end_cross()
    x_keep.wait()
    for n in range(7):
        od, oe, _ = mates[n]
        arrived(lives.at[od * 4 + oe], recv_live.at[od * 4 + oe], me)
    rows_store = local(X, rows_all, store_sem.at[3])
    rows_store.start()
    cols_stage(3)
    cols_store = local(Wc, w_cols, store_sem.at[5])
    cols_store.start()
    out_g.relay_stage(1)

    def project(g, _):
        at = pl.ds(g * 4, 4)
        block = X[at].reshape(4 * rows, width)
        for m, ref in enumerate((q_raw, k_raw)):
            ref[at] = jnp.dot(block, Wc[m], preferred_element_type=f32).reshape(4, rows, 256)
        v_low[at] = jnp.dot(block, Wc[2], preferred_element_type=f32).astype(bf).reshape(4, rows, 256)
        for i in range(4):
            for m, ref in enumerate((q_raw, k_raw)):
                values = ref[g * 4 + i]
                parts[slot_me, m, pl.ds(g * 4 + i, 1), :] = as_row(jnp.sum(values * values, axis=1, keepdims=True))
        return 0

    lax.fori_loop(0, 2, project, 0)
    to_mates(lambda mate: parts.at[slot_me], parts.at[slot_me], recv_sq.at[slot_me], 1)
    out_g.own_stage(2)
    dy_b.line_begin(0)
    for n in range(7):
        od, oe, _ = mates[n]
        arrived(parts.at[od * 4 + oe], recv_sq.at[od * 4 + oe], me)
    squares[...] = (((parts[0] + parts[1]) + (parts[2] + parts[3]))
                    + ((parts[4] + parts[5]) + (parts[6] + parts[7]))) * (1.0 / width)
    cos_t = jnp.concatenate([cosine[...]] * 2, axis=0)
    sin_t = jnp.concatenate([sine[...]] * 2, axis=0)

    def attend(d, _):
        allowed = allowed_keys(lives[d][0:1])
        for m, (raw, low) in enumerate(((q_raw, q_low), (k_raw, k_low))):
            scale = lax.rsqrt(as_column(squares[m, pl.ds(d, 1), :], HDIM) + EPSILON)
            for hh in range(2):
                cc = slice(hh * HDIM, (hh + 1) * HDIM)
                gains = R[18 + m:19 + m, pl.ds(pl.multiple_of(e * 512 + dp * 256 + hh * HDIM, HDIM), HDIM)].astype(f32)
                u = raw[d, :, cc] * scale * gains
                low[d, :, cc] = (u * cos_t + pltpu.roll(u, HDIM // 2, 1) * sin_t).astype(bf)
        for hh in range(2):
            cc = slice(hh * HDIM, (hh + 1) * HDIM)
            scores = times_transposed(q_low[d, :, cc], k_low[d, :, cc]) * (HDIM ** (-0.5))
            probs = softmax_rows(jnp.where(allowed, scores, -1e30))
            mixed_cols[d, :, cc] = jnp.dot(probs.astype(bf), v_low[d, :, cc], preferred_element_type=f32).astype(bf)
        return 0

    lax.fori_loop(0, 4, attend, 0)
    out_g.relay_stage(2)
    out_g.own_stage(3)
    dy_b.line_begin(1)
    lax.fori_loop(4, 8, attend, 0)
    to_mates(lambda mate: mixed_cols.at[mate[0] * 4 + mate[1]], mixed_own.at[:, own_cols], recv_mix.at[slot_me], 2)
    mixed_own[:, own_cols] = mixed_cols[slot_me]
    out_g.last_stage(1)
    out_g.relay_stage(3)
    dy_a.own_stage(1)
    for n in range(7):
        od, oe, _ = mates[n]
        arrived(mixed_own.at[:, columns_of(od, oe)], recv_mix.at[od * 4 + oe], me)
    mixed[...] = mixed_own[...]
    out_g.last_stage(2)
    dy_b.line_stage(1, 0)
    dy_a.relay_stage(1)
    out_g.last_stage(3)
    out_g.cross_stage()
    full_o = local(Wo, w_out, store_sem.at[4])
    full_o.start()

    def out_col(j, _):
        cc = pl.ds(pl.multiple_of(j * 512, 512), 512)
        hidden[:, cc] = tok[:, cc].astype(f32) + jnp.dot(mixed[...], Wo[:, cc], preferred_element_type=f32)
        return 0

    lax.fori_loop(0, 4, out_col, 0)
    h1 = hidden[...]
    b = (h1 * factor(h1) * gain(1)).astype(bf)
    ffn_in[...] = b
    lane = lax.broadcasted_iota(jnp.int32, (rows, EXTRA), 1)
    logits = jnp.where(lane < 16, times_transposed(b, R[...]), -1e30)
    picks = softmax_rows(logits)
    router[...] = picks
    gates = jnp.where(chosen_experts(route_ids[...]), picks, 0.0)
    high = gates.astype(bf).astype(f32)
    extra = high + pltpu.roll(gates - high, 16, 1)
    sent[:, :, :width] = b.reshape(2, rows // 2, width)
    sent[:, :, width:] = extra.astype(bf).reshape(2, rows // 2, EXTRA)
    keep = local(sent, wide_all.at[slot_z], store_sem.at[6])
    keep.start()
    keep.wait()
    b_all.begin_plane()
    b_all.begin_z()
    dy_a.own_stage(2)
    dy_b.line_stage(1, 1)
    dy_a.relay_stage(2)
    b_all.relay_stage(0)
    b_all.own_stage(1)
    dy_a.own_stage(3)
    dy_b.line_stage(2, 0)
    b_all.relay_stage(1)
    b_all.own_stage(2)
    dy_a.relay_stage(3)
    dy_b.line_stage(2, 1)
    b_all.relay_stage(2)
    b_all.own_stage(3)
    b_all.relay_stage(3)
    for group in (0, 1):
        dy_b.line_stage(3, group)
    for k in range(4):
        dy_a.last_stage(k)
    for k in range(4):
        b_all.last_stage(k)
    for i, dst in enumerate((wg_far, wu_far, wd_far)):
        arrived(dst, recv_far.at[i], me)
    copies.drain()
    x_plane.drain()
    for store in (dy_store, full_o, rows_store, cols_store):
        store.wait()


def front(tok, cot, live, route_ids, cosine, sine, route_in, gains_in, *weights):
    bf, f32 = jnp.bfloat16, jnp.float32
    dma = pltpu.SemaphoreType.DMA
    shape = jax.ShapeDtypeStruct
    vmem = pl.BlockSpec(memory_space=pltpu.VMEM)
    rows, width = tok.shape
    wg, wu, wd = weights[4:]
    return pl.pallas_call(
        front_kernel,
        out_shape=(
            shape((8, rows, 256), f32),
            shape((8, rows, 256), f32),
            shape((8, rows, 256), bf),
            shape((8, rows, 256), bf),
            shape((8, rows, 256), bf),
            shape((2, 8, rows), f32),
            shape((8, 8, rows), f32),
            shape((rows, width), bf),
            shape((rows, width), f32),
            shape((rows, width), bf),
            shape((rows, EXTRA), f32),
            shape((4, EXTRA, width // 4), bf),
            shape((2, rows // 2, width), bf),
            shape((8, rows, width), bf),
            shape((3, width, 256), bf),
            shape((width, width), bf),
            shape((16, 2, rows // 2, width + EXTRA), bf),
            shape((16, 2, rows // 2, width), bf),
            shape(wg.shape, bf),
            shape(wu.shape, bf),
            shape(wd.shape, bf),
        ),
        in_specs=[vmem] * 8 + [ANY] * 7,
        out_specs=(vmem,) * 13 + (ANY,) * 8,
        scratch_shapes=[
            pltpu.VMEM((8, rows, width), bf),
            pltpu.VMEM((3, width, 256), bf),
            pltpu.VMEM((width, width), bf),
            pltpu.VMEM((EXTRA, width), bf),
            pltpu.VMEM((EXTRA, width // 4), bf),
            pltpu.VMEM((rows, width), bf),
            pltpu.VMEM((8, rows, 256), bf),
            pltpu.VMEM((rows, width), bf),
            pltpu.VMEM((8, 2, 8, rows), f32),
            pltpu.VMEM((2, rows // 2, width + EXTRA), bf),
            dma((4,)),
            dma((7,)),
            dma((2, 8)),
            dma((3, 2)),
            dma((2,)),
            dma((3, 2)),
            dma((2, 4)),
            dma((2, 16)),
            dma((2, 16)),
            dma((2, 16)),
            dma((2, 16)),
            dma((2, 16)),
            dma((4,)),
            dma((3,)),
            dma((8,)),
            dma((8,)),
            dma((8,)),
            dma((3, 7)),
            dma((330,)),
        ],
        compiler_params=pltpu.CompilerParams(collective_id=0, has_side_effects=True, vmem_limit_bytes=62 * 2**20),
        name="attention_front",
    )(tok, cot, live, route_ids, cosine, sine, route_in, gains_in, *weights)


def times(left, right):
    return jnp.dot(left, right, preferred_element_type=jnp.float32)


def experts_kernel(
    wide, dy, wg, wu, wd, wgf, wuf, wdf,
    res, eg, eu, ed, part, a_buf, b_buf,
    c_buf, WG, WU, WD, rows_in, dy_rows, hidden, saved, acc, stage, addend, turned, column, far_out,
    w_sem, dy_sem, in_sem, part_sem, add_sem, col_sem, fin_sem, out_sem,
    a_sem, b_sem, c_sem, a_send, b_send, c_send, gu_send, gu_sem, dn_send, dn_sem, free_sem,
):
    dp, e, z = place()
    px, py = x_of(e), y_of(e)
    diag = x_of(y_of(e))
    me = (dp, e, z)
    far_core = (1 - dp, e, z)
    f32, bf = jnp.float32, jnp.bfloat16
    width = dy.shape[3]
    half_f = wg.shape[1]
    total_width = part.shape[3]

    def local(src, dst, sem):
        return pltpu.make_async_copy(src, dst, sem)

    def remote(src, dst, send_sem, recv_sem, device):
        return pltpu.make_async_remote_copy(
            src_ref=src, dst_ref=dst, send_sem=send_sem, recv_sem=recv_sem,
            device_id=device, device_id_type=MESH_ID)

    def column_of(c):
        return jnp.where(c == 0, diag, jnp.where(c == 1, py, jnp.where(c == 2, px, e)))

    def zed(i):
        return lax.rem(z + jnp.where(i == 0, 2, jnp.where(i == 1, 1, jnp.where(i == 2, 3, 0))), 4)

    def kind_of(s):
        return jnp.where(s < 2, 0, jnp.where(s < 4, 3, 1 + lax.rem(s, 2)))

    def zed_of(s, i):
        return zed(2 * jnp.where(s < 4, lax.rem(s, 2), (s - 4) // 2) + i)

    def slot_of(s, i):
        return column_of(kind_of(s)) * 4 + zed_of(s, i)

    def rows_load(s, i, buf):
        return local(wide.at[slot_of(s, i)], rows_in.at[buf, i], in_sem.at[buf, i])

    weights = [
        local(src, dst, w_sem.at[n])
        for n, (src, dst) in enumerate((
            (wg, WG.at[0]), (wu, WU.at[0]), (wd, WD.at[0]), (wgf, WG.at[1]), (wuf, WU.at[1]), (wdf, WD.at[1])))
    ]
    for i in range(2):
        rows_load(0, i, 0).start()
    weights[0].start()
    weights[1].start()
    def dy_load(s, i):
        return local(dy.at[slot_of(s, i)], dy_rows.at[slot_of(s, i)], dy_sem.at[s, i])

    for i in range(2):
        dy_load(0, i).start()
    for load in weights[2:]:
        load.start()
    for s in range(1, 8):
        for i in range(2):
            dy_load(s, i).start()
    greet([(dp, e, lax.rem(z + d, 4)) for d in (1, 2, 3)] + [(dp, px, z), (dp, py, z), far_core])

    def part_write(s, i):
        return local(stage.at[lax.rem(s, 2), i], part.at[slot_of(s, i)], part_sem.at[lax.rem(s, 2), i])

    def a_copy(h, g, slot, zz, target):
        return remote(part.at[slot, h], a_buf.at[h, g, zz], a_send.at[h, g, zz], a_sem.at[h, g, zz], (dp, target, z))

    def b_copy(h, slot, zz, target):
        return remote(part.at[slot, h], b_buf.at[h, zz], b_send.at[h, zz], b_sem.at[h, zz], (dp, target, z))

    def send_step(s):
        c = kind_of(s)
        for i in range(2):
            part_write(s, i).wait()
            zz = zed_of(s, i)

            @pl.when(c == 0)
            def _():
                a_copy(0, 0, diag * 4 + zz, zz, py).start()
                a_copy(1, 0, diag * 4 + zz, zz, px).start()

            @pl.when(c == 1)
            def _():
                a_copy(0, 1, py * 4 + zz, zz, py).start()
                b_copy(1, py * 4 + zz, zz, py).start()

            @pl.when(c == 2)
            def _():
                a_copy(1, 1, px * 4 + zz, zz, px).start()
                b_copy(0, px * 4 + zz, zz, px).start()

    def addend_load(s, i):
        h = jnp.where(kind_of(s) == 1, 1, 0)
        zz = zed_of(s, i)
        return local(a_buf.at[h, 0, zz], addend.at[i], add_sem.at[i])

    mine = e * 4 + z
    route_rows = turned
    lane = lax.broadcasted_iota(jnp.int32, (256, EXTRA), 1)
    at_high, at_low = lane == mine, lane == mine + 16

    weights[0].wait()
    weights[1].wait()

    def step(s, _):
        buf = lax.rem(s, 2)

        @pl.when(s + 1 < 8)
        def _():
            for i in range(2):
                rows_load(s + 1, i, 1 - buf).start()
        for i in range(2):
            rows_load(s, i, buf).wait()
            dy_load(s, i).wait()
        slots = [slot_of(s, i) for i in range(2)]
        extra = rows_in[buf, :, :, :, width:].reshape(256, EXTRA).astype(f32)
        gate = jnp.sum(jnp.where(at_high | at_low, extra, 0.0), axis=1, keepdims=True)

        def dy_step():
            return jnp.concatenate([dy_rows[slot].reshape(128, width) for slot in slots], axis=0)

        def put(ref, values, at):
            for i in range(2):
                ref[slots[i], :, pl.ds(pl.multiple_of(at, half_f), half_f)] = values[i * 128:(i + 1) * 128]

        dy_route = (gate * dy_step().astype(f32)).astype(bf)
        route_rows[...] = dy_route
        acc[...] = jnp.zeros_like(acc)

        def half_step(n, _):
            @pl.when((s == 0) & (n == 1))
            def _():
                for load in weights[3:]:
                    load.wait()

            @pl.when((s > 0) & (n == 1))
            def _():
                send_step(s - 1)

            @pl.when((s >= 4) & (n == 1))
            def _():
                for i in range(2):
                    h = jnp.where(kind_of(s) == 1, 1, 0)
                    zz = zed_of(s, i)
                    arrived(a_buf.at[h, 0, zz], a_sem.at[h, 0, zz], me)
                    addend_load(s, i).start()
            x = rows_in[buf, :, :, :, :width].reshape(256, width)
            gate_pre = times(x, WG[n])
            up_value = times(x, WU[n])
            sigmoid_gate = jax.nn.sigmoid(gate_pre)
            activated = gate_pre * sigmoid_gate
            inner = (activated * up_value).astype(bf)
            put(hidden, inner, n * half_f)

            @pl.when((s == 0) & (n == 0))
            def _():
                weights[2].wait()
            d_inner = times_transposed(route_rows[...], WD[n])
            d_gate = (d_inner * up_value * (sigmoid_gate + gate_pre * sigmoid_gate * (1.0 - sigmoid_gate))).astype(bf)
            d_up = (d_inner * activated).astype(bf)
            put(saved, d_gate, 2 * n * half_f)
            put(saved, d_up, (2 * n + 1) * half_f)
            acc[0] += times(inner, WD[n])
            acc[1] += times_transposed(d_gate, WG[n]) + times_transposed(d_up, WU[n])
            return 0

        lax.fori_loop(0, 2, half_step, 0)
        y_low = acc[0].astype(bf).astype(f32)
        d_own = jnp.sum(y_low * dy_step().astype(f32), axis=1, keepdims=True)
        high = d_own.astype(bf).astype(f32)
        tail = jnp.where(at_high, high, jnp.where(at_low, d_own - high, 0.0)).astype(bf)

        def lay(values):
            return values.reshape(2, 2, 64, values.shape[1])

        stage[buf, :, :, :, :width] = lay((gate * y_low).astype(bf))
        stage[buf, :, :, :, width:width + EXTRA] = lay(tail)
        stage[buf, :, :, :, width + EXTRA:] = lay(acc[1].astype(bf))
        for i in range(2):
            dy_rows[slots[i]] = route_rows[i * 128:(i + 1) * 128].reshape(2, 64, width)

        @pl.when(s >= 4)
        def _():
            h = jnp.where(kind_of(s) == 1, 1, 0)
            for i in range(2):
                addend_load(s, i).wait()
                stage[buf, i, h] = (stage[buf, i, h].astype(f32) + addend[i].astype(f32)).astype(bf)
        for i in range(2):
            part_write(s, i).start()
        return 0

    lax.fori_loop(0, 8, step, 0)
    pl.semaphore_signal(free_sem, inc=1, device_id=far_core, device_id_type=MESH_ID)
    send_step(7)

    def finish_loads(k):
        zz = zed(k)
        return (local(part.at[e * 4 + zz], stage.at[0, 0], fin_sem.at[0]),
                local(a_buf.at[:, 1, zz], stage.at[0, 1], fin_sem.at[1]),
                local(b_buf.at[:, zz], stage.at[1, 0], fin_sem.at[2]))

    def begin(k):
        zz = zed(k)
        for h in range(2):
            arrived(a_buf.at[h, 1, zz], a_sem.at[h, 1, zz], me)
            arrived(b_buf.at[h, zz], b_sem.at[h, zz], me)
        for load in finish_loads(k):
            load.start()

    def result_write(k):
        return local(stage.at[1, 1], part.at[e * 4 + zed(k)], fin_sem.at[3])

    def c_copy(k):
        zz = zed(k)
        there = (0, 2, 1)[k]
        return remote(part.at[e * 4 + zz], c_buf.at[there], c_send.at[k], c_sem.at[there], (dp, e, zz))

    def close(k):
        for load in finish_loads(k):
            load.wait()
        for h in range(2):
            total = (stage[0, 0, h].astype(f32) + stage[0, 1, h].astype(f32)) + stage[1, 0, h].astype(f32)
            if k < 3:
                stage[1, 1, h] = total.astype(bf)
            else:
                res[h] = total
        if k < 3:
            result_write(k).start()

    def fire(k):
        result_write(k).wait()
        c_copy(k).start()

    def turn_hidden(n):
        turned[...] = hidden[:, :, pl.ds(pl.multiple_of(n * 256, 256), 256)].reshape(2048, 256).T

    def down_block(dst):
        def col(j, _):
            cc = pl.ds(pl.multiple_of(j * 512, 512), 512)
            dst(cc, times(turned[...], dy_rows[:, :, :, cc].reshape(2048, 512)))
            return 0
        lax.fori_loop(0, 4, col, 0)

    def column_load(n):
        return local(wide.at[:, :, :, pl.ds(pl.multiple_of(n * 256, 256), 256)], column.at[lax.rem(n, 2)],
                     col_sem.at[lax.rem(n, 2)])

    def down_send(n):
        return remote(far_out.at[n], WD.at[1, pl.ds(n * 256, 256)], dn_send.at[n], dn_sem.at[n], far_core)

    column_load(0).start()
    for n in range(2):
        turn_hidden(2 + n)

        def to_far(cc, values, n=n):
            far_out[n, :, cc] = values.astype(bf)
        down_block(to_far)
        if n == 0:
            pl.semaphore_wait(free_sem, 1)
        down_send(n).start()

    def row_block(n):
        return pl.ds(pl.multiple_of(n * 256, 256), 256)

    def gu_copy(n, w):
        buf = lax.rem(n, 2)
        return remote(far_out.at[buf, :, w * 512:(w + 1) * 512], WG.at[w, row_block(n)],
                      gu_send.at[buf, w], gu_sem.at[n, w], far_core)

    def gu_out(n, w):
        buf = lax.rem(n, 2)
        return local(acc.at[buf, :, w * 512:(w + 1) * 512], (eg, eu)[w].at[row_block(n)], out_sem.at[buf, w])

    def settle(n):
        buf = lax.rem(n, 2)
        for w in range(2):
            arrived(WG.at[w, row_block(n)], gu_sem.at[n, w], me)
            acc[buf, :, w * 512:(w + 1) * 512] += WG[w, row_block(n)].astype(f32)
            gu_out(n, w).start()

    def gate_up(n, _):
        buf = lax.rem(n, 2)

        @pl.when(n + 1 < 8)
        def _():
            column_load(n + 1).start()
        column_load(n).wait()
        turned[...] = column[buf].reshape(2048, 256).T

        @pl.when(n < 2)
        def _():
            for k in range(2):
                @pl.when(n == k)
                def _(k=k):
                    down_send(k).wait_send()

        @pl.when(n >= 2)
        def _():
            for w in range(2):
                gu_copy(n - 2, w).wait_send()
                gu_out(n - 2, w).wait()

        def far_col(j, _):
            cc = pl.ds(pl.multiple_of(j * 512, 512), 512)
            src = pl.ds(pl.multiple_of(1024 + j * 512, 512), 512)
            far_out[buf, :, cc] = times(turned[...], saved[:, :, src].reshape(2048, 512)).astype(bf)
            return 0

        def near_col(j, _):
            cc = pl.ds(pl.multiple_of(j * 512, 512), 512)
            acc[buf, :, cc] = times(turned[...], saved[:, :, cc].reshape(2048, 512))
            return 0
        lax.fori_loop(0, 2, far_col, 0)
        for w in range(2):
            gu_copy(n, w).start()
        lax.fori_loop(0, 2, near_col, 0)

        @pl.when(n > 0)
        def _():
            settle(n - 1)
        for at, act in ((2, lambda: begin(0)), (3, lambda: close(0)), (4, lambda: fire(0)),
                        (5, lambda: begin(1)), (6, lambda: close(1)), (7, lambda: fire(1))):
            pl.when(n == at)(act)
        return 0

    lax.fori_loop(0, 8, gate_up, 0)
    settle(7)
    for n in (6, 7):
        for w in range(2):
            gu_copy(n, w).wait_send()
            gu_out(n, w).wait()

    def down_out(n):
        return local(acc.at[n], ed.at[pl.ds(n * 256, 256)], out_sem.at[n, 0])

    for n in range(2):
        turn_hidden(n)

        def keep(cc, values, n=n):
            acc[n, :, cc] = values
        down_block(keep)
        arrived(WD.at[1, pl.ds(n * 256, 256)], dn_sem.at[n], me)
        acc[n] += WD[1, pl.ds(n * 256, 256)].astype(f32)
        down_out(n).start()
    begin(2)
    close(2)
    fire(2)
    begin(3)
    close(3)
    for k in range(3):
        arrived(c_buf.at[k], c_sem.at[k], me)
        for h in range(2):
            res[h] += c_buf[k, h].astype(f32)
    for n in range(2):
        down_out(n).wait()
    for k in range(3):
        c_copy(k).wait_send()

    def drain(zz, _):
        a_copy(0, 0, diag * 4 + zz, zz, py).wait_send()
        a_copy(1, 0, diag * 4 + zz, zz, px).wait_send()
        a_copy(0, 1, py * 4 + zz, zz, py).wait_send()
        b_copy(1, py * 4 + zz, zz, py).wait_send()
        a_copy(1, 1, px * 4 + zz, zz, px).wait_send()
        b_copy(0, px * 4 + zz, zz, px).wait_send()
        return 0
    lax.fori_loop(0, 4, drain, 0)


def experts(wide, dy, near, far):
    dma = pltpu.SemaphoreType.DMA
    bf, f32 = jnp.bfloat16, jnp.float32
    wg, wu, wd = near
    width, half_f = wg.shape
    rows = wide.shape[2]
    total_width = 2 * width + EXTRA
    shape = jax.ShapeDtypeStruct
    every = 16 * 2 * rows
    outs = pl.pallas_call(
        experts_kernel,
        out_shape=(
            shape((2, rows, total_width), f32),
            shape((width, half_f), f32),
            shape((width, half_f), f32),
            shape((half_f, width), f32),
            shape((16, 2, rows, total_width), bf),
            shape((2, 2, 4, rows, total_width), bf),
            shape((2, 4, rows, total_width), bf),
        ),
        in_specs=[ANY] * 8,
        out_specs=(pl.BlockSpec(memory_space=pltpu.VMEM),) + (ANY,) * 6,
        scratch_shapes=[
            pltpu.VMEM((3, 2, rows, total_width), bf),
            pltpu.VMEM((2, width, half_f), bf),
            pltpu.VMEM((2, width, half_f), bf),
            pltpu.VMEM((2, half_f, width), bf),
            pltpu.VMEM((2, 2, 2, rows, width + EXTRA), bf),
            pltpu.VMEM((16, 2, rows, width), bf),
            pltpu.VMEM((16, 2 * rows, 2 * half_f), bf),
            pltpu.VMEM((16, 2 * rows, 4 * half_f), bf),
            pltpu.VMEM((2, 256, width), f32),
            pltpu.VMEM((2, 2, 2, rows, total_width), bf),
            pltpu.VMEM((2, rows, total_width), bf),
            pltpu.VMEM((256, every), bf),
            pltpu.VMEM((2, 16, 2, rows, 256), bf),
            pltpu.VMEM((2, 256, width), bf),
            dma((6,)),
            dma((8, 2)),
            dma((2, 2)),
            dma((2, 2)),
            dma((2,)),
            dma((2,)),
            dma((4,)),
            dma((2, 2)),
            dma((2, 2, 4)),
            dma((2, 4)),
            dma((4,)),
            dma((2, 2, 4)),
            dma((2, 4)),
            dma((3,)),
            dma((2, 2)),
            dma((8, 2)),
            dma((2,)),
            dma((2,)),
            pltpu.SemaphoreType.REGULAR,
        ],
        compiler_params=pltpu.CompilerParams(collective_id=2, has_side_effects=True, vmem_limit_bytes=67043328),
        name="owned_expert",
    )(wide, dy, *near, *far)
    return outs[:4]


def back_kernel(
    sums, tok, route_ids, cosine, sine, dy, mixed, q_raw, k_raw, q_low, k_low, v_low, squares, lives, hidden, ffn_in,
    router, small_rows, rows_all, w_cols, w_out,
    mixed_out, grad_tokens, out, small_out,
    Wo, Wc, R, d_hidden, d_heads, DH, d_mix, g_q, g_k, parts, means, X, D, turned, G, own_sum, hop, send_buf, mine,
    far_rows, home_rows, small, s_z, s_all,
    w_sem, load_sem, x_recv, x_send, x_relay, x_cross, d_sem, d_send, h_sem, h_send, q_sem, q_send,
    hop_sem, hop_send, f_sem, f_send, r_sem, r_send, sz_sem, sz_send, sa_sem, sa_send,
    g_sem, g_send, g_pass, g_far, out_sem,
):
    dp, e, z = place()
    px, py = x_of(e), y_of(e)
    diag = x_of(py)
    plane = (px, py, diag)
    me, far = (dp, e, z), (1 - dp, e, z)
    f32, bf = jnp.float32, jnp.bfloat16
    rows, width = tok.shape
    quarter = width // 4
    slot_me = dp * 4 + e
    zs = [lax.rem(z + d, 4) for d in range(4)]
    mates = mates_of()
    own_cols = columns_of(dp, e)

    def local(src, dst, sem):
        return pltpu.make_async_copy(src, dst, sem)

    def remote(src, dst, send_sem, recv_sem, device):
        return pltpu.make_async_remote_copy(
            src_ref=src, dst_ref=dst, send_sem=send_sem, recv_sem=recv_sem,
            device_id=device, device_id_type=MESH_ID)

    load_out = local(w_out, Wo, w_sem.at[0])
    load_cols = local(w_cols, Wc, w_sem.at[1])
    load_rows = local(rows_all, X.at[0], load_sem.at[0])
    load_mixed = local(mixed, X.at[1, slot_me], load_sem.at[1])
    for load in (load_out, load_mixed, load_cols, load_rows):
        load.start()
    greet([(dp, e, zz) for zz in zs[1:]] + mates)
    m_plane = Plane(mixed, X.at[1], x_recv, x_send, x_relay, x_cross)
    m_plane.begin()

    def d_copy(n):
        od, oe, _ = mates[n]
        return remote(d_mix.at[:, columns_of(od, oe)], D.at[3, slot_me], d_send.at[n], d_sem.at[slot_me], mates[n])

    def h_copy(n):
        od, oe, _ = mates[n]
        return remote(d_heads.at[:, columns_of(od, oe)], DH.at[slot_me], h_send.at[n], h_sem.at[slot_me], mates[n])

    def q_copy(n):
        return remote(parts.at[slot_me], parts.at[slot_me], q_send.at[n], q_sem.at[slot_me], mates[n])

    def from_mates(ref, sem):
        for n in range(7):
            od, oe, _ = mates[n]
            arrived(ref.at[od * 4 + oe], sem.at[od * 4 + oe], me)

    def compute(m, i, buf):
        turned[...] = D[m].reshape(8 * rows, 256).T

        def block(zz, _):
            at = pl.ds(pl.multiple_of(zz * 512, 512), 512)
            G[buf, zz] = jnp.dot(turned[...], X[i, :, :, at].reshape(8 * rows, 512), preferred_element_type=f32)
            return 0
        lax.fori_loop(0, 4, block, 0)
        own_sum[m] = G[buf, z]

    middle = (z == 1) | (z == 2)
    lower = z < 2
    targets = (jnp.where(lower, 3, 0), jnp.where(lower, 2, 1), z + 1 - 2 * lax.rem(z, 2))

    def hop_copy(m, j):
        zt = targets[j]
        up = zt > z
        there = jnp.where(zt == z - 1, 4, zt)
        return remote(send_buf.at[m, j], hop.at[m, there], hop_send.at[m, j], hop_sem.at[m, there],
                      (dp, e, jnp.where(up, z + 1, z - 1)))

    def pass_on(m, buf):
        for j in range(3):
            zt = targets[j]

            @pl.when(middle)
            def _():
                arrived(hop.at[m, zt], hop_sem.at[m, zt], me)
                send_buf[m, j] = (G[buf, zt] + hop[m, zt].astype(f32)).astype(bf)

            @pl.when(jnp.logical_not(middle))
            def _():
                send_buf[m, j] = G[buf, zt].astype(bf)
            hop_copy(m, j).start()

    def out_at(m, d, ee, h):
        return out.at[m, pl.ds(h * 256, 256), columns_of(d, ee)]

    def g_copy(m, n, h):
        return remote(mine.at[m, pl.ds(h * 256, 256)], out_at(m, dp, e, h), g_send.at[m, n, h],
                      g_sem.at[m, h, slot_me], far if n == 2 else (dp, plane[n], z))

    def g_relay(m, h):
        ref = out_at(m, dp, plane[h], h)
        return remote(ref, ref, g_pass.at[m, h], g_sem.at[m, h, dp * 4 + plane[h]], (dp, plane[1 - h], z))

    def g_onward(m, n, h):
        ref = out_at(m, dp, plane[n], h)
        return remote(ref, ref, g_far.at[m, n, h], g_sem.at[m, h, dp * 4 + plane[n]], far)

    def wait_g(m, h, d, ee):
        arrived(out_at(m, d, ee, h), g_sem.at[m, h, d * 4 + ee], me)

    def keep(m):
        return local(mine.at[m], out.at[m, :, own_cols], out_sem.at[m])

    def finish(m):
        @pl.when(z > 0)
        def _():
            arrived(hop.at[m, z], hop_sem.at[m, z], me)
            own_sum[m] += hop[m, z].astype(f32)

        @pl.when(z < 3)
        def _():
            arrived(hop.at[m, 4], hop_sem.at[m, 4], me)
            own_sum[m] += hop[m, 4].astype(f32)
        mine[m] = own_sum[m].T.astype(bf)
        for h in (0, 1):
            for n in range(3):
                g_copy(m, n, h).start()
        keep(m).start()

    def relay_out(m):
        for h in (0, 1):
            wait_g(m, h, dp, plane[h])
            g_relay(m, h).start()
            g_onward(m, h, h).start()

    def end_out(m):
        for h in (0, 1):
            wait_g(m, h, dp, plane[1 - h])
            g_onward(m, 1 - h, h).start()
        for h in (0, 1):
            wait_g(m, h, dp, diag)
            g_onward(m, 2, h).start()

    for zz in range(4):
        R[:, zz * quarter:(zz + 1) * quarter] = small_rows[zz]

    def gain(i):
        return R[16 + i:17 + i, :].astype(f32)

    def norm_grad(values, gain_vec, incoming):
        factor = lax.rsqrt(jnp.mean(values * values, axis=1, keepdims=True) + EPSILON)
        unit = values * factor
        weighted = incoming * gain_vec
        back_values = factor * (weighted - unit * jnp.mean(weighted * unit, axis=1, keepdims=True))
        return back_values, jnp.sum(incoming * unit, axis=0, keepdims=True)

    def put_small(at, count, values):
        for zz in range(4):
            small[zz, at:at + count] = values[:, zz * quarter:(zz + 1) * quarter]

    for zz in range(4):
        small[zz] = jnp.zeros(small.shape[1:], f32)
    mixed_out[...] = (hidden[...] + sums[:, :width]).astype(bf)
    extra = sums[:, width:width + EXTRA]
    d_gates = extra + pltpu.roll(extra, EXTRA - 16, 1)
    picks = router[...]
    d_router = jnp.where(chosen_experts(route_ids[...]), d_gates, 0.0)
    d_logits = (picks * (d_router - jnp.sum(picks * d_router, axis=1, keepdims=True))).astype(bf)
    put_small(0, 16, jnp.dot(d_logits.T, ffn_in[...], preferred_element_type=f32)[:16])
    d_ffn = sums[:, width + EXTRA:] + jnp.dot(d_logits, R[...], preferred_element_type=f32)
    back_values, gain_grad = norm_grad(hidden[...], gain(1), d_ffn)
    put_small(17, 1, gain_grad)
    total = dy[...].astype(f32) + back_values
    d_hidden[...] = total
    d_mix[...] = total.astype(bf)
    load_out.wait()

    def heads_back(j, _):
        at = pl.ds(pl.multiple_of(j * 512, 512), 512)
        d_heads[:, at] = times_transposed(d_mix[...], Wo[at, :]).astype(bf)
        return 0

    lax.fori_loop(0, 4, heads_back, 0)
    for n in range(7):
        h_copy(n).start()
    for n in range(7):
        d_copy(n).start()
    DH[slot_me] = d_heads[:, own_cols]
    D[3, slot_me] = d_mix[:, own_cols]
    m_plane.pass_on()
    from_mates(DH, h_sem)

    cos_t = jnp.concatenate([cosine[...]] * 2, axis=0)
    sin_t = jnp.concatenate([sine[...]] * 2, axis=0)
    scale = HDIM ** (-0.5)

    def heads(d, grads):
        allowed = allowed_keys(lives[d][0:1])
        pieces = []
        for hh in range(2):
            cc = slice(hh * HDIM, (hh + 1) * HDIM)
            q, k, v, dh = q_low[d, :, cc], k_low[d, :, cc], v_low[d, :, cc], DH[d, :, cc]
            probs = softmax_rows(jnp.where(allowed, times_transposed(q, k) * scale, -1e30))
            d_probs = times_transposed(dh, v)
            D[2, d, :, cc] = jnp.dot(probs.astype(bf).T, dh, preferred_element_type=f32).astype(bf)
            d_scores = (probs * (d_probs - jnp.sum(probs * d_probs, axis=1, keepdims=True))).astype(bf)
            for z_in in (jnp.dot(d_scores, k, preferred_element_type=f32) * scale,
                         jnp.dot(d_scores.T, q, preferred_element_type=f32) * scale):
                pieces.append(z_in * cos_t - pltpu.roll(z_in, HDIM // 2, 1) * sin_t)
        outs = []
        for m, (raw, ref) in enumerate(((q_raw, g_q), (k_raw, g_k))):
            incoming = jnp.concatenate([pieces[m], pieces[2 + m]], axis=1)
            ref[d] = incoming
            factor = lax.rsqrt(as_column(squares[m, pl.ds(d, 1), :], 256) + EPSILON)
            unit = raw[d] * factor
            gains = R[18 + m:19 + m, own_cols].astype(f32)
            through = incoming * unit
            parts[slot_me, m, pl.ds(d, 1), :] = as_row(jnp.sum(through * gains, axis=1, keepdims=True))
            outs.append(grads[m] + jnp.sum(through, axis=0, keepdims=True))
        return tuple(outs)

    none = jnp.zeros((1, 256), f32)
    gain_grads = lax.fori_loop(0, 8, heads, (none, none))
    for n in range(7):
        q_copy(n).start()
    for m in range(2):
        small[e, 18 + m:19 + m, pl.ds(pl.multiple_of(dp * 256, 256), 256)] = gain_grads[m]
    m_plane.end()
    from_mates(D.at[3], d_sem)
    m_plane.end_cross()
    load_mixed.wait()
    compute(3, 1, 0)
    pass_on(3, 0)
    load_rows.wait()
    compute(2, 0, 1)
    from_mates(parts, q_sem)
    means[...] = (((parts[0] + parts[1]) + (parts[2] + parts[3]))
                  + ((parts[4] + parts[5]) + (parts[6] + parts[7]))) * (1.0 / width)

    def raw_back(d, _):
        for m, (raw, ref) in enumerate(((q_raw, g_q), (k_raw, g_k))):
            factor = lax.rsqrt(as_column(squares[m, pl.ds(d, 1), :], 256) + EPSILON)
            mean = as_column(means[m, pl.ds(d, 1), :], 256)
            gains = R[18 + m:19 + m, own_cols].astype(f32)
            D[m, d] = (factor * (ref[d] * gains - raw[d] * factor * mean)).astype(bf)
        return 0

    lax.fori_loop(0, 8, raw_back, 0)
    pass_on(2, 1)

    load_cols.wait()

    def part_of(d):
        values = times_transposed(D[0, d], Wc[0]) + times_transposed(D[1, d], Wc[1])
        return values + times_transposed(D[2, d], Wc[2])

    def f_copy(ee):
        return remote(Wo.at[pl.ds(ee * rows, rows)], far_rows.at[ee], f_send.at[ee], f_sem.at[ee], far)

    def r_copy(n):
        return remote(home_rows.at[3 + n], home_rows.at[n], r_send.at[n], r_sem.at[n], (dp, plane[n], z))

    for ee in range(4):
        Wo[ee * rows:(ee + 1) * rows] = part_of((1 - dp) * 4 + ee).astype(bf)
        f_copy(ee).start()
    for n in range(3):
        values = part_of(dp * 4 + plane[n])
        arrived(far_rows.at[plane[n]], f_sem.at[plane[n]], me)
        home_rows[3 + n] = (values + far_rows[plane[n]].astype(f32)).astype(bf)
        r_copy(n).start()
    compute(0, 0, 0)
    pass_on(0, 0)
    values = part_of(slot_me)
    arrived(far_rows.at[e], f_sem.at[e], me)
    grad_tokens[...] = values + far_rows[e].astype(f32)
    finish(3)
    compute(1, 0, 1)
    pass_on(1, 1)
    for n in range(3):
        arrived(home_rows.at[n], r_sem.at[n], me)
    back_values, gain_grad = norm_grad(
        tok[...].astype(f32), gain(0),
        (grad_tokens[...] + home_rows[0].astype(f32)) + (home_rows[1].astype(f32) + home_rows[2].astype(f32)))
    put_small(16, 1, gain_grad)
    grad_tokens[...] = d_hidden[...] + back_values

    def sz_copy(d):
        return remote(small.at[zs[d]], s_z.at[z], sz_send.at[d - 1], sz_sem.at[z], (dp, e, zs[d]))

    def sa_copy(d):
        return remote(s_all.at[slot_me], s_all.at[slot_me], sa_send.at[d - 1], sa_sem.at[slot_me], mates[d - 1])

    for d in (1, 2, 3):
        sz_copy(d).start()
    finish(2)
    relay_out(3)
    for d in (1, 2, 3):
        arrived(s_z.at[zs[d]], sz_sem.at[zs[d]], me)
    s_all[slot_me] = (small[z] + s_z[zs[1]]) + (s_z[zs[2]] + s_z[zs[3]])
    for d in range(1, 8):
        sa_copy(d).start()
    finish(0)
    relay_out(2)
    end_out(3)
    finish(1)
    relay_out(0)
    end_out(2)
    from_mates(s_all, sa_sem)
    small_out[...] = (((s_all[0] + s_all[1]) + (s_all[2] + s_all[3]))
                      + ((s_all[4] + s_all[5]) + (s_all[6] + s_all[7])))
    relay_out(1)
    end_out(0)
    end_out(1)
    for m in range(4):
        for h in (0, 1):
            for ee in range(4):
                wait_g(m, h, 1 - dp, ee)
            for n in range(3):
                g_copy(m, n, h).wait_send()
                g_onward(m, n, h).wait_send()
            g_relay(m, h).wait_send()
        keep(m).wait()
        for j in range(3):
            hop_copy(m, j).wait_send()
    m_plane.drain()
    for n in range(7):
        d_copy(n).wait_send()
        h_copy(n).wait_send()
        q_copy(n).wait_send()
        sa_copy(n + 1).wait_send()
    for ee in range(4):
        f_copy(ee).wait_send()
    for n in range(3):
        r_copy(n).wait_send()
        sz_copy(n + 1).wait_send()


def back(*args):
    dma = pltpu.SemaphoreType.DMA
    bf, f32 = jnp.bfloat16, jnp.float32
    shape = jax.ShapeDtypeStruct
    vmem = pl.BlockSpec(memory_space=pltpu.VMEM)
    rows, width = args[1].shape
    small_shape = (4, 24, width // 4)
    return pl.pallas_call(
        back_kernel,
        out_shape=(
            shape((rows, width), bf),
            shape((rows, width), f32),
            shape((4, width // 4, width), bf),
            shape(small_shape[1:], f32),
        ),
        in_specs=[vmem] * 18 + [ANY] * 3,
        out_specs=(vmem, vmem, ANY, vmem),
        scratch_shapes=[
            pltpu.VMEM((width, width), bf),
            pltpu.VMEM((3, width, 256), bf),
            pltpu.VMEM((EXTRA, width), bf),
            pltpu.VMEM((rows, width), f32),
            pltpu.VMEM((rows, width), bf),
            pltpu.VMEM((8, rows, 256), bf),
            pltpu.VMEM((rows, width), bf),
            pltpu.VMEM((8, rows, 256), f32),
            pltpu.VMEM((8, rows, 256), f32),
            pltpu.VMEM((8, 2, 8, rows), f32),
            pltpu.VMEM((2, 8, rows), f32),
            pltpu.VMEM((2, 8, rows, width), bf),
            pltpu.VMEM((4, 8, rows, 256), bf),
            pltpu.VMEM((256, 8 * rows), bf),
            pltpu.VMEM((2, 4, 256, 512), f32),
            pltpu.VMEM((4, 256, 512), f32),
            pltpu.VMEM((4, 5, 256, 512), bf),
            pltpu.VMEM((4, 3, 256, 512), bf),
            pltpu.VMEM((4, 512, 256), bf),
            pltpu.VMEM((4, rows, width), bf),
            pltpu.VMEM((6, rows, width), bf),
            pltpu.VMEM(small_shape, f32),
            pltpu.VMEM(small_shape, f32),
            pltpu.VMEM((8,) + small_shape[1:], f32),
            dma((2,)),
            dma((2,)),
            dma((2, 8)),
            dma((3, 2)),
            dma((2,)),
            dma((3, 2)),
            dma((8,)),
            dma((7,)),
            dma((8,)),
            dma((7,)),
            dma((8,)),
            dma((7,)),
            dma((4, 5)),
            dma((4, 3)),
            dma((4,)),
            dma((4,)),
            dma((3,)),
            dma((3,)),
            dma((4,)),
            dma((3,)),
            dma((8,)),
            dma((7,)),
            dma((4, 2, 8)),
            dma((4, 3, 2)),
            dma((4, 2)),
            dma((4, 3, 2)),
            dma((4,)),
        ],
        compiler_params=pltpu.CompilerParams(collective_id=3, has_side_effects=True, vmem_limit_bytes=63 * 2**20),
        name="attention_back",
    )(*args)


def gathered(
    tokens,
    cotangent,
    lengths,
    routes,
    w_query,
    w_key,
    w_value,
    w_out,
    w_router,
    g_attn,
    g_ffn,
    g_query,
    g_key,
    w_gate,
    w_up,
    w_down,
):
    micro_count, _, seq_len, model_width = tokens.shape
    expert_count = w_router.shape[1]
    f32, bf = jnp.float32, jnp.bfloat16
    places = jnp.arange(seq_len)
    length = lengths[:, 0]
    live = places[None, :] < length[:, None]
    rows = micro_count * seq_len
    gains = jnp.pad(jnp.stack([g_attn, g_ffn, g_query, g_key]), ((0, EXTRA - expert_count - 4), (0, 0)))
    half = HDIM // 2
    angles = np.arange(seq_len)[:, None] * 10000.0 ** (-2.0 * np.arange(half) / HDIM)[None, :]
    cosine_table = np.concatenate([np.cos(angles)] * 2, axis=1).astype(np.float32)
    turned_sine = np.concatenate([-np.sin(angles), np.sin(angles)], axis=1).astype(np.float32)
    live_rows = jnp.broadcast_to(live.astype(f32).reshape(1, rows), (8, rows))
    route_ids = routes[:, 0].reshape(rows, -1)
    tokens_here = tokens[:, 0].reshape(rows, model_width)
    (query_raw, key_raw, query_low, key_low, value_low, squares, lives, mixed_low, hidden_state, ffn_in, router,
     small_rows, dy, rows_all, w_cols, out_full, spread_rows, dy_all, gate_far, up_far, down_far) = front(
        tokens_here, cotangent[:, 0].reshape(rows, model_width), live_rows, route_ids, cosine_table, turned_sine,
        w_router, gains,
        w_query, w_key, w_value, w_out, w_gate[0], w_up[0], w_down[0])
    expert_sums, *expert_grads = experts(
        spread_rows, dy_all, (w_gate[0], w_up[0], w_down[0]), (gate_far, up_far, down_far))
    mixed_out, grad_tokens, sums, small_sums = back(
        expert_sums.reshape(rows, -1), tokens_here, route_ids, cosine_table, turned_sine,
        dy.reshape(rows, model_width), mixed_low, query_raw, key_raw, query_low, key_low, value_low, squares, lives,
        hidden_state, ffn_in, router, small_rows, rows_all, w_cols, out_full)
    return (
        mixed_out.reshape(micro_count, 1, seq_len, model_width),
        grad_tokens.reshape(micro_count, 1, seq_len, model_width),
        sums[0].astype(f32),
        sums[1].astype(f32),
        sums[2].astype(f32),
        sums[3].astype(f32),
        small_sums[:expert_count].T,
        small_sums[expert_count],
        small_sums[expert_count + 1],
        small_sums[expert_count + 2],
        small_sums[expert_count + 3],
        *(g[None] for g in expert_grads),
    )


def dispatch_rows(buffer):
    return lax.all_to_all(buffer, ("expert", "shard"), split_axis=0, concat_axis=0, tiled=True)


def collect_rows(buffer):
    return lax.all_to_all(buffer, ("expert", "shard"), split_axis=0, concat_axis=0, tiled=True)


def dispatch_grads(buffer):
    return lax.all_to_all(buffer, ("expert", "shard"), split_axis=0, concat_axis=0, tiled=True)


def collect_grads(buffer):
    return lax.all_to_all(buffer, ("expert", "shard"), split_axis=0, concat_axis=0, tiled=True)


def to_experts(arrived, local_experts, capacity):
    sources = arrived.shape[0]
    model_width = arrived.shape[2]
    split_rows = arrived.reshape(sources, local_experts, capacity, model_width)
    return jnp.swapaxes(split_rows, 0, 1).reshape(local_experts, sources * capacity, model_width)


def from_experts(expert_token_rows, owners, capacity):
    local_experts = expert_token_rows.shape[0]
    model_width = expert_token_rows.shape[2]
    split_rows = expert_token_rows.reshape(local_experts, owners, capacity, model_width)
    return jnp.swapaxes(split_rows, 0, 1).reshape(owners, local_experts * capacity, model_width)


def exchanged(
    tokens,
    cotangent,
    lengths,
    routes,
    w_query,
    w_key,
    w_value,
    w_out,
    w_router,
    g_attn,
    g_ffn,
    g_query,
    g_key,
    w_gate,
    w_up,
    w_down,
):
    micro_count = tokens.shape[0]
    seq_len = tokens.shape[2]
    model_width = tokens.shape[3]
    top_count = routes.shape[3]
    expert_count = w_router.shape[1]
    local_experts = w_gate.shape[0]
    owners = expert_count // local_experts
    capacity = min(seq_len, max(2, 2 * seq_len * top_count // expert_count))
    slot_total = expert_count * capacity
    gate_weight_complete, up_weight_complete, down_weight_complete = (
        lax.all_gather(w_gate, "dp", axis=2, tiled=True),
        lax.all_gather(w_up, "dp", axis=2, tiled=True),
        lax.all_gather(w_down, "dp", axis=1, tiled=True),
    )
    cosine_table, sine_table = rope_tables(seq_len, HDIM)
    places = jnp.arange(seq_len)
    slot_ids = jnp.arange(slot_total)
    expert_ids = jnp.arange(expert_count)
    score_scale = HDIM ** (-0.5)
    grad_query = jnp.zeros((model_width, model_width), jnp.float32)
    grad_key = jnp.zeros((model_width, model_width), jnp.float32)
    grad_value = jnp.zeros((model_width, model_width), jnp.float32)
    grad_out = jnp.zeros((model_width, model_width), jnp.float32)
    grad_router = jnp.zeros((model_width, expert_count), jnp.float32)
    grad_gain_attn = jnp.zeros((model_width,), jnp.float32)
    grad_gain_ffn = jnp.zeros((model_width,), jnp.float32)
    grad_gain_query = jnp.zeros((model_width,), jnp.float32)
    grad_gain_key = jnp.zeros((model_width,), jnp.float32)
    grad_gate = jnp.zeros(gate_weight_complete.shape, jnp.float32)
    grad_up = jnp.zeros(up_weight_complete.shape, jnp.float32)
    grad_down = jnp.zeros(down_weight_complete.shape, jnp.float32)
    outs_mixed = []
    outs_grad = []
    for micro_step in range(micro_count):
        layer_set = (
            lax.all_gather(w_query, "shard", axis=0, tiled=True),
            lax.all_gather(w_key, "shard", axis=0, tiled=True),
            lax.all_gather(w_value, "shard", axis=0, tiled=True),
            lax.all_gather(w_out, "shard", axis=0, tiled=True),
            lax.all_gather(w_router, "shard", axis=0, tiled=True),
            lax.all_gather(g_attn, "shard", axis=0, tiled=True),
            lax.all_gather(g_ffn, "shard", axis=0, tiled=True),
            lax.all_gather(g_query, "shard", axis=0, tiled=True),
            lax.all_gather(g_key, "shard", axis=0, tiled=True),
        )
        query_full, key_full, value_full, out_full, route_full = (
            layer_set[0],
            layer_set[1],
            layer_set[2],
            layer_set[3],
            layer_set[4],
        )
        gain_attn = layer_set[5].astype(jnp.float32)
        gain_ffn = layer_set[6].astype(jnp.float32)
        gain_query = layer_set[7].astype(jnp.float32)
        gain_key = layer_set[8].astype(jnp.float32)
        inputs = tokens[micro_step, 0].astype(jnp.float32)
        length = lengths[micro_step, 0]
        route_ids = routes[micro_step, 0]
        normed = rms_norm(inputs, gain_attn).astype(jnp.bfloat16)
        query_raw = matmul(normed, query_full)
        key_raw = matmul(normed, key_full)
        value_raw = matmul(normed, value_full)
        value_low = value_raw.astype(jnp.bfloat16).reshape(seq_len, HEADS, HDIM)
        query_low = rotate(
            rms_norm(query_raw, gain_query).reshape(seq_len, HEADS, HDIM), cosine_table, sine_table
        ).astype(jnp.bfloat16)
        key_low = rotate(
            rms_norm(key_raw, gain_key).reshape(seq_len, HEADS, HDIM), cosine_table, sine_table
        ).astype(jnp.bfloat16)
        allowed = (places[None, :] <= places[:, None]) & (places[None, :] < length)
        scores = (
            jnp.einsum("qhd,khd->hqk", query_low, key_low, preferred_element_type=jnp.float32)
            * score_scale
        )
        attn_probs = softmax_rows(jnp.where(allowed[None], scores, -1e30))
        probs_low = attn_probs.astype(jnp.bfloat16)
        mixed_low = (
            jnp.einsum("hqk,khd->qhd", probs_low, value_low, preferred_element_type=jnp.float32)
            .reshape(seq_len, model_width)
            .astype(jnp.bfloat16)
        )
        attn_part = matmul(mixed_low, out_full)
        hidden_state = inputs + attn_part
        ffn_in = rms_norm(hidden_state, gain_ffn).astype(jnp.bfloat16)
        logits = matmul(ffn_in, route_full)
        router = softmax_rows(logits)
        chosen = route_ids[:, :, None] == expert_ids[None, None, :]
        gate_vals = jnp.sum(jnp.where(chosen, router[:, None, :], 0.0), axis=2)
        flat_chosen = chosen.reshape(seq_len * top_count, expert_count).astype(jnp.int32)
        before = jnp.cumsum(flat_chosen, axis=0) - flat_chosen
        slot_rank = jnp.sum(before * flat_chosen, axis=1)
        target = route_ids.reshape(-1) * capacity + slot_rank
        placing = (slot_ids[:, None] == target[None, :]).astype(jnp.bfloat16)
        token_placing = jnp.sum(placing.reshape(slot_total, seq_len, top_count), axis=2)
        outgoing = matmul(token_placing, ffn_in).astype(jnp.bfloat16)
        arrived = dispatch_rows(outgoing.reshape(owners, local_experts * capacity, model_width))
        expert_token_rows = to_experts(arrived, local_experts, capacity)
        gate_pre = jnp.einsum(
            "qjs,qsy->qjy",
            expert_token_rows,
            gate_weight_complete,
            preferred_element_type=jnp.float32,
        )
        up_value = jnp.einsum(
            "qjs,qsy->qjy",
            expert_token_rows,
            up_weight_complete,
            preferred_element_type=jnp.float32,
        )
        sigmoid_gate = jax.nn.sigmoid(gate_pre)
        activated = gate_pre * sigmoid_gate
        inner_activation = (activated * up_value).astype(jnp.bfloat16)
        expert_out = jnp.einsum(
            "aqc,aco->aqo",
            inner_activation,
            down_weight_complete,
            preferred_element_type=jnp.float32,
        ).astype(jnp.bfloat16)
        returned = collect_rows(from_experts(expert_out, owners, capacity)).reshape(
            slot_total, model_width
        )
        picked = (
            jnp.take(returned, target, axis=0)
            .astype(jnp.float32)
            .reshape(seq_len, top_count, model_width)
        )
        expert_sum = jnp.sum(picked * gate_vals[:, :, None], axis=1)
        outs_mixed.append((hidden_state + expert_sum).astype(jnp.bfloat16))
        live_mask = (places < length).astype(jnp.float32)
        d_output = cotangent[micro_step, 0].astype(jnp.float32) * live_mask[:, None]
        d_gates = jnp.sum(picked * d_output[:, None, :], axis=2)
        d_slots = (
            (gate_vals[:, :, None] * d_output[:, None, :])
            .astype(jnp.bfloat16)
            .reshape(seq_len * top_count, model_width)
        )
        d_outgoing = matmul(placing, d_slots).astype(jnp.bfloat16)
        d_arrived = dispatch_grads(
            d_outgoing.reshape(owners, local_experts * capacity, model_width)
        )
        expert_output_gradient = to_experts(d_arrived, local_experts, capacity)
        d_inner = jnp.einsum(
            "azy,ajy->azj",
            expert_output_gradient,
            down_weight_complete,
            preferred_element_type=jnp.float32,
        )
        grad_down = grad_down + jnp.einsum(
            "qti,qtj->qij",
            inner_activation,
            expert_output_gradient,
            preferred_element_type=jnp.float32,
        )
        gate_preactivation_gradient = (
            d_inner * up_value * (sigmoid_gate + gate_pre * sigmoid_gate * (1.0 - sigmoid_gate))
        ).astype(jnp.bfloat16)
        up_projection_value_gradient = (d_inner * activated).astype(jnp.bfloat16)
        grad_gate = grad_gate + jnp.einsum(
            "hzo,hzg->hog",
            expert_token_rows,
            gate_preactivation_gradient,
            preferred_element_type=jnp.float32,
        )
        grad_up = grad_up + jnp.einsum(
            "hzo,hzg->hog",
            expert_token_rows,
            up_projection_value_gradient,
            preferred_element_type=jnp.float32,
        )
        d_rows = jnp.einsum(
            "ing,itg->int",
            gate_preactivation_gradient,
            gate_weight_complete,
            preferred_element_type=jnp.float32,
        )
        d_rows = (
            d_rows
            + jnp.einsum(
                "ing,itg->int",
                up_projection_value_gradient,
                up_weight_complete,
                preferred_element_type=jnp.float32,
            )
        ).astype(jnp.bfloat16)
        d_returned = collect_grads(from_experts(d_rows, owners, capacity)).reshape(
            slot_total, model_width
        )
        d_ffn_in = jnp.sum(
            jnp.take(d_returned, target, axis=0)
            .astype(jnp.float32)
            .reshape(seq_len, top_count, model_width),
            axis=1,
        )
        d_router = jnp.sum(jnp.where(chosen, d_gates[:, :, None], 0.0), axis=1)
        d_logits = (router * (d_router - jnp.sum(router * d_router, axis=1, keepdims=True))).astype(
            jnp.bfloat16
        )
        grad_router = grad_router + transposed_times(ffn_in, d_logits)
        d_ffn_in = d_ffn_in + times_transposed(d_logits, route_full)
        d_hidden_norm, d_gain_ffn = norm_back(hidden_state, gain_ffn, d_ffn_in)
        grad_gain_ffn = grad_gain_ffn + d_gain_ffn
        d_hidden = d_output + d_hidden_norm
        d_attn_low = d_hidden.astype(jnp.bfloat16)
        grad_out = grad_out + transposed_times(mixed_low, d_attn_low)
        d_mixed_wide = times_transposed(d_attn_low, out_full)
        d_mixed = d_mixed_wide.astype(jnp.bfloat16).reshape(seq_len, HEADS, HDIM)
        d_probs = jnp.einsum("qhd,khd->hqk", d_mixed, value_low, preferred_element_type=jnp.float32)
        d_value = (
            jnp.einsum("hqk,qhd->khd", probs_low, d_mixed, preferred_element_type=jnp.float32)
            .reshape(seq_len, model_width)
            .astype(jnp.bfloat16)
        )
        d_scores = (
            attn_probs * (d_probs - jnp.sum(attn_probs * d_probs, axis=-1, keepdims=True))
        ).astype(jnp.bfloat16)
        d_query = (
            jnp.einsum("hqk,khd->qhd", d_scores, key_low, preferred_element_type=jnp.float32)
            * score_scale
        )
        d_key = (
            jnp.einsum("hqk,qhd->khd", d_scores, query_low, preferred_element_type=jnp.float32)
            * score_scale
        )
        d_query_raw, d_gain_query = norm_back(
            query_raw,
            gain_query,
            rotate_back(d_query, cosine_table, sine_table).reshape(seq_len, model_width),
        )
        d_key_raw, d_gain_key = norm_back(
            key_raw,
            gain_key,
            rotate_back(d_key, cosine_table, sine_table).reshape(seq_len, model_width),
        )
        grad_gain_query = grad_gain_query + d_gain_query
        grad_gain_key = grad_gain_key + d_gain_key
        d_query_low = d_query_raw.astype(jnp.bfloat16)
        d_key_low = d_key_raw.astype(jnp.bfloat16)
        grad_query = grad_query + transposed_times(normed, d_query_low)
        grad_key = grad_key + transposed_times(normed, d_key_low)
        grad_value = grad_value + transposed_times(normed, d_value)
        d_normed = (
            times_transposed(d_query_low, query_full)
            + times_transposed(d_key_low, key_full)
            + times_transposed(d_value, value_full)
        )
        d_input_norm, d_gain_attn = norm_back(inputs, gain_attn, d_normed)
        grad_gain_attn = grad_gain_attn + d_gain_attn
        outs_grad.append(d_hidden + d_input_norm)
    layer_sums = (
        lax.psum_scatter(
            grad_query.astype(jnp.bfloat16), "shard", scatter_dimension=0, tiled=True
        ).astype(jnp.float32),
        lax.psum_scatter(
            grad_key.astype(jnp.bfloat16), "shard", scatter_dimension=0, tiled=True
        ).astype(jnp.float32),
        lax.psum_scatter(
            grad_value.astype(jnp.bfloat16), "shard", scatter_dimension=0, tiled=True
        ).astype(jnp.float32),
        lax.psum_scatter(
            grad_out.astype(jnp.bfloat16), "shard", scatter_dimension=0, tiled=True
        ).astype(jnp.float32),
        lax.psum_scatter(
            grad_router.astype(jnp.bfloat16), "shard", scatter_dimension=0, tiled=True
        ).astype(jnp.float32),
        lax.psum_scatter(
            grad_gain_attn.astype(jnp.bfloat16), "shard", scatter_dimension=0, tiled=True
        ).astype(jnp.float32),
        lax.psum_scatter(
            grad_gain_ffn.astype(jnp.bfloat16), "shard", scatter_dimension=0, tiled=True
        ).astype(jnp.float32),
        lax.psum_scatter(
            grad_gain_query.astype(jnp.bfloat16), "shard", scatter_dimension=0, tiled=True
        ).astype(jnp.float32),
        lax.psum_scatter(
            grad_gain_key.astype(jnp.bfloat16), "shard", scatter_dimension=0, tiled=True
        ).astype(jnp.float32),
    )
    layer_totals = (
        lax.psum(layer_sums[0].astype(jnp.bfloat16), ("dp", "expert")).astype(jnp.float32),
        lax.psum(layer_sums[1].astype(jnp.bfloat16), ("dp", "expert")).astype(jnp.float32),
        lax.psum(layer_sums[2].astype(jnp.bfloat16), ("dp", "expert")).astype(jnp.float32),
        lax.psum(layer_sums[3].astype(jnp.bfloat16), ("dp", "expert")).astype(jnp.float32),
        lax.psum(layer_sums[4].astype(jnp.bfloat16), ("dp", "expert")).astype(jnp.float32),
        lax.psum(layer_sums[5].astype(jnp.bfloat16), ("dp", "expert")).astype(jnp.float32),
        lax.psum(layer_sums[6].astype(jnp.bfloat16), ("dp", "expert")).astype(jnp.float32),
        lax.psum(layer_sums[7].astype(jnp.bfloat16), ("dp", "expert")).astype(jnp.float32),
        lax.psum(layer_sums[8].astype(jnp.bfloat16), ("dp", "expert")).astype(jnp.float32),
    )
    expert_totals = (
        lax.psum_scatter(
            grad_gate.astype(jnp.bfloat16), "dp", scatter_dimension=2, tiled=True
        ).astype(jnp.float32),
        lax.psum_scatter(
            grad_up.astype(jnp.bfloat16), "dp", scatter_dimension=2, tiled=True
        ).astype(jnp.float32),
        lax.psum_scatter(
            grad_down.astype(jnp.bfloat16), "dp", scatter_dimension=1, tiled=True
        ).astype(jnp.float32),
    )
    mixed_out = jnp.stack(outs_mixed)[:, None]
    grad_tokens = jnp.stack(outs_grad)[:, None]
    return (
        mixed_out,
        grad_tokens,
        layer_totals[0],
        layer_totals[1],
        layer_totals[2],
        layer_totals[3],
        layer_totals[4],
        layer_totals[5],
        layer_totals[6],
        layer_totals[7],
        layer_totals[8],
        expert_totals[0],
        expert_totals[1],
        expert_totals[2],
    )


def solution(mesh):
    placed = (
        P(None, ("dp", "expert", "shard"), None, None),
        P(None, ("dp", "expert", "shard"), None, None),
        P(None, ("dp", "expert", "shard")),
        P(None, ("dp", "expert", "shard"), None, None),
        P("shard", None),
        P("shard", None),
        P("shard", None),
        P("shard", None),
        P("shard", None),
        P("shard"),
        P("shard"),
        P("shard"),
        P("shard"),
        P(("expert", "shard"), None, "dp"),
        P(("expert", "shard"), None, "dp"),
        P(("expert", "shard"), "dp", None),
    )
    sizes = (mesh.shape["dp"], mesh.shape["expert"], mesh.shape["shard"])
    return jax.shard_map(
        gathered if sizes == (2, 4, 4) else exchanged,
        mesh=mesh,
        in_specs=placed,
        out_specs=(
            P(None, ("dp", "expert", "shard"), None, None),
            P(None, ("dp", "expert", "shard"), None, None),
            P("shard", None),
            P("shard", None),
            P("shard", None),
            P("shard", None),
            P("shard", None),
            P("shard"),
            P("shard"),
            P("shard"),
            P("shard"),
            P(("expert", "shard"), None, "dp"),
            P(("expert", "shard"), None, "dp"),
            P(("expert", "shard"), "dp", None),
        ),
        check_vma=False,
    )
```

```python
import functools

import jax
import jax.numpy as jnp
import numpy as np
from jax import lax
from jax.experimental import pallas as pl
from jax.experimental.pallas import tpu as pltpu
from jax.sharding import PartitionSpec as P

HEADS = 16
HDIM = 128


EPSILON = 1e-05


def matmul(left, right):
    return jnp.dot(left, right, preferred_element_type=jnp.float32)


def times_transposed(left, right):
    return lax.dot_general(
        left, right, (((1,), (1,)), ((), ())), preferred_element_type=jnp.float32
    )


def transposed_times(left, right):
    return lax.dot_general(
        left, right, (((0,), (0,)), ((), ())), preferred_element_type=jnp.float32
    )


def rms_norm(values, gain_vec):
    factor = lax.rsqrt(jnp.mean(values * values, axis=-1, keepdims=True) + EPSILON)
    return values * factor * gain_vec


def norm_back(values, gain_vec, incoming):
    factor = lax.rsqrt(jnp.mean(values * values, axis=-1, keepdims=True) + EPSILON)
    unit_rows = values * factor
    weighted = incoming * gain_vec
    d_values = factor * (
        weighted - unit_rows * jnp.mean(weighted * unit_rows, axis=-1, keepdims=True)
    )
    return (d_values, jnp.sum(incoming * unit_rows, axis=0))


def rope_tables(seq_count, head_size):
    half_dim = head_size // 2
    freqs = 10000.0 ** (-2.0 * jnp.arange(half_dim).astype(jnp.float32) / head_size)
    angles = jnp.arange(seq_count).astype(jnp.float32)[:, None] * freqs[None, :]
    cosine_table = jnp.concatenate([jnp.cos(angles), jnp.cos(angles)], axis=-1)
    sine_table = jnp.concatenate([jnp.sin(angles), jnp.sin(angles)], axis=-1)
    return (cosine_table, sine_table)


def rotate(head_rows, cosine_table, sine_table):
    half_dim = head_rows.shape[-1] // 2
    turned = jnp.concatenate([-head_rows[..., half_dim:], head_rows[..., :half_dim]], axis=-1)
    return head_rows * cosine_table[:, None, :] + turned * sine_table[:, None, :]


def rotate_back(incoming, cosine_table, sine_table):
    half_dim = incoming.shape[-1] // 2
    moved_part = incoming * sine_table[:, None, :]
    turned = jnp.concatenate([moved_part[..., half_dim:], -moved_part[..., :half_dim]], axis=-1)
    return incoming * cosine_table[:, None, :] + turned


def softmax_rows(scores):
    shifted = jnp.exp(scores - jnp.max(scores, axis=-1, keepdims=True))
    return shifted / jnp.sum(shifted, axis=-1, keepdims=True)


MESH_ID = pl.DeviceIdType.MESH
EXTRA = 128
ANY = pl.BlockSpec(memory_space=pl.ANY)


def place():
    return lax.axis_index("dp"), lax.axis_index("expert"), lax.axis_index("shard")


def x_of(e):
    return e + 1 - 2 * lax.rem(e, 2)


def y_of(e):
    return lax.rem(e + 2, 4)


def greet(peers):
    barrier = pltpu.get_barrier_semaphore()
    for peer in peers:
        pl.semaphore_signal(barrier, inc=1, device_id=peer, device_id_type=MESH_ID)
    pl.semaphore_wait(barrier, len(peers))


class Copies:
    def __init__(self):
        self.started = []

    def send(self, src, dst, send_sem, recv_sem, device, when=None):
        copy = pltpu.make_async_remote_copy(
            src_ref=src,
            dst_ref=dst,
            send_sem=send_sem,
            recv_sem=recv_sem,
            device_id=device,
            device_id_type=MESH_ID,
        )
        if when is None:
            copy.start()
        else:
            pl.when(when)(copy.start)
        self.started.append((copy, when))

    def drain(self):
        for copy, when in self.started:
            if when is None:
                copy.wait_send()
            else:
                pl.when(when)(copy.wait_send)


def arrived(ref, sem, other):
    pltpu.make_async_remote_copy(
        src_ref=ref,
        dst_ref=ref,
        send_sem=sem,
        recv_sem=sem,
        device_id=other,
        device_id_type=MESH_ID,
    ).wait_recv()


class SemPool:
    def __init__(self, ref):
        self.ref = ref
        self.used = 0

    def take(self):
        self.used += 1
        assert self.used <= self.ref.shape[0]
        return self.ref.at[self.used - 1]


class Item:
    def __init__(self, own, dst, recv, skip=False, cross=None, cross_recv=None):
        self.own, self.dst, self.recv = own, dst, recv
        self.skip, self.cross, self.cross_recv = skip, cross, cross_recv


class Gather:
    def __init__(self, item, copies, pool):
        self.item, self.copies, self.pool = item, copies, pool
        self.dp, self.e, self.z = place()
        self.px, self.py = x_of(self.e), y_of(self.e)
        self.diag = x_of(self.py)
        self.firsts, self.seconds = (self.px, self.py), (self.py, self.px)

    def send(self, h, ee, zz, target, zt, when, own=False):
        item = self.item
        ref = item.dst(zz, ee, h)
        self.copies.send(item.own(h) if own else ref, ref, self.pool.take(), item.recv.at[h, ee * 4 + zz],
                         (self.dp, target, zt), when)

    def across(self, h, ee, zz, when):
        item = self.item
        if item.cross is not None:
            ref = item.dst(zz, ee, h)
            self.copies.send(ref, ref, self.pool.take(), item.cross_recv.at[h, ee * 4 + zz],
                             (1 - self.dp, self.e, self.z), when)

    def wait(self, h, ee, zz, when):
        def body():
            arrived(self.item.dst(zz, ee, h), self.item.recv.at[h, ee * 4 + zz], (self.dp, self.e, self.z))
        if when is None:
            body()
        else:
            pl.when(when)(body)

    def steps(self, k):
        if k == 0:
            return [(self.z, None, 1)]
        out = []
        for sign in (-1, 1):
            zz = self.z + sign * k
            out.append((zz, (zz >= 0) & (zz <= 3), sign))
        return out

    def begin_z(self):
        for h in (0, 1):
            for sign in (-1, 1):
                nxt = self.z + sign
                self.send(h, self.e, self.z, self.e, nxt, (nxt >= 0) & (nxt <= 3), own=True)

    def begin_plane(self):
        for h in (0, 1):
            for target in (self.firsts[h], self.seconds[h]):
                self.send(h, self.e, self.z, target, self.z, None, own=True)

    def own_stage(self, k):
        for zz, valid, sign in self.steps(k):
            nxt = self.z - sign
            for h in (0, 1):
                self.wait(h, self.e, zz, valid)
                self.send(h, self.e, zz, self.e, nxt, valid & (nxt >= 0) & (nxt <= 3))
                self.send(h, self.e, zz, self.firsts[h], self.z, valid)
                self.send(h, self.e, zz, self.seconds[h], self.z, valid)
                self.across(h, self.e, zz, valid)

    def relay_stage(self, k):
        if k == 0 and self.item.skip:
            return
        for zz, valid, _ in self.steps(k):
            for h in (0, 1):
                self.wait(h, self.firsts[h], zz, valid)
                self.send(h, self.firsts[h], zz, self.seconds[h], self.z, valid)
                self.across(h, self.firsts[h], zz, valid)

    def last_stage(self, k):
        if k == 0 and self.item.skip:
            return
        for zz, valid, _ in self.steps(k):
            for h in (0, 1):
                for ee in (self.seconds[h], self.diag):
                    self.wait(h, ee, zz, valid)
                    self.across(h, ee, zz, valid)

    def cross_stage(self):
        if self.item.cross is None:
            return
        for k in (1, 2, 3):
            for zz, valid, _ in self.steps(k):
                @pl.when(valid)
                def _(zz=zz):
                    for ee in range(4):
                        for h in (0, 1):
                            arrived(self.item.cross(zz, ee, h), self.item.cross_recv.at[h, ee * 4 + zz],
                                    (self.dp, self.e, self.z))

    def both_ways(self, h, ee, own=False):
        for sign in (-1, 1):
            nxt = self.z + sign
            self.send(h, ee, self.z, self.e, nxt, (nxt >= 0) & (nxt <= 3), own=own)

    def plane_relay(self):
        for h in (0, 1):
            self.wait(h, self.firsts[h], self.z, None)
            self.send(h, self.firsts[h], self.z, self.seconds[h], self.z, None)

    def line_begin(self, group):
        for h in (0, 1):
            if group == 0:
                self.both_ways(h, self.e, own=True)
                self.both_ways(h, self.firsts[h])
            else:
                for ee in (self.seconds[h], self.diag):
                    self.wait(h, ee, self.z, None)
                    self.both_ways(h, ee)

    def line_stage(self, k, group):
        for zz, valid, sign in self.steps(k):
            nxt = self.z - sign
            for h in (0, 1):
                for ee in ((self.e, self.firsts[h]), (self.seconds[h], self.diag))[group]:
                    self.wait(h, ee, zz, valid)
                    self.send(h, ee, zz, self.e, nxt, valid & (nxt >= 0) & (nxt <= 3))


class Plane:
    def __init__(self, own, all_rows, recv, send, relay, cross):
        self.own, self.all_rows, self.recv = own, all_rows, recv
        self.send, self.relay, self.cross = send, relay, cross
        self.dp, self.e, self.z = place()
        px, py = x_of(self.e), y_of(self.e)
        self.plane = (px, py, x_of(py))
        self.half = all_rows.shape[1] // 2

    def at(self, ref, h):
        return ref.at[pl.ds(h * self.half, self.half)]

    def copy(self, src, slot, h, send_sem, device):
        return pltpu.make_async_remote_copy(
            src_ref=src, dst_ref=self.at(self.all_rows.at[slot], h), send_sem=send_sem,
            recv_sem=self.recv.at[h, slot], device_id=device, device_id_type=MESH_ID)

    def first(self, n, h):
        target = (1 - self.dp, self.e, self.z) if n == 2 else (self.dp, self.plane[n], self.z)
        return self.copy(self.at(self.own, h), self.dp * 4 + self.e, h, self.send.at[n, h], target)

    def on(self, h):
        slot = self.dp * 4 + self.plane[h]
        return self.copy(self.at(self.all_rows.at[slot], h), slot, h, self.relay.at[h],
                         (self.dp, self.plane[1 - h], self.z))

    def over(self, n, h):
        slot = self.dp * 4 + self.plane[n]
        return self.copy(self.at(self.all_rows.at[slot], h), slot, h, self.cross.at[n, h],
                         (1 - self.dp, self.e, self.z))

    def wait(self, h, slot):
        arrived(self.at(self.all_rows.at[slot], h), self.recv.at[h, slot], (self.dp, self.e, self.z))

    def begin(self):
        for n in range(3):
            for h in (0, 1):
                self.first(n, h).start()

    def pass_on(self):
        for h in (0, 1):
            self.wait(h, self.dp * 4 + self.plane[h])
            self.on(h).start()
            self.over(h, h).start()

    def end(self):
        for h in (0, 1):
            self.wait(h, self.dp * 4 + self.plane[1 - h])
            self.over(1 - h, h).start()
        for h in (0, 1):
            self.wait(h, self.dp * 4 + self.plane[2])
            self.over(2, h).start()

    def end_cross(self):
        for ee in range(4):
            for h in (0, 1):
                self.wait(h, (1 - self.dp) * 4 + ee)

    def drain(self):
        for h in (0, 1):
            for n in range(3):
                self.first(n, h).wait_send()
                self.over(n, h).wait_send()
            self.on(h).wait_send()


def mates_of():
    dp, e, z = place()
    return [(lax.rem(dp + d // 4, 2), lax.rem(e + d % 4, 4), z) for d in range(1, 8)]


def columns_of(d, ee):
    return pl.ds(pl.multiple_of(ee * 512 + d * 256, 256), 256)


def as_column(row, count):
    return jnp.broadcast_to(row, (count, row.shape[1])).T


def as_row(column):
    return jnp.broadcast_to(column, (column.shape[0], 128)).T[0:1]


def chosen_experts(route_ids):
    lane = lax.broadcasted_iota(jnp.int32, (route_ids.shape[0], EXTRA), 1)
    found = route_ids[:, 0:1] == lane
    for r in range(1, route_ids.shape[1]):
        found = found | (route_ids[:, r:r + 1] == lane)
    return found


def allowed_keys(live_row):
    rows = live_row.shape[1]
    i = lax.broadcasted_iota(jnp.int32, (rows, rows), 0)
    j = lax.broadcasted_iota(jnp.int32, (rows, rows), 1)
    half = rows // 2
    return ((i < half) == (j < half)) & (j <= i) & (live_row > 0.5)


def front_kernel(
    tok, cot, live, route_ids, cosine, sine, route_in, gains_in, wq, wk, wv, wo, wg, wu, wd,
    q_raw, k_raw, q_low, k_low, v_low, squares, lives, mixed, hidden, ffn_in, router, small_rows, dy,
    rows_all, w_cols, w_out, wide_all, dy_all, wg_far, wu_far, wd_far,
    X, Wc, Wo, R, small, normed, mixed_cols, mixed_own, parts, sent, load_sem, store_sem, x_recv, x_send, x_relay, x_cross,
    recv_w, recv_o, cross_o, recv_a, recv_b, recv_r, recv_small, recv_far, recv_live, recv_sq, recv_mix,
    mate_send, send_sems,
):
    dp, e, z = place()
    px, py = x_of(e), y_of(e)
    me, far = (dp, e, z), (1 - dp, e, z)
    f32, bf = jnp.float32, jnp.bfloat16
    rows, width = tok.shape
    quarter = width // 4
    slot_z = e * 4 + z
    slot_me = dp * 4 + e
    mates = mates_of()
    own_cols = columns_of(dp, e)

    def local(src, dst, sem):
        return pltpu.make_async_copy(src, dst, sem)

    z_rows = pl.ds(pl.multiple_of(z * 512, 512), 512)
    loads = [local(ref.at[:, own_cols], Wc.at[m, z_rows], load_sem.at[m]) for m, ref in enumerate((wq, wk, wv))]
    loads.append(local(wo, Wo.at[z_rows], load_sem.at[3]))
    for load in loads:
        load.start()
    unit = (lax.broadcasted_iota(jnp.int32, (16, 16), 0) == lax.broadcasted_iota(jnp.int32, (16, 16), 1)).astype(bf)
    small[0:16] = times_transposed(unit, route_in[...]).astype(bf)
    small[16:] = gains_in[...]
    dy_live = jnp.where(as_column(live[0:1], rows)[:, :1] > 0.5, cot[...].astype(f32), 0.0)
    dy[...] = dy_live.astype(bf).reshape(dy.shape)
    greet([(dp, e, lax.rem(z + d, 4)) for d in (1, 2, 3)] + mates)
    copies, pool = Copies(), SemPool(send_sems)

    def to_mates(src, dst, recv_at, kind):
        for n, mate in enumerate(mates):
            copies.send(src(mate), dst, mate_send.at[kind, n], recv_at, mate)

    def cols_piece(zz, h):
        return Wc.at[:, pl.ds(pl.multiple_of(zz * 512 + h * 256, 256), 256), :]

    def cols_send(zz, h, sign, when):
        nxt = z + sign
        on = (nxt >= 0) & (nxt <= 3)
        copies.send(cols_piece(zz, h), cols_piece(zz, h), pool.take(), recv_w.at[h, zz], (dp, e, nxt),
                    on if when is None else on & when)

    def cols_stage(k):
        for sign in (-1, 1):
            zz = z + sign * k
            valid = (zz >= 0) & (zz <= 3)
            for h in (0, 1):
                @pl.when(valid)
                def _(zz=zz, h=h):
                    arrived(cols_piece(zz, h), recv_w.at[h, zz], me)
                cols_send(zz, h, -sign, valid)

    def out_piece(d):
        def at(zz, ee, h):
            return Wo.at[pl.ds(pl.multiple_of(zz * 512 + ee * 128 + d * 64 + h * 32, 32), 32), :]
        return at

    out_at = out_piece(dp)
    cuts = (32, 32)
    out_g = Gather(Item(lambda h: out_at(z, e, h), out_at, recv_o, skip=True, cross=out_piece(1 - dp),
                        cross_recv=cross_o), copies, pool)
    dy_a = Gather(Item(lambda h: dy.at[h, 0:cuts[h]], lambda zz, ee, h: dy_all.at[ee * 4 + zz, h, 0:cuts[h]], recv_a),
                  copies, pool)
    dy_b = Gather(Item(lambda h: dy.at[h, cuts[h]:64], lambda zz, ee, h: dy_all.at[ee * 4 + zz, h, cuts[h]:64], recv_b),
                  copies, pool)
    b_all = Gather(Item(lambda h: wide_all.at[slot_z, h], lambda zz, ee, h: wide_all.at[ee * 4 + zz, h], recv_r),
                   copies, pool)
    x_plane = Plane(normed, X, x_recv, x_send, x_relay, x_cross)

    for d in (1, 2, 3):
        copies.send(small, small_rows.at[z], pool.take(), recv_small.at[z], (dp, e, lax.rem(z + d, 4)))
    to_mates(lambda mate: live, lives.at[slot_me], recv_live.at[slot_me], 0)
    small_store = local(small, small_rows.at[z], store_sem.at[0])
    small_store.start()
    dy_store = local(dy, dy_all.at[slot_z], store_sem.at[1])
    dy_store.start()
    for load in loads:
        load.wait()
    for h in (0, 1):
        for sign in (-1, 1):
            cols_send(z, h, sign, None)
    small_store.wait()
    for d in (1, 2, 3):
        zz = lax.rem(z + d, 4)
        arrived(small_rows.at[zz], recv_small.at[zz], me)
    for zz in range(4):
        R[:, zz * quarter:(zz + 1) * quarter] = small_rows[zz]

    def gain(i):
        return R[16 + i:17 + i, :].astype(f32)

    def factor(values):
        return lax.rsqrt(jnp.mean(values * values, axis=1, keepdims=True) + EPSILON)

    x = tok[...].astype(f32)
    normed[...] = (x * factor(x) * gain(0)).astype(bf)
    x_plane.begin()
    x_keep = local(normed, X.at[slot_me], store_sem.at[2])
    x_keep.start()
    lives[slot_me] = live[...]
    dy_a.begin_plane()
    dy_b.begin_plane()
    cols_stage(1)
    out_g.begin_z()
    x_plane.pass_on()
    for i, (src, dst) in enumerate(((wg, wg_far), (wu, wu_far), (wd, wd_far))):
        copies.send(src, dst, pool.take(), recv_far.at[i], far)
    dy_a.relay_stage(0)
    dy_b.plane_relay()
    cols_stage(2)
    x_plane.end()
    out_g.own_stage(1)
    dy_a.begin_z()
    x_plane.end_cross()
    x_keep.wait()
    for n in range(7):
        od, oe, _ = mates[n]
        arrived(lives.at[od * 4 + oe], recv_live.at[od * 4 + oe], me)
    rows_store = local(X, rows_all, store_sem.at[3])
    rows_store.start()
    cols_stage(3)
    cols_store = local(Wc, w_cols, store_sem.at[5])
    cols_store.start()
    out_g.relay_stage(1)

    def project(g, _):
        at = pl.ds(g * 4, 4)
        block = X[at].reshape(4 * rows, width)
        for m, ref in enumerate((q_raw, k_raw)):
            ref[at] = jnp.dot(block, Wc[m], preferred_element_type=f32).reshape(4, rows, 256)
        v_low[at] = jnp.dot(block, Wc[2], preferred_element_type=f32).astype(bf).reshape(4, rows, 256)
        for i in range(4):
            for m, ref in enumerate((q_raw, k_raw)):
                values = ref[g * 4 + i]
                parts[slot_me, m, pl.ds(g * 4 + i, 1), :] = as_row(jnp.sum(values * values, axis=1, keepdims=True))
        return 0

    lax.fori_loop(0, 2, project, 0)
    to_mates(lambda mate: parts.at[slot_me], parts.at[slot_me], recv_sq.at[slot_me], 1)
    out_g.own_stage(2)
    dy_b.line_begin(0)
    for n in range(7):
        od, oe, _ = mates[n]
        arrived(parts.at[od * 4 + oe], recv_sq.at[od * 4 + oe], me)
    squares[...] = (((parts[0] + parts[1]) + (parts[2] + parts[3]))
                    + ((parts[4] + parts[5]) + (parts[6] + parts[7]))) * (1.0 / width)
    cos_t = jnp.concatenate([cosine[...]] * 2, axis=0)
    sin_t = jnp.concatenate([sine[...]] * 2, axis=0)

    def attend(d, _):
        allowed = allowed_keys(lives[d][0:1])
        for m, (raw, low) in enumerate(((q_raw, q_low), (k_raw, k_low))):
            scale = lax.rsqrt(as_column(squares[m, pl.ds(d, 1), :], HDIM) + EPSILON)
            for hh in range(2):
                cc = slice(hh * HDIM, (hh + 1) * HDIM)
                gains = R[18 + m:19 + m, pl.ds(pl.multiple_of(e * 512 + dp * 256 + hh * HDIM, HDIM), HDIM)].astype(f32)
                u = raw[d, :, cc] * scale * gains
                low[d, :, cc] = (u * cos_t + pltpu.roll(u, HDIM // 2, 1) * sin_t).astype(bf)
        for hh in range(2):
            cc = slice(hh * HDIM, (hh + 1) * HDIM)
            scores = times_transposed(q_low[d, :, cc], k_low[d, :, cc]) * (HDIM ** (-0.5))
            probs = softmax_rows(jnp.where(allowed, scores, -1e30))
            mixed_cols[d, :, cc] = jnp.dot(probs.astype(bf), v_low[d, :, cc], preferred_element_type=f32).astype(bf)
        return 0

    lax.fori_loop(0, 4, attend, 0)
    out_g.relay_stage(2)
    out_g.own_stage(3)
    dy_b.line_begin(1)
    lax.fori_loop(4, 8, attend, 0)
    to_mates(lambda mate: mixed_cols.at[mate[0] * 4 + mate[1]], mixed_own.at[:, own_cols], recv_mix.at[slot_me], 2)
    mixed_own[:, own_cols] = mixed_cols[slot_me]
    out_g.last_stage(1)
    out_g.relay_stage(3)
    dy_a.own_stage(1)
    for n in range(7):
        od, oe, _ = mates[n]
        arrived(mixed_own.at[:, columns_of(od, oe)], recv_mix.at[od * 4 + oe], me)
    mixed[...] = mixed_own[...]
    out_g.last_stage(2)
    dy_b.line_stage(1, 0)
    dy_a.relay_stage(1)
    out_g.last_stage(3)
    out_g.cross_stage()
    full_o = local(Wo, w_out, store_sem.at[4])
    full_o.start()

    def out_col(j, _):
        cc = pl.ds(pl.multiple_of(j * 512, 512), 512)
        hidden[:, cc] = tok[:, cc].astype(f32) + jnp.dot(mixed[...], Wo[:, cc], preferred_element_type=f32)
        return 0

    lax.fori_loop(0, 4, out_col, 0)
    h1 = hidden[...]
    b = (h1 * factor(h1) * gain(1)).astype(bf)
    ffn_in[...] = b
    lane = lax.broadcasted_iota(jnp.int32, (rows, EXTRA), 1)
    logits = jnp.where(lane < 16, times_transposed(b, R[...]), -1e30)
    picks = softmax_rows(logits)
    router[...] = picks
    gates = jnp.where(chosen_experts(route_ids[...]), picks, 0.0)
    high = gates.astype(bf).astype(f32)
    extra = high + pltpu.roll(gates - high, 16, 1)
    sent[:, :, :width] = b.reshape(2, rows // 2, width)
    sent[:, :, width:] = extra.astype(bf).reshape(2, rows // 2, EXTRA)
    keep = local(sent, wide_all.at[slot_z], store_sem.at[6])
    keep.start()
    keep.wait()
    b_all.begin_plane()
    b_all.begin_z()
    dy_a.own_stage(2)
    dy_b.line_stage(1, 1)
    dy_a.relay_stage(2)
    b_all.relay_stage(0)
    b_all.own_stage(1)
    dy_a.own_stage(3)
    dy_b.line_stage(2, 0)
    b_all.relay_stage(1)
    b_all.own_stage(2)
    dy_a.relay_stage(3)
    dy_b.line_stage(2, 1)
    b_all.relay_stage(2)
    b_all.own_stage(3)
    b_all.relay_stage(3)
    for group in (0, 1):
        dy_b.line_stage(3, group)
    for k in range(4):
        dy_a.last_stage(k)
    for k in range(4):
        b_all.last_stage(k)
    for i, dst in enumerate((wg_far, wu_far, wd_far)):
        arrived(dst, recv_far.at[i], me)
    copies.drain()
    x_plane.drain()
    for store in (dy_store, full_o, rows_store, cols_store):
        store.wait()


def front(tok, cot, live, route_ids, cosine, sine, route_in, gains_in, *weights):
    bf, f32 = jnp.bfloat16, jnp.float32
    dma = pltpu.SemaphoreType.DMA
    shape = jax.ShapeDtypeStruct
    vmem = pl.BlockSpec(memory_space=pltpu.VMEM)
    rows, width = tok.shape
    wg, wu, wd = weights[4:]
    return pl.pallas_call(
        front_kernel,
        out_shape=(
            shape((8, rows, 256), f32),
            shape((8, rows, 256), f32),
            shape((8, rows, 256), bf),
            shape((8, rows, 256), bf),
            shape((8, rows, 256), bf),
            shape((2, 8, rows), f32),
            shape((8, 8, rows), f32),
            shape((rows, width), bf),
            shape((rows, width), f32),
            shape((rows, width), bf),
            shape((rows, EXTRA), f32),
            shape((4, EXTRA, width // 4), bf),
            shape((2, rows // 2, width), bf),
            shape((8, rows, width), bf),
            shape((3, width, 256), bf),
            shape((width, width), bf),
            shape((16, 2, rows // 2, width + EXTRA), bf),
            shape((16, 2, rows // 2, width), bf),
            shape(wg.shape, bf),
            shape(wu.shape, bf),
            shape(wd.shape, bf),
        ),
        in_specs=[vmem] * 8 + [ANY] * 7,
        out_specs=(vmem,) * 13 + (ANY,) * 8,
        scratch_shapes=[
            pltpu.VMEM((8, rows, width), bf),
            pltpu.VMEM((3, width, 256), bf),
            pltpu.VMEM((width, width), bf),
            pltpu.VMEM((EXTRA, width), bf),
            pltpu.VMEM((EXTRA, width // 4), bf),
            pltpu.VMEM((rows, width), bf),
            pltpu.VMEM((8, rows, 256), bf),
            pltpu.VMEM((rows, width), bf),
            pltpu.VMEM((8, 2, 8, rows), f32),
            pltpu.VMEM((2, rows // 2, width + EXTRA), bf),
            dma((4,)),
            dma((7,)),
            dma((2, 8)),
            dma((3, 2)),
            dma((2,)),
            dma((3, 2)),
            dma((2, 4)),
            dma((2, 16)),
            dma((2, 16)),
            dma((2, 16)),
            dma((2, 16)),
            dma((2, 16)),
            dma((4,)),
            dma((3,)),
            dma((8,)),
            dma((8,)),
            dma((8,)),
            dma((3, 7)),
            dma((330,)),
        ],
        compiler_params=pltpu.CompilerParams(collective_id=0, has_side_effects=True, vmem_limit_bytes=62 * 2**20),
        name="attention_front",
    )(tok, cot, live, route_ids, cosine, sine, route_in, gains_in, *weights)


def times(left, right):
    return jnp.dot(left, right, preferred_element_type=jnp.float32)


def experts_kernel(
    wide, dy, wg, wu, wd, wgf, wuf, wdf,
    res, eg, eu, ed, part, a_buf, b_buf,
    c_buf, WG, WU, WD, rows_in, dy_rows, hidden, saved, acc, stage, addend, turned, column, far_out,
    w_sem, dy_sem, in_sem, part_sem, add_sem, col_sem, fin_sem, out_sem,
    a_sem, b_sem, c_sem, a_send, b_send, c_send, gu_send, gu_sem, dn_send, dn_sem, free_sem,
):
    dp, e, z = place()
    px, py = x_of(e), y_of(e)
    diag = x_of(y_of(e))
    me = (dp, e, z)
    far_core = (1 - dp, e, z)
    f32, bf = jnp.float32, jnp.bfloat16
    width = dy.shape[3]
    half_f = wg.shape[1]
    total_width = part.shape[3]

    def local(src, dst, sem):
        return pltpu.make_async_copy(src, dst, sem)

    def remote(src, dst, send_sem, recv_sem, device):
        return pltpu.make_async_remote_copy(
            src_ref=src, dst_ref=dst, send_sem=send_sem, recv_sem=recv_sem,
            device_id=device, device_id_type=MESH_ID)

    def column_of(c):
        return jnp.where(c == 0, diag, jnp.where(c == 1, py, jnp.where(c == 2, px, e)))

    def zed(i):
        return lax.rem(z + jnp.where(i == 0, 2, jnp.where(i == 1, 1, jnp.where(i == 2, 3, 0))), 4)

    def kind_of(s):
        return jnp.where(s < 2, 0, jnp.where(s < 4, 3, 1 + lax.rem(s, 2)))

    def zed_of(s, i):
        return zed(2 * jnp.where(s < 4, lax.rem(s, 2), (s - 4) // 2) + i)

    def slot_of(s, i):
        return column_of(kind_of(s)) * 4 + zed_of(s, i)

    def rows_load(s, i, buf):
        return local(wide.at[slot_of(s, i)], rows_in.at[buf, i], in_sem.at[buf, i])

    weights = [
        local(src, dst, w_sem.at[n])
        for n, (src, dst) in enumerate((
            (wg, WG.at[0]), (wu, WU.at[0]), (wd, WD.at[0]), (wgf, WG.at[1]), (wuf, WU.at[1]), (wdf, WD.at[1])))
    ]
    for i in range(2):
        rows_load(0, i, 0).start()
    weights[0].start()
    weights[1].start()
    def dy_load(s, i):
        return local(dy.at[slot_of(s, i)], dy_rows.at[slot_of(s, i)], dy_sem.at[s, i])

    for i in range(2):
        dy_load(0, i).start()
    for load in weights[2:]:
        load.start()
    for s in range(1, 8):
        for i in range(2):
            dy_load(s, i).start()
    greet([(dp, e, lax.rem(z + d, 4)) for d in (1, 2, 3)] + [(dp, px, z), (dp, py, z), far_core])

    def part_write(s, i):
        return local(stage.at[lax.rem(s, 2), i], part.at[slot_of(s, i)], part_sem.at[lax.rem(s, 2), i])

    def a_copy(h, g, slot, zz, target):
        return remote(part.at[slot, h], a_buf.at[h, g, zz], a_send.at[h, g, zz], a_sem.at[h, g, zz], (dp, target, z))

    def b_copy(h, slot, zz, target):
        return remote(part.at[slot, h], b_buf.at[h, zz], b_send.at[h, zz], b_sem.at[h, zz], (dp, target, z))

    def send_step(s):
        c = kind_of(s)
        for i in range(2):
            part_write(s, i).wait()
            zz = zed_of(s, i)

            @pl.when(c == 0)
            def _():
                a_copy(0, 0, diag * 4 + zz, zz, py).start()
                a_copy(1, 0, diag * 4 + zz, zz, px).start()

            @pl.when(c == 1)
            def _():
                a_copy(0, 1, py * 4 + zz, zz, py).start()
                b_copy(1, py * 4 + zz, zz, py).start()

            @pl.when(c == 2)
            def _():
                a_copy(1, 1, px * 4 + zz, zz, px).start()
                b_copy(0, px * 4 + zz, zz, px).start()

    def addend_load(s, i):
        h = jnp.where(kind_of(s) == 1, 1, 0)
        zz = zed_of(s, i)
        return local(a_buf.at[h, 0, zz], addend.at[i], add_sem.at[i])

    mine = e * 4 + z
    route_rows = turned
    lane = lax.broadcasted_iota(jnp.int32, (256, EXTRA), 1)
    at_high, at_low = lane == mine, lane == mine + 16

    weights[0].wait()
    weights[1].wait()

    def step(s, _):
        buf = lax.rem(s, 2)

        @pl.when(s + 1 < 8)
        def _():
            for i in range(2):
                rows_load(s + 1, i, 1 - buf).start()
        for i in range(2):
            rows_load(s, i, buf).wait()
            dy_load(s, i).wait()
        slots = [slot_of(s, i) for i in range(2)]
        extra = rows_in[buf, :, :, :, width:].reshape(256, EXTRA).astype(f32)
        gate = jnp.sum(jnp.where(at_high | at_low, extra, 0.0), axis=1, keepdims=True)

        def dy_step():
            return jnp.concatenate([dy_rows[slot].reshape(128, width) for slot in slots], axis=0)

        def put(ref, values, at):
            for i in range(2):
                ref[slots[i], :, pl.ds(pl.multiple_of(at, half_f), half_f)] = values[i * 128:(i + 1) * 128]

        dy_route = (gate * dy_step().astype(f32)).astype(bf)
        route_rows[...] = dy_route
        acc[...] = jnp.zeros_like(acc)

        def half_step(n, _):
            @pl.when((s == 0) & (n == 1))
            def _():
                for load in weights[3:]:
                    load.wait()

            @pl.when((s > 1) & (n == 1))
            def _():
                send_step(s - 1)

            @pl.when((s >= 4) & (n == 1))
            def _():
                for i in range(2):
                    h = jnp.where(kind_of(s) == 1, 1, 0)
                    zz = zed_of(s, i)
                    arrived(a_buf.at[h, 0, zz], a_sem.at[h, 0, zz], me)
                    addend_load(s, i).start()
            x = rows_in[buf, :, :, :, :width].reshape(256, width)
            gate_pre = times(x, WG[n])
            up_value = times(x, WU[n])
            sigmoid_gate = jax.nn.sigmoid(gate_pre)
            activated = gate_pre * sigmoid_gate
            inner = (activated * up_value).astype(bf)
            put(hidden, inner, n * half_f)

            @pl.when((s == 0) & (n == 0))
            def _():
                weights[2].wait()
            d_inner = times_transposed(route_rows[...], WD[n])
            d_gate = (d_inner * up_value * (sigmoid_gate + gate_pre * sigmoid_gate * (1.0 - sigmoid_gate))).astype(bf)
            d_up = (d_inner * activated).astype(bf)
            put(saved, d_gate, 2 * n * half_f)
            put(saved, d_up, (2 * n + 1) * half_f)
            acc[0] += times(inner, WD[n])
            acc[1] += times_transposed(d_gate, WG[n]) + times_transposed(d_up, WU[n])
            return 0

        lax.fori_loop(0, 2, half_step, 0)
        y_low = acc[0].astype(bf).astype(f32)
        d_own = jnp.sum(y_low * dy_step().astype(f32), axis=1, keepdims=True)
        high = d_own.astype(bf).astype(f32)
        tail = jnp.where(at_high, high, jnp.where(at_low, d_own - high, 0.0)).astype(bf)

        def lay(values):
            return values.reshape(2, 2, 64, values.shape[1])

        stage[buf, :, :, :, :width] = lay((gate * y_low).astype(bf))
        stage[buf, :, :, :, width:width + EXTRA] = lay(tail)
        stage[buf, :, :, :, width + EXTRA:] = lay(acc[1].astype(bf))
        for i in range(2):
            dy_rows[slots[i]] = route_rows[i * 128:(i + 1) * 128].reshape(2, 64, width)

        @pl.when(s >= 4)
        def _():
            h = jnp.where(kind_of(s) == 1, 1, 0)
            for i in range(2):
                addend_load(s, i).wait()
                stage[buf, i, h] = (stage[buf, i, h].astype(f32) + addend[i].astype(f32)).astype(bf)
        for i in range(2):
            part_write(s, i).start()

        @pl.when(s == 0)
        def _():
            send_step(s)
        return 0

    lax.fori_loop(0, 8, step, 0)
    pl.semaphore_signal(free_sem, inc=1, device_id=far_core, device_id_type=MESH_ID)
    send_step(7)

    def finish_loads(k):
        zz = zed(k)
        return (local(part.at[e * 4 + zz], stage.at[0, 0], fin_sem.at[0]),
                local(a_buf.at[:, 1, zz], stage.at[0, 1], fin_sem.at[1]),
                local(b_buf.at[:, zz], stage.at[1, 0], fin_sem.at[2]))

    def begin(k):
        zz = zed(k)
        for h in range(2):
            arrived(a_buf.at[h, 1, zz], a_sem.at[h, 1, zz], me)
            arrived(b_buf.at[h, zz], b_sem.at[h, zz], me)
        for load in finish_loads(k):
            load.start()

    def result_write(k):
        return local(stage.at[1, 1], part.at[e * 4 + zed(k)], fin_sem.at[3])

    def c_copy(k):
        zz = zed(k)
        there = (0, 2, 1)[k]
        return remote(part.at[e * 4 + zz], c_buf.at[there], c_send.at[k], c_sem.at[there], (dp, e, zz))

    def close(k):
        for load in finish_loads(k):
            load.wait()
        for h in range(2):
            total = (stage[0, 0, h].astype(f32) + stage[0, 1, h].astype(f32)) + stage[1, 0, h].astype(f32)
            if k < 3:
                stage[1, 1, h] = total.astype(bf)
            else:
                res[h] = total
        if k < 3:
            result_write(k).start()

    def fire(k):
        result_write(k).wait()
        c_copy(k).start()

    def turn_hidden(n):
        turned[...] = hidden[:, :, pl.ds(pl.multiple_of(n * 256, 256), 256)].reshape(2048, 256).T

    def down_block(dst):
        def col(j, _):
            cc = pl.ds(pl.multiple_of(j * 512, 512), 512)
            dst(cc, times(turned[...], dy_rows[:, :, :, cc].reshape(2048, 512)))
            return 0
        lax.fori_loop(0, 4, col, 0)

    def column_load(n):
        return local(wide.at[:, :, :, pl.ds(pl.multiple_of(n * 256, 256), 256)], column.at[lax.rem(n, 2)],
                     col_sem.at[lax.rem(n, 2)])

    def down_send(n):
        return remote(far_out.at[n], WD.at[1, pl.ds(n * 256, 256)], dn_send.at[n], dn_sem.at[n], far_core)

    column_load(0).start()
    for n in range(2):
        turn_hidden(2 + n)

        def to_far(cc, values, n=n):
            far_out[n, :, cc] = values.astype(bf)
        down_block(to_far)
        if n == 0:
            pl.semaphore_wait(free_sem, 1)
        down_send(n).start()

    def row_block(n):
        return pl.ds(pl.multiple_of(n * 256, 256), 256)

    def gu_copy(n, w):
        buf = lax.rem(n, 2)
        return remote(far_out.at[buf, :, w * 512:(w + 1) * 512], WG.at[w, row_block(n)],
                      gu_send.at[buf, w], gu_sem.at[n, w], far_core)

    def gu_out(n, w):
        buf = lax.rem(n, 2)
        return local(acc.at[buf, :, w * 512:(w + 1) * 512], (eg, eu)[w].at[row_block(n)], out_sem.at[buf, w])

    def settle(n):
        buf = lax.rem(n, 2)
        for w in range(2):
            arrived(WG.at[w, row_block(n)], gu_sem.at[n, w], me)
            acc[buf, :, w * 512:(w + 1) * 512] += WG[w, row_block(n)].astype(f32)
            gu_out(n, w).start()

    def gate_up(n, _):
        buf = lax.rem(n, 2)

        @pl.when(n + 1 < 8)
        def _():
            column_load(n + 1).start()
        column_load(n).wait()
        turned[...] = column[buf].reshape(2048, 256).T

        @pl.when(n < 2)
        def _():
            for k in range(2):
                @pl.when(n == k)
                def _(k=k):
                    down_send(k).wait_send()

        @pl.when(n >= 2)
        def _():
            for w in range(2):
                gu_copy(n - 2, w).wait_send()
                gu_out(n - 2, w).wait()

        def far_col(j, _):
            cc = pl.ds(pl.multiple_of(j * 512, 512), 512)
            src = pl.ds(pl.multiple_of(1024 + j * 512, 512), 512)
            far_out[buf, :, cc] = times(turned[...], saved[:, :, src].reshape(2048, 512)).astype(bf)
            return 0

        def near_col(j, _):
            cc = pl.ds(pl.multiple_of(j * 512, 512), 512)
            acc[buf, :, cc] = times(turned[...], saved[:, :, cc].reshape(2048, 512))
            return 0
        lax.fori_loop(0, 2, far_col, 0)
        for w in range(2):
            gu_copy(n, w).start()
        lax.fori_loop(0, 2, near_col, 0)

        @pl.when(n > 0)
        def _():
            settle(n - 1)
        for at, act in ((2, lambda: begin(0)), (3, lambda: close(0)), (4, lambda: fire(0)),
                        (5, lambda: begin(1)), (6, lambda: close(1)), (7, lambda: fire(1))):
            pl.when(n == at)(act)
        return 0

    lax.fori_loop(0, 8, gate_up, 0)
    settle(7)
    for n in (6, 7):
        for w in range(2):
            gu_copy(n, w).wait_send()
            gu_out(n, w).wait()

    def down_out(n):
        return local(acc.at[n], ed.at[pl.ds(n * 256, 256)], out_sem.at[n, 0])

    for n in range(2):
        turn_hidden(n)

        def keep(cc, values, n=n):
            acc[n, :, cc] = values
        down_block(keep)
        arrived(WD.at[1, pl.ds(n * 256, 256)], dn_sem.at[n], me)
        acc[n] += WD[1, pl.ds(n * 256, 256)].astype(f32)
        down_out(n).start()
    begin(2)
    close(2)
    fire(2)
    begin(3)
    close(3)
    for k in range(3):
        arrived(c_buf.at[k], c_sem.at[k], me)
        for h in range(2):
            res[h] += c_buf[k, h].astype(f32)
    for n in range(2):
        down_out(n).wait()
    for k in range(3):
        c_copy(k).wait_send()

    def drain(zz, _):
        a_copy(0, 0, diag * 4 + zz, zz, py).wait_send()
        a_copy(1, 0, diag * 4 + zz, zz, px).wait_send()
        a_copy(0, 1, py * 4 + zz, zz, py).wait_send()
        b_copy(1, py * 4 + zz, zz, py).wait_send()
        a_copy(1, 1, px * 4 + zz, zz, px).wait_send()
        b_copy(0, px * 4 + zz, zz, px).wait_send()
        return 0
    lax.fori_loop(0, 4, drain, 0)


def experts(wide, dy, near, far):
    dma = pltpu.SemaphoreType.DMA
    bf, f32 = jnp.bfloat16, jnp.float32
    wg, wu, wd = near
    width, half_f = wg.shape
    rows = wide.shape[2]
    total_width = 2 * width + EXTRA
    shape = jax.ShapeDtypeStruct
    every = 16 * 2 * rows
    outs = pl.pallas_call(
        experts_kernel,
        out_shape=(
            shape((2, rows, total_width), f32),
            shape((width, half_f), f32),
            shape((width, half_f), f32),
            shape((half_f, width), f32),
            shape((16, 2, rows, total_width), bf),
            shape((2, 2, 4, rows, total_width), bf),
            shape((2, 4, rows, total_width), bf),
        ),
        in_specs=[ANY] * 8,
        out_specs=(pl.BlockSpec(memory_space=pltpu.VMEM),) + (ANY,) * 6,
        scratch_shapes=[
            pltpu.VMEM((3, 2, rows, total_width), bf),
            pltpu.VMEM((2, width, half_f), bf),
            pltpu.VMEM((2, width, half_f), bf),
            pltpu.VMEM((2, half_f, width), bf),
            pltpu.VMEM((2, 2, 2, rows, width + EXTRA), bf),
            pltpu.VMEM((16, 2, rows, width), bf),
            pltpu.VMEM((16, 2 * rows, 2 * half_f), bf),
            pltpu.VMEM((16, 2 * rows, 4 * half_f), bf),
            pltpu.VMEM((2, 256, width), f32),
            pltpu.VMEM((2, 2, 2, rows, total_width), bf),
            pltpu.VMEM((2, rows, total_width), bf),
            pltpu.VMEM((256, every), bf),
            pltpu.VMEM((2, 16, 2, rows, 256), bf),
            pltpu.VMEM((2, 256, width), bf),
            dma((6,)),
            dma((8, 2)),
            dma((2, 2)),
            dma((2, 2)),
            dma((2,)),
            dma((2,)),
            dma((4,)),
            dma((2, 2)),
            dma((2, 2, 4)),
            dma((2, 4)),
            dma((4,)),
            dma((2, 2, 4)),
            dma((2, 4)),
            dma((3,)),
            dma((2, 2)),
            dma((8, 2)),
            dma((2,)),
            dma((2,)),
            pltpu.SemaphoreType.REGULAR,
        ],
        compiler_params=pltpu.CompilerParams(collective_id=2, has_side_effects=True, vmem_limit_bytes=67043328),
        name="owned_expert",
    )(wide, dy, *near, *far)
    return outs[:4]


def back_kernel(
    sums, tok, route_ids, cosine, sine, dy, mixed, q_raw, k_raw, q_low, k_low, v_low, squares, lives, hidden, ffn_in,
    router, small_rows, rows_all, w_cols, w_out,
    mixed_out, grad_tokens, out, small_out,
    Wo, Wc, R, d_hidden, d_heads, DH, d_mix, g_q, g_k, parts, means, X, D, turned, G, own_sum, hop, send_buf, mine,
    far_rows, home_rows, small, s_z, s_all,
    w_sem, load_sem, x_recv, x_send, x_relay, x_cross, d_sem, d_send, h_sem, h_send, q_sem, q_send,
    hop_sem, hop_send, f_sem, f_send, r_sem, r_send, sz_sem, sz_send, sa_sem, sa_send,
    g_sem, g_send, g_pass, g_far, out_sem,
):
    dp, e, z = place()
    px, py = x_of(e), y_of(e)
    diag = x_of(py)
    plane = (px, py, diag)
    me, far = (dp, e, z), (1 - dp, e, z)
    f32, bf = jnp.float32, jnp.bfloat16
    rows, width = tok.shape
    quarter = width // 4
    slot_me = dp * 4 + e
    zs = [lax.rem(z + d, 4) for d in range(4)]
    mates = mates_of()
    own_cols = columns_of(dp, e)

    def local(src, dst, sem):
        return pltpu.make_async_copy(src, dst, sem)

    def remote(src, dst, send_sem, recv_sem, device):
        return pltpu.make_async_remote_copy(
            src_ref=src, dst_ref=dst, send_sem=send_sem, recv_sem=recv_sem,
            device_id=device, device_id_type=MESH_ID)

    load_out = local(w_out, Wo, w_sem.at[0])
    load_cols = local(w_cols, Wc, w_sem.at[1])
    load_rows = local(rows_all, X.at[0], load_sem.at[0])
    load_mixed = local(mixed, X.at[1, slot_me], load_sem.at[1])
    for load in (load_out, load_mixed, load_cols, load_rows):
        load.start()
    greet([(dp, e, zz) for zz in zs[1:]] + mates)
    m_plane = Plane(mixed, X.at[1], x_recv, x_send, x_relay, x_cross)
    m_plane.begin()

    def d_copy(n):
        od, oe, _ = mates[n]
        return remote(d_mix.at[:, columns_of(od, oe)], D.at[3, slot_me], d_send.at[n], d_sem.at[slot_me], mates[n])

    def h_copy(n):
        od, oe, _ = mates[n]
        return remote(d_heads.at[:, columns_of(od, oe)], DH.at[slot_me], h_send.at[n], h_sem.at[slot_me], mates[n])

    def q_copy(n):
        return remote(parts.at[slot_me], parts.at[slot_me], q_send.at[n], q_sem.at[slot_me], mates[n])

    def from_mates(ref, sem):
        for n in range(7):
            od, oe, _ = mates[n]
            arrived(ref.at[od * 4 + oe], sem.at[od * 4 + oe], me)

    def compute(m, i, buf):
        turned[...] = D[m].reshape(8 * rows, 256).T

        def block(zz, _):
            at = pl.ds(pl.multiple_of(zz * 512, 512), 512)
            G[buf, zz] = jnp.dot(turned[...], X[i, :, :, at].reshape(8 * rows, 512), preferred_element_type=f32)
            return 0
        lax.fori_loop(0, 4, block, 0)
        own_sum[m] = G[buf, z]

    middle = (z == 1) | (z == 2)
    lower = z < 2
    targets = (jnp.where(lower, 3, 0), jnp.where(lower, 2, 1), z + 1 - 2 * lax.rem(z, 2))

    def hop_copy(m, j):
        zt = targets[j]
        up = zt > z
        there = jnp.where(zt == z - 1, 4, zt)
        return remote(send_buf.at[m, j], hop.at[m, there], hop_send.at[m, j], hop_sem.at[m, there],
                      (dp, e, jnp.where(up, z + 1, z - 1)))

    def pass_on(m, buf):
        for j in range(3):
            zt = targets[j]

            @pl.when(middle)
            def _():
                arrived(hop.at[m, zt], hop_sem.at[m, zt], me)
                send_buf[m, j] = (G[buf, zt] + hop[m, zt].astype(f32)).astype(bf)

            @pl.when(jnp.logical_not(middle))
            def _():
                send_buf[m, j] = G[buf, zt].astype(bf)
            hop_copy(m, j).start()

    def out_at(m, d, ee, h):
        return out.at[m, pl.ds(h * 256, 256), columns_of(d, ee)]

    def g_copy(m, n, h):
        return remote(mine.at[m, pl.ds(h * 256, 256)], out_at(m, dp, e, h), g_send.at[m, n, h],
                      g_sem.at[m, h, slot_me], far if n == 2 else (dp, plane[n], z))

    def g_relay(m, h):
        ref = out_at(m, dp, plane[h], h)
        return remote(ref, ref, g_pass.at[m, h], g_sem.at[m, h, dp * 4 + plane[h]], (dp, plane[1 - h], z))

    def g_onward(m, n, h):
        ref = out_at(m, dp, plane[n], h)
        return remote(ref, ref, g_far.at[m, n, h], g_sem.at[m, h, dp * 4 + plane[n]], far)

    def wait_g(m, h, d, ee):
        arrived(out_at(m, d, ee, h), g_sem.at[m, h, d * 4 + ee], me)

    def keep(m):
        return local(mine.at[m], out.at[m, :, own_cols], out_sem.at[m])

    def finish(m):
        @pl.when(z > 0)
        def _():
            arrived(hop.at[m, z], hop_sem.at[m, z], me)
            own_sum[m] += hop[m, z].astype(f32)

        @pl.when(z < 3)
        def _():
            arrived(hop.at[m, 4], hop_sem.at[m, 4], me)
            own_sum[m] += hop[m, 4].astype(f32)
        mine[m] = own_sum[m].T.astype(bf)
        for h in (0, 1):
            for n in range(3):
                g_copy(m, n, h).start()
        keep(m).start()

    def relay_out(m):
        for h in (0, 1):
            wait_g(m, h, dp, plane[h])
            g_relay(m, h).start()
            g_onward(m, h, h).start()

    def end_out(m):
        for h in (0, 1):
            wait_g(m, h, dp, plane[1 - h])
            g_onward(m, 1 - h, h).start()
        for h in (0, 1):
            wait_g(m, h, dp, diag)
            g_onward(m, 2, h).start()

    for zz in range(4):
        R[:, zz * quarter:(zz + 1) * quarter] = small_rows[zz]

    def gain(i):
        return R[16 + i:17 + i, :].astype(f32)

    def norm_grad(values, gain_vec, incoming):
        factor = lax.rsqrt(jnp.mean(values * values, axis=1, keepdims=True) + EPSILON)
        unit = values * factor
        weighted = incoming * gain_vec
        back_values = factor * (weighted - unit * jnp.mean(weighted * unit, axis=1, keepdims=True))
        return back_values, jnp.sum(incoming * unit, axis=0, keepdims=True)

    def put_small(at, count, values):
        for zz in range(4):
            small[zz, at:at + count] = values[:, zz * quarter:(zz + 1) * quarter]

    for zz in range(4):
        small[zz] = jnp.zeros(small.shape[1:], f32)
    mixed_out[...] = (hidden[...] + sums[:, :width]).astype(bf)
    extra = sums[:, width:width + EXTRA]
    d_gates = extra + pltpu.roll(extra, EXTRA - 16, 1)
    picks = router[...]
    d_router = jnp.where(chosen_experts(route_ids[...]), d_gates, 0.0)
    d_logits = (picks * (d_router - jnp.sum(picks * d_router, axis=1, keepdims=True))).astype(bf)
    put_small(0, 16, jnp.dot(d_logits.T, ffn_in[...], preferred_element_type=f32)[:16])
    d_ffn = sums[:, width + EXTRA:] + jnp.dot(d_logits, R[...], preferred_element_type=f32)
    back_values, gain_grad = norm_grad(hidden[...], gain(1), d_ffn)
    put_small(17, 1, gain_grad)
    total = dy[...].astype(f32) + back_values
    d_hidden[...] = total
    d_mix[...] = total.astype(bf)
    load_out.wait()

    def heads_back(j, _):
        at = pl.ds(pl.multiple_of(j * 512, 512), 512)
        d_heads[:, at] = times_transposed(d_mix[...], Wo[at, :]).astype(bf)
        return 0

    lax.fori_loop(0, 4, heads_back, 0)
    for n in range(7):
        h_copy(n).start()
    for n in range(7):
        d_copy(n).start()
    DH[slot_me] = d_heads[:, own_cols]
    D[3, slot_me] = d_mix[:, own_cols]
    m_plane.pass_on()
    from_mates(DH, h_sem)

    cos_t = jnp.concatenate([cosine[...]] * 2, axis=0)
    sin_t = jnp.concatenate([sine[...]] * 2, axis=0)
    scale = HDIM ** (-0.5)

    def heads(d, grads):
        allowed = allowed_keys(lives[d][0:1])
        pieces = []
        for hh in range(2):
            cc = slice(hh * HDIM, (hh + 1) * HDIM)
            q, k, v, dh = q_low[d, :, cc], k_low[d, :, cc], v_low[d, :, cc], DH[d, :, cc]
            probs = softmax_rows(jnp.where(allowed, times_transposed(q, k) * scale, -1e30))
            d_probs = times_transposed(dh, v)
            D[2, d, :, cc] = jnp.dot(probs.astype(bf).T, dh, preferred_element_type=f32).astype(bf)
            d_scores = (probs * (d_probs - jnp.sum(probs * d_probs, axis=1, keepdims=True))).astype(bf)
            for z_in in (jnp.dot(d_scores, k, preferred_element_type=f32) * scale,
                         jnp.dot(d_scores.T, q, preferred_element_type=f32) * scale):
                pieces.append(z_in * cos_t - pltpu.roll(z_in, HDIM // 2, 1) * sin_t)
        outs = []
        for m, (raw, ref) in enumerate(((q_raw, g_q), (k_raw, g_k))):
            incoming = jnp.concatenate([pieces[m], pieces[2 + m]], axis=1)
            ref[d] = incoming
            factor = lax.rsqrt(as_column(squares[m, pl.ds(d, 1), :], 256) + EPSILON)
            unit = raw[d] * factor
            gains = R[18 + m:19 + m, own_cols].astype(f32)
            through = incoming * unit
            parts[slot_me, m, pl.ds(d, 1), :] = as_row(jnp.sum(through * gains, axis=1, keepdims=True))
            outs.append(grads[m] + jnp.sum(through, axis=0, keepdims=True))
        return tuple(outs)

    none = jnp.zeros((1, 256), f32)
    gain_grads = lax.fori_loop(0, 8, heads, (none, none))
    for n in range(7):
        q_copy(n).start()
    for m in range(2):
        small[e, 18 + m:19 + m, pl.ds(pl.multiple_of(dp * 256, 256), 256)] = gain_grads[m]
    m_plane.end()
    from_mates(D.at[3], d_sem)
    m_plane.end_cross()
    load_mixed.wait()
    compute(3, 1, 0)
    pass_on(3, 0)
    load_rows.wait()
    compute(2, 0, 1)
    from_mates(parts, q_sem)
    means[...] = (((parts[0] + parts[1]) + (parts[2] + parts[3]))
                  + ((parts[4] + parts[5]) + (parts[6] + parts[7]))) * (1.0 / width)

    def raw_back(d, _):
        for m, (raw, ref) in enumerate(((q_raw, g_q), (k_raw, g_k))):
            factor = lax.rsqrt(as_column(squares[m, pl.ds(d, 1), :], 256) + EPSILON)
            mean = as_column(means[m, pl.ds(d, 1), :], 256)
            gains = R[18 + m:19 + m, own_cols].astype(f32)
            D[m, d] = (factor * (ref[d] * gains - raw[d] * factor * mean)).astype(bf)
        return 0

    lax.fori_loop(0, 8, raw_back, 0)
    pass_on(2, 1)

    load_cols.wait()

    def part_of(d):
        values = times_transposed(D[0, d], Wc[0]) + times_transposed(D[1, d], Wc[1])
        return values + times_transposed(D[2, d], Wc[2])

    def f_copy(ee):
        return remote(Wo.at[pl.ds(ee * rows, rows)], far_rows.at[ee], f_send.at[ee], f_sem.at[ee], far)

    def r_copy(n):
        return remote(home_rows.at[3 + n], home_rows.at[n], r_send.at[n], r_sem.at[n], (dp, plane[n], z))

    for ee in range(4):
        Wo[ee * rows:(ee + 1) * rows] = part_of((1 - dp) * 4 + ee).astype(bf)
        f_copy(ee).start()
    for n in range(3):
        values = part_of(dp * 4 + plane[n])
        arrived(far_rows.at[plane[n]], f_sem.at[plane[n]], me)
        home_rows[3 + n] = (values + far_rows[plane[n]].astype(f32)).astype(bf)
        r_copy(n).start()
    compute(0, 0, 0)
    pass_on(0, 0)
    values = part_of(slot_me)
    arrived(far_rows.at[e], f_sem.at[e], me)
    grad_tokens[...] = values + far_rows[e].astype(f32)
    finish(3)
    compute(1, 0, 1)
    pass_on(1, 1)
    for n in range(3):
        arrived(home_rows.at[n], r_sem.at[n], me)
    back_values, gain_grad = norm_grad(
        tok[...].astype(f32), gain(0),
        (grad_tokens[...] + home_rows[0].astype(f32)) + (home_rows[1].astype(f32) + home_rows[2].astype(f32)))
    put_small(16, 1, gain_grad)
    grad_tokens[...] = d_hidden[...] + back_values

    def sz_copy(d):
        return remote(small.at[zs[d]], s_z.at[z], sz_send.at[d - 1], sz_sem.at[z], (dp, e, zs[d]))

    def sa_copy(d):
        return remote(s_all.at[slot_me], s_all.at[slot_me], sa_send.at[d - 1], sa_sem.at[slot_me], mates[d - 1])

    for d in (1, 2, 3):
        sz_copy(d).start()
    finish(2)
    relay_out(3)
    for d in (1, 2, 3):
        arrived(s_z.at[zs[d]], sz_sem.at[zs[d]], me)
    s_all[slot_me] = (small[z] + s_z[zs[1]]) + (s_z[zs[2]] + s_z[zs[3]])
    for d in range(1, 8):
        sa_copy(d).start()
    finish(0)
    relay_out(2)
    end_out(3)
    finish(1)
    relay_out(0)
    end_out(2)
    from_mates(s_all, sa_sem)
    small_out[...] = (((s_all[0] + s_all[1]) + (s_all[2] + s_all[3]))
                      + ((s_all[4] + s_all[5]) + (s_all[6] + s_all[7])))
    relay_out(1)
    end_out(0)
    end_out(1)
    for m in range(4):
        for h in (0, 1):
            for ee in range(4):
                wait_g(m, h, 1 - dp, ee)
            for n in range(3):
                g_copy(m, n, h).wait_send()
                g_onward(m, n, h).wait_send()
            g_relay(m, h).wait_send()
        keep(m).wait()
        for j in range(3):
            hop_copy(m, j).wait_send()
    m_plane.drain()
    for n in range(7):
        d_copy(n).wait_send()
        h_copy(n).wait_send()
        q_copy(n).wait_send()
        sa_copy(n + 1).wait_send()
    for ee in range(4):
        f_copy(ee).wait_send()
    for n in range(3):
        r_copy(n).wait_send()
        sz_copy(n + 1).wait_send()


def back(*args):
    dma = pltpu.SemaphoreType.DMA
    bf, f32 = jnp.bfloat16, jnp.float32
    shape = jax.ShapeDtypeStruct
    vmem = pl.BlockSpec(memory_space=pltpu.VMEM)
    rows, width = args[1].shape
    small_shape = (4, 24, width // 4)
    return pl.pallas_call(
        back_kernel,
        out_shape=(
            shape((rows, width), bf),
            shape((rows, width), f32),
            shape((4, width // 4, width), bf),
            shape(small_shape[1:], f32),
        ),
        in_specs=[vmem] * 18 + [ANY] * 3,
        out_specs=(vmem, vmem, ANY, vmem),
        scratch_shapes=[
            pltpu.VMEM((width, width), bf),
            pltpu.VMEM((3, width, 256), bf),
            pltpu.VMEM((EXTRA, width), bf),
            pltpu.VMEM((rows, width), f32),
            pltpu.VMEM((rows, width), bf),
            pltpu.VMEM((8, rows, 256), bf),
            pltpu.VMEM((rows, width), bf),
            pltpu.VMEM((8, rows, 256), f32),
            pltpu.VMEM((8, rows, 256), f32),
            pltpu.VMEM((8, 2, 8, rows), f32),
            pltpu.VMEM((2, 8, rows), f32),
            pltpu.VMEM((2, 8, rows, width), bf),
            pltpu.VMEM((4, 8, rows, 256), bf),
            pltpu.VMEM((256, 8 * rows), bf),
            pltpu.VMEM((2, 4, 256, 512), f32),
            pltpu.VMEM((4, 256, 512), f32),
            pltpu.VMEM((4, 5, 256, 512), bf),
            pltpu.VMEM((4, 3, 256, 512), bf),
            pltpu.VMEM((4, 512, 256), bf),
            pltpu.VMEM((4, rows, width), bf),
            pltpu.VMEM((6, rows, width), bf),
            pltpu.VMEM(small_shape, f32),
            pltpu.VMEM(small_shape, f32),
            pltpu.VMEM((8,) + small_shape[1:], f32),
            dma((2,)),
            dma((2,)),
            dma((2, 8)),
            dma((3, 2)),
            dma((2,)),
            dma((3, 2)),
            dma((8,)),
            dma((7,)),
            dma((8,)),
            dma((7,)),
            dma((8,)),
            dma((7,)),
            dma((4, 5)),
            dma((4, 3)),
            dma((4,)),
            dma((4,)),
            dma((3,)),
            dma((3,)),
            dma((4,)),
            dma((3,)),
            dma((8,)),
            dma((7,)),
            dma((4, 2, 8)),
            dma((4, 3, 2)),
            dma((4, 2)),
            dma((4, 3, 2)),
            dma((4,)),
        ],
        compiler_params=pltpu.CompilerParams(collective_id=3, has_side_effects=True, vmem_limit_bytes=63 * 2**20),
        name="attention_back",
    )(*args)


def lay_out_kernel(sums, eg, eu, ed, mixed, grad_in, o_q, o_k, o_v, o_o, o_eg, o_eu, o_ed, o_mixed, o_grad):
    for m, ref in enumerate((o_q, o_k, o_v, o_o)):
        ref[...] = sums[m].astype(jnp.float32)
    for src, dst in ((eg, o_eg), (eu, o_eu), (ed, o_ed), (mixed, o_mixed), (grad_in, o_grad)):
        dst[...] = src[...]


def lay_out(sums, *arrays):
    steps = 8
    f32 = jnp.float32
    wide = (sums.shape[1] // steps, sums.shape[2])

    def rows_spec(array):
        return pl.BlockSpec((array.shape[0] // steps, array.shape[1]), lambda i: (i, 0))

    rows = [rows_spec(a) for a in arrays]
    return pl.pallas_call(
        lay_out_kernel,
        grid=(steps,),
        out_shape=tuple([jax.ShapeDtypeStruct(sums.shape[1:], f32)] * 4
                        + [jax.ShapeDtypeStruct(a.shape, a.dtype) for a in arrays]),
        in_specs=[pl.BlockSpec((4,) + wide, lambda i: (0, i, 0))] + rows,
        out_specs=tuple([pl.BlockSpec(wide, lambda i: (i, 0))] * 4 + rows),
        compiler_params=pltpu.CompilerParams(vmem_limit_bytes=60 * 2**20),
        name="lay_out",
    )(sums, *arrays)


def gathered(
    tokens,
    cotangent,
    lengths,
    routes,
    w_query,
    w_key,
    w_value,
    w_out,
    w_router,
    g_attn,
    g_ffn,
    g_query,
    g_key,
    w_gate,
    w_up,
    w_down,
):
    micro_count, _, seq_len, model_width = tokens.shape
    expert_count = w_router.shape[1]
    f32, bf = jnp.float32, jnp.bfloat16
    places = jnp.arange(seq_len)
    length = lengths[:, 0]
    live = places[None, :] < length[:, None]
    rows = micro_count * seq_len
    gains = jnp.pad(jnp.stack([g_attn, g_ffn, g_query, g_key]), ((0, EXTRA - expert_count - 4), (0, 0)))
    half = HDIM // 2
    angles = np.arange(seq_len)[:, None] * 10000.0 ** (-2.0 * np.arange(half) / HDIM)[None, :]
    cosine_table = np.concatenate([np.cos(angles)] * 2, axis=1).astype(np.float32)
    turned_sine = np.concatenate([-np.sin(angles), np.sin(angles)], axis=1).astype(np.float32)
    live_rows = jnp.broadcast_to(live.astype(f32).reshape(1, rows), (8, rows))
    route_ids = routes[:, 0].reshape(rows, -1)
    tokens_here = tokens[:, 0].reshape(rows, model_width)
    (query_raw, key_raw, query_low, key_low, value_low, squares, lives, mixed_low, hidden_state, ffn_in, router,
     small_rows, dy, rows_all, w_cols, out_full, spread_rows, dy_all, gate_far, up_far, down_far) = front(
        tokens_here, cotangent[:, 0].reshape(rows, model_width), live_rows, route_ids, cosine_table, turned_sine,
        w_router, gains,
        w_query, w_key, w_value, w_out, w_gate[0], w_up[0], w_down[0])
    expert_sums, *expert_grads = experts(
        spread_rows, dy_all, (w_gate[0], w_up[0], w_down[0]), (gate_far, up_far, down_far))
    mixed_out, grad_tokens, sums, small_sums = back(
        expert_sums.reshape(rows, -1), tokens_here, route_ids, cosine_table, turned_sine,
        dy.reshape(rows, model_width), mixed_low, query_raw, key_raw, query_low, key_low, value_low, squares, lives,
        hidden_state, ffn_in, router, small_rows, rows_all, w_cols, out_full)
    *sums, grad_gate, grad_up, grad_down, mixed_out, grad_tokens = lay_out(
        sums, *expert_grads, mixed_out, grad_tokens)
    return (
        mixed_out.reshape(micro_count, 1, seq_len, model_width),
        grad_tokens.reshape(micro_count, 1, seq_len, model_width),
        sums[0],
        sums[1],
        sums[2],
        sums[3],
        small_sums[:expert_count].T,
        small_sums[expert_count],
        small_sums[expert_count + 1],
        small_sums[expert_count + 2],
        small_sums[expert_count + 3],
        grad_gate[None],
        grad_up[None],
        grad_down[None],
    )


def dispatch_rows(buffer):
    return lax.all_to_all(buffer, ("expert", "shard"), split_axis=0, concat_axis=0, tiled=True)


def collect_rows(buffer):
    return lax.all_to_all(buffer, ("expert", "shard"), split_axis=0, concat_axis=0, tiled=True)


def dispatch_grads(buffer):
    return lax.all_to_all(buffer, ("expert", "shard"), split_axis=0, concat_axis=0, tiled=True)


def collect_grads(buffer):
    return lax.all_to_all(buffer, ("expert", "shard"), split_axis=0, concat_axis=0, tiled=True)


def to_experts(arrived, local_experts, capacity):
    sources = arrived.shape[0]
    model_width = arrived.shape[2]
    split_rows = arrived.reshape(sources, local_experts, capacity, model_width)
    return jnp.swapaxes(split_rows, 0, 1).reshape(local_experts, sources * capacity, model_width)


def from_experts(expert_token_rows, owners, capacity):
    local_experts = expert_token_rows.shape[0]
    model_width = expert_token_rows.shape[2]
    split_rows = expert_token_rows.reshape(local_experts, owners, capacity, model_width)
    return jnp.swapaxes(split_rows, 0, 1).reshape(owners, local_experts * capacity, model_width)


def exchanged(
    tokens,
    cotangent,
    lengths,
    routes,
    w_query,
    w_key,
    w_value,
    w_out,
    w_router,
    g_attn,
    g_ffn,
    g_query,
    g_key,
    w_gate,
    w_up,
    w_down,
):
    micro_count = tokens.shape[0]
    seq_len = tokens.shape[2]
    model_width = tokens.shape[3]
    top_count = routes.shape[3]
    expert_count = w_router.shape[1]
    local_experts = w_gate.shape[0]
    owners = expert_count // local_experts
    capacity = min(seq_len, max(2, 2 * seq_len * top_count // expert_count))
    slot_total = expert_count * capacity
    gate_weight_complete, up_weight_complete, down_weight_complete = (
        lax.all_gather(w_gate, "dp", axis=2, tiled=True),
        lax.all_gather(w_up, "dp", axis=2, tiled=True),
        lax.all_gather(w_down, "dp", axis=1, tiled=True),
    )
    cosine_table, sine_table = rope_tables(seq_len, HDIM)
    places = jnp.arange(seq_len)
    slot_ids = jnp.arange(slot_total)
    expert_ids = jnp.arange(expert_count)
    score_scale = HDIM ** (-0.5)
    grad_query = jnp.zeros((model_width, model_width), jnp.float32)
    grad_key = jnp.zeros((model_width, model_width), jnp.float32)
    grad_value = jnp.zeros((model_width, model_width), jnp.float32)
    grad_out = jnp.zeros((model_width, model_width), jnp.float32)
    grad_router = jnp.zeros((model_width, expert_count), jnp.float32)
    grad_gain_attn = jnp.zeros((model_width,), jnp.float32)
    grad_gain_ffn = jnp.zeros((model_width,), jnp.float32)
    grad_gain_query = jnp.zeros((model_width,), jnp.float32)
    grad_gain_key = jnp.zeros((model_width,), jnp.float32)
    grad_gate = jnp.zeros(gate_weight_complete.shape, jnp.float32)
    grad_up = jnp.zeros(up_weight_complete.shape, jnp.float32)
    grad_down = jnp.zeros(down_weight_complete.shape, jnp.float32)
    outs_mixed = []
    outs_grad = []
    for micro_step in range(micro_count):
        layer_set = (
            lax.all_gather(w_query, "shard", axis=0, tiled=True),
            lax.all_gather(w_key, "shard", axis=0, tiled=True),
            lax.all_gather(w_value, "shard", axis=0, tiled=True),
            lax.all_gather(w_out, "shard", axis=0, tiled=True),
            lax.all_gather(w_router, "shard", axis=0, tiled=True),
            lax.all_gather(g_attn, "shard", axis=0, tiled=True),
            lax.all_gather(g_ffn, "shard", axis=0, tiled=True),
            lax.all_gather(g_query, "shard", axis=0, tiled=True),
            lax.all_gather(g_key, "shard", axis=0, tiled=True),
        )
        query_full, key_full, value_full, out_full, route_full = (
            layer_set[0],
            layer_set[1],
            layer_set[2],
            layer_set[3],
            layer_set[4],
        )
        gain_attn = layer_set[5].astype(jnp.float32)
        gain_ffn = layer_set[6].astype(jnp.float32)
        gain_query = layer_set[7].astype(jnp.float32)
        gain_key = layer_set[8].astype(jnp.float32)
        inputs = tokens[micro_step, 0].astype(jnp.float32)
        length = lengths[micro_step, 0]
        route_ids = routes[micro_step, 0]
        normed = rms_norm(inputs, gain_attn).astype(jnp.bfloat16)
        query_raw = matmul(normed, query_full)
        key_raw = matmul(normed, key_full)
        value_raw = matmul(normed, value_full)
        value_low = value_raw.astype(jnp.bfloat16).reshape(seq_len, HEADS, HDIM)
        query_low = rotate(
            rms_norm(query_raw, gain_query).reshape(seq_len, HEADS, HDIM), cosine_table, sine_table
        ).astype(jnp.bfloat16)
        key_low = rotate(
            rms_norm(key_raw, gain_key).reshape(seq_len, HEADS, HDIM), cosine_table, sine_table
        ).astype(jnp.bfloat16)
        allowed = (places[None, :] <= places[:, None]) & (places[None, :] < length)
        scores = (
            jnp.einsum("qhd,khd->hqk", query_low, key_low, preferred_element_type=jnp.float32)
            * score_scale
        )
        attn_probs = softmax_rows(jnp.where(allowed[None], scores, -1e30))
        probs_low = attn_probs.astype(jnp.bfloat16)
        mixed_low = (
            jnp.einsum("hqk,khd->qhd", probs_low, value_low, preferred_element_type=jnp.float32)
            .reshape(seq_len, model_width)
            .astype(jnp.bfloat16)
        )
        attn_part = matmul(mixed_low, out_full)
        hidden_state = inputs + attn_part
        ffn_in = rms_norm(hidden_state, gain_ffn).astype(jnp.bfloat16)
        logits = matmul(ffn_in, route_full)
        router = softmax_rows(logits)
        chosen = route_ids[:, :, None] == expert_ids[None, None, :]
        gate_vals = jnp.sum(jnp.where(chosen, router[:, None, :], 0.0), axis=2)
        flat_chosen = chosen.reshape(seq_len * top_count, expert_count).astype(jnp.int32)
        before = jnp.cumsum(flat_chosen, axis=0) - flat_chosen
        slot_rank = jnp.sum(before * flat_chosen, axis=1)
        target = route_ids.reshape(-1) * capacity + slot_rank
        placing = (slot_ids[:, None] == target[None, :]).astype(jnp.bfloat16)
        token_placing = jnp.sum(placing.reshape(slot_total, seq_len, top_count), axis=2)
        outgoing = matmul(token_placing, ffn_in).astype(jnp.bfloat16)
        arrived = dispatch_rows(outgoing.reshape(owners, local_experts * capacity, model_width))
        expert_token_rows = to_experts(arrived, local_experts, capacity)
        gate_pre = jnp.einsum(
            "qjs,qsy->qjy",
            expert_token_rows,
            gate_weight_complete,
            preferred_element_type=jnp.float32,
        )
        up_value = jnp.einsum(
            "qjs,qsy->qjy",
            expert_token_rows,
            up_weight_complete,
            preferred_element_type=jnp.float32,
        )
        sigmoid_gate = jax.nn.sigmoid(gate_pre)
        activated = gate_pre * sigmoid_gate
        inner_activation = (activated * up_value).astype(jnp.bfloat16)
        expert_out = jnp.einsum(
            "aqc,aco->aqo",
            inner_activation,
            down_weight_complete,
            preferred_element_type=jnp.float32,
        ).astype(jnp.bfloat16)
        returned = collect_rows(from_experts(expert_out, owners, capacity)).reshape(
            slot_total, model_width
        )
        picked = (
            jnp.take(returned, target, axis=0)
            .astype(jnp.float32)
            .reshape(seq_len, top_count, model_width)
        )
        expert_sum = jnp.sum(picked * gate_vals[:, :, None], axis=1)
        outs_mixed.append((hidden_state + expert_sum).astype(jnp.bfloat16))
        live_mask = (places < length).astype(jnp.float32)
        d_output = cotangent[micro_step, 0].astype(jnp.float32) * live_mask[:, None]
        d_gates = jnp.sum(picked * d_output[:, None, :], axis=2)
        d_slots = (
            (gate_vals[:, :, None] * d_output[:, None, :])
            .astype(jnp.bfloat16)
            .reshape(seq_len * top_count, model_width)
        )
        d_outgoing = matmul(placing, d_slots).astype(jnp.bfloat16)
        d_arrived = dispatch_grads(
            d_outgoing.reshape(owners, local_experts * capacity, model_width)
        )
        expert_output_gradient = to_experts(d_arrived, local_experts, capacity)
        d_inner = jnp.einsum(
            "azy,ajy->azj",
            expert_output_gradient,
            down_weight_complete,
            preferred_element_type=jnp.float32,
        )
        grad_down = grad_down + jnp.einsum(
            "qti,qtj->qij",
            inner_activation,
            expert_output_gradient,
            preferred_element_type=jnp.float32,
        )
        gate_preactivation_gradient = (
            d_inner * up_value * (sigmoid_gate + gate_pre * sigmoid_gate * (1.0 - sigmoid_gate))
        ).astype(jnp.bfloat16)
        up_projection_value_gradient = (d_inner * activated).astype(jnp.bfloat16)
        grad_gate = grad_gate + jnp.einsum(
            "hzo,hzg->hog",
            expert_token_rows,
            gate_preactivation_gradient,
            preferred_element_type=jnp.float32,
        )
        grad_up = grad_up + jnp.einsum(
            "hzo,hzg->hog",
            expert_token_rows,
            up_projection_value_gradient,
            preferred_element_type=jnp.float32,
        )
        d_rows = jnp.einsum(
            "ing,itg->int",
            gate_preactivation_gradient,
            gate_weight_complete,
            preferred_element_type=jnp.float32,
        )
        d_rows = (
            d_rows
            + jnp.einsum(
                "ing,itg->int",
                up_projection_value_gradient,
                up_weight_complete,
                preferred_element_type=jnp.float32,
            )
        ).astype(jnp.bfloat16)
        d_returned = collect_grads(from_experts(d_rows, owners, capacity)).reshape(
            slot_total, model_width
        )
        d_ffn_in = jnp.sum(
            jnp.take(d_returned, target, axis=0)
            .astype(jnp.float32)
            .reshape(seq_len, top_count, model_width),
            axis=1,
        )
        d_router = jnp.sum(jnp.where(chosen, d_gates[:, :, None], 0.0), axis=1)
        d_logits = (router * (d_router - jnp.sum(router * d_router, axis=1, keepdims=True))).astype(
            jnp.bfloat16
        )
        grad_router = grad_router + transposed_times(ffn_in, d_logits)
        d_ffn_in = d_ffn_in + times_transposed(d_logits, route_full)
        d_hidden_norm, d_gain_ffn = norm_back(hidden_state, gain_ffn, d_ffn_in)
        grad_gain_ffn = grad_gain_ffn + d_gain_ffn
        d_hidden = d_output + d_hidden_norm
        d_attn_low = d_hidden.astype(jnp.bfloat16)
        grad_out = grad_out + transposed_times(mixed_low, d_attn_low)
        d_mixed_wide = times_transposed(d_attn_low, out_full)
        d_mixed = d_mixed_wide.astype(jnp.bfloat16).reshape(seq_len, HEADS, HDIM)
        d_probs = jnp.einsum("qhd,khd->hqk", d_mixed, value_low, preferred_element_type=jnp.float32)
        d_value = (
            jnp.einsum("hqk,qhd->khd", probs_low, d_mixed, preferred_element_type=jnp.float32)
            .reshape(seq_len, model_width)
            .astype(jnp.bfloat16)
        )
        d_scores = (
            attn_probs * (d_probs - jnp.sum(attn_probs * d_probs, axis=-1, keepdims=True))
        ).astype(jnp.bfloat16)
        d_query = (
            jnp.einsum("hqk,khd->qhd", d_scores, key_low, preferred_element_type=jnp.float32)
            * score_scale
        )
        d_key = (
            jnp.einsum("hqk,qhd->khd", d_scores, query_low, preferred_element_type=jnp.float32)
            * score_scale
        )
        d_query_raw, d_gain_query = norm_back(
            query_raw,
            gain_query,
            rotate_back(d_query, cosine_table, sine_table).reshape(seq_len, model_width),
        )
        d_key_raw, d_gain_key = norm_back(
            key_raw,
            gain_key,
            rotate_back(d_key, cosine_table, sine_table).reshape(seq_len, model_width),
        )
        grad_gain_query = grad_gain_query + d_gain_query
        grad_gain_key = grad_gain_key + d_gain_key
        d_query_low = d_query_raw.astype(jnp.bfloat16)
        d_key_low = d_key_raw.astype(jnp.bfloat16)
        grad_query = grad_query + transposed_times(normed, d_query_low)
        grad_key = grad_key + transposed_times(normed, d_key_low)
        grad_value = grad_value + transposed_times(normed, d_value)
        d_normed = (
            times_transposed(d_query_low, query_full)
            + times_transposed(d_key_low, key_full)
            + times_transposed(d_value, value_full)
        )
        d_input_norm, d_gain_attn = norm_back(inputs, gain_attn, d_normed)
        grad_gain_attn = grad_gain_attn + d_gain_attn
        outs_grad.append(d_hidden + d_input_norm)
    layer_sums = (
        lax.psum_scatter(
            grad_query.astype(jnp.bfloat16), "shard", scatter_dimension=0, tiled=True
        ).astype(jnp.float32),
        lax.psum_scatter(
            grad_key.astype(jnp.bfloat16), "shard", scatter_dimension=0, tiled=True
        ).astype(jnp.float32),
        lax.psum_scatter(
            grad_value.astype(jnp.bfloat16), "shard", scatter_dimension=0, tiled=True
        ).astype(jnp.float32),
        lax.psum_scatter(
            grad_out.astype(jnp.bfloat16), "shard", scatter_dimension=0, tiled=True
        ).astype(jnp.float32),
        lax.psum_scatter(
            grad_router.astype(jnp.bfloat16), "shard", scatter_dimension=0, tiled=True
        ).astype(jnp.float32),
        lax.psum_scatter(
            grad_gain_attn.astype(jnp.bfloat16), "shard", scatter_dimension=0, tiled=True
        ).astype(jnp.float32),
        lax.psum_scatter(
            grad_gain_ffn.astype(jnp.bfloat16), "shard", scatter_dimension=0, tiled=True
        ).astype(jnp.float32),
        lax.psum_scatter(
            grad_gain_query.astype(jnp.bfloat16), "shard", scatter_dimension=0, tiled=True
        ).astype(jnp.float32),
        lax.psum_scatter(
            grad_gain_key.astype(jnp.bfloat16), "shard", scatter_dimension=0, tiled=True
        ).astype(jnp.float32),
    )
    layer_totals = (
        lax.psum(layer_sums[0].astype(jnp.bfloat16), ("dp", "expert")).astype(jnp.float32),
        lax.psum(layer_sums[1].astype(jnp.bfloat16), ("dp", "expert")).astype(jnp.float32),
        lax.psum(layer_sums[2].astype(jnp.bfloat16), ("dp", "expert")).astype(jnp.float32),
        lax.psum(layer_sums[3].astype(jnp.bfloat16), ("dp", "expert")).astype(jnp.float32),
        lax.psum(layer_sums[4].astype(jnp.bfloat16), ("dp", "expert")).astype(jnp.float32),
        lax.psum(layer_sums[5].astype(jnp.bfloat16), ("dp", "expert")).astype(jnp.float32),
        lax.psum(layer_sums[6].astype(jnp.bfloat16), ("dp", "expert")).astype(jnp.float32),
        lax.psum(layer_sums[7].astype(jnp.bfloat16), ("dp", "expert")).astype(jnp.float32),
        lax.psum(layer_sums[8].astype(jnp.bfloat16), ("dp", "expert")).astype(jnp.float32),
    )
    expert_totals = (
        lax.psum_scatter(
            grad_gate.astype(jnp.bfloat16), "dp", scatter_dimension=2, tiled=True
        ).astype(jnp.float32),
        lax.psum_scatter(
            grad_up.astype(jnp.bfloat16), "dp", scatter_dimension=2, tiled=True
        ).astype(jnp.float32),
        lax.psum_scatter(
            grad_down.astype(jnp.bfloat16), "dp", scatter_dimension=1, tiled=True
        ).astype(jnp.float32),
    )
    mixed_out = jnp.stack(outs_mixed)[:, None]
    grad_tokens = jnp.stack(outs_grad)[:, None]
    return (
        mixed_out,
        grad_tokens,
        layer_totals[0],
        layer_totals[1],
        layer_totals[2],
        layer_totals[3],
        layer_totals[4],
        layer_totals[5],
        layer_totals[6],
        layer_totals[7],
        layer_totals[8],
        expert_totals[0],
        expert_totals[1],
        expert_totals[2],
    )


def solution(mesh):
    placed = (
        P(None, ("dp", "expert", "shard"), None, None),
        P(None, ("dp", "expert", "shard"), None, None),
        P(None, ("dp", "expert", "shard")),
        P(None, ("dp", "expert", "shard"), None, None),
        P("shard", None),
        P("shard", None),
        P("shard", None),
        P("shard", None),
        P("shard", None),
        P("shard"),
        P("shard"),
        P("shard"),
        P("shard"),
        P(("expert", "shard"), None, "dp"),
        P(("expert", "shard"), None, "dp"),
        P(("expert", "shard"), "dp", None),
    )
    sizes = (mesh.shape["dp"], mesh.shape["expert"], mesh.shape["shard"])
    return jax.shard_map(
        gathered if sizes == (2, 4, 4) else exchanged,
        mesh=mesh,
        in_specs=placed,
        out_specs=(
            P(None, ("dp", "expert", "shard"), None, None),
            P(None, ("dp", "expert", "shard"), None, None),
            P("shard", None),
            P("shard", None),
            P("shard", None),
            P("shard", None),
            P("shard", None),
            P("shard"),
            P("shard"),
            P("shard"),
            P("shard"),
            P(("expert", "shard"), None, "dp"),
            P(("expert", "shard"), None, "dp"),
            P(("expert", "shard"), "dp", None),
        ),
        check_vma=False,
    )
```

```python
import functools

import jax
import jax.numpy as jnp
import numpy as np
from jax import lax
from jax.experimental import pallas as pl
from jax.experimental.pallas import tpu as pltpu
from jax.sharding import PartitionSpec as P

HEADS = 16
HDIM = 128


EPSILON = 1e-05


def matmul(left, right):
    return jnp.dot(left, right, preferred_element_type=jnp.float32)


def times_transposed(left, right):
    return lax.dot_general(
        left, right, (((1,), (1,)), ((), ())), preferred_element_type=jnp.float32
    )


def transposed_times(left, right):
    return lax.dot_general(
        left, right, (((0,), (0,)), ((), ())), preferred_element_type=jnp.float32
    )


def rms_norm(values, gain_vec):
    factor = lax.rsqrt(jnp.mean(values * values, axis=-1, keepdims=True) + EPSILON)
    return values * factor * gain_vec


def norm_back(values, gain_vec, incoming):
    factor = lax.rsqrt(jnp.mean(values * values, axis=-1, keepdims=True) + EPSILON)
    unit_rows = values * factor
    weighted = incoming * gain_vec
    d_values = factor * (
        weighted - unit_rows * jnp.mean(weighted * unit_rows, axis=-1, keepdims=True)
    )
    return (d_values, jnp.sum(incoming * unit_rows, axis=0))


def rope_tables(seq_count, head_size):
    half_dim = head_size // 2
    freqs = 10000.0 ** (-2.0 * jnp.arange(half_dim).astype(jnp.float32) / head_size)
    angles = jnp.arange(seq_count).astype(jnp.float32)[:, None] * freqs[None, :]
    cosine_table = jnp.concatenate([jnp.cos(angles), jnp.cos(angles)], axis=-1)
    sine_table = jnp.concatenate([jnp.sin(angles), jnp.sin(angles)], axis=-1)
    return (cosine_table, sine_table)


def rotate(head_rows, cosine_table, sine_table):
    half_dim = head_rows.shape[-1] // 2
    turned = jnp.concatenate([-head_rows[..., half_dim:], head_rows[..., :half_dim]], axis=-1)
    return head_rows * cosine_table[:, None, :] + turned * sine_table[:, None, :]


def rotate_back(incoming, cosine_table, sine_table):
    half_dim = incoming.shape[-1] // 2
    moved_part = incoming * sine_table[:, None, :]
    turned = jnp.concatenate([moved_part[..., half_dim:], -moved_part[..., :half_dim]], axis=-1)
    return incoming * cosine_table[:, None, :] + turned


def softmax_rows(scores):
    shifted = jnp.exp(scores - jnp.max(scores, axis=-1, keepdims=True))
    return shifted / jnp.sum(shifted, axis=-1, keepdims=True)


MESH_ID = pl.DeviceIdType.MESH
EXTRA = 128
ANY = pl.BlockSpec(memory_space=pl.ANY)


def place():
    return lax.axis_index("dp"), lax.axis_index("expert"), lax.axis_index("shard")


def x_of(e):
    return e + 1 - 2 * lax.rem(e, 2)


def y_of(e):
    return lax.rem(e + 2, 4)


def greet(peers):
    barrier = pltpu.get_barrier_semaphore()
    for peer in peers:
        pl.semaphore_signal(barrier, inc=1, device_id=peer, device_id_type=MESH_ID)
    pl.semaphore_wait(barrier, len(peers))


class Copies:
    def __init__(self):
        self.started = []

    def send(self, src, dst, send_sem, recv_sem, device, when=None):
        copy = pltpu.make_async_remote_copy(
            src_ref=src,
            dst_ref=dst,
            send_sem=send_sem,
            recv_sem=recv_sem,
            device_id=device,
            device_id_type=MESH_ID,
        )
        if when is None:
            copy.start()
        else:
            pl.when(when)(copy.start)
        self.started.append((copy, when))

    def drain(self):
        for copy, when in self.started:
            if when is None:
                copy.wait_send()
            else:
                pl.when(when)(copy.wait_send)


def arrived(ref, sem, other):
    pltpu.make_async_remote_copy(
        src_ref=ref,
        dst_ref=ref,
        send_sem=sem,
        recv_sem=sem,
        device_id=other,
        device_id_type=MESH_ID,
    ).wait_recv()


class SemPool:
    def __init__(self, ref):
        self.ref = ref
        self.used = 0

    def take(self):
        self.used += 1
        assert self.used <= self.ref.shape[0]
        return self.ref.at[self.used - 1]


class Item:
    def __init__(self, own, dst, recv, skip=False, cross=None, cross_recv=None):
        self.own, self.dst, self.recv = own, dst, recv
        self.skip, self.cross, self.cross_recv = skip, cross, cross_recv


class Gather:
    def __init__(self, item, copies, pool):
        self.item, self.copies, self.pool = item, copies, pool
        self.dp, self.e, self.z = place()
        self.px, self.py = x_of(self.e), y_of(self.e)
        self.diag = x_of(self.py)
        self.firsts, self.seconds = (self.px, self.py), (self.py, self.px)

    def send(self, h, ee, zz, target, zt, when, own=False):
        item = self.item
        ref = item.dst(zz, ee, h)
        self.copies.send(item.own(h) if own else ref, ref, self.pool.take(), item.recv.at[h, ee * 4 + zz],
                         (self.dp, target, zt), when)

    def across(self, h, ee, zz, when):
        item = self.item
        if item.cross is not None:
            ref = item.dst(zz, ee, h)
            self.copies.send(ref, ref, self.pool.take(), item.cross_recv.at[h, ee * 4 + zz],
                             (1 - self.dp, self.e, self.z), when)

    def wait(self, h, ee, zz, when):
        def body():
            arrived(self.item.dst(zz, ee, h), self.item.recv.at[h, ee * 4 + zz], (self.dp, self.e, self.z))
        if when is None:
            body()
        else:
            pl.when(when)(body)

    def steps(self, k):
        if k == 0:
            return [(self.z, None, 1)]
        out = []
        for sign in (-1, 1):
            zz = self.z + sign * k
            out.append((zz, (zz >= 0) & (zz <= 3), sign))
        return out

    def begin_z(self):
        for h in (0, 1):
            for sign in (-1, 1):
                nxt = self.z + sign
                self.send(h, self.e, self.z, self.e, nxt, (nxt >= 0) & (nxt <= 3), own=True)

    def begin_plane(self):
        for h in (0, 1):
            for target in (self.firsts[h], self.seconds[h]):
                self.send(h, self.e, self.z, target, self.z, None, own=True)

    def own_stage(self, k):
        for zz, valid, sign in self.steps(k):
            nxt = self.z - sign
            for h in (0, 1):
                self.wait(h, self.e, zz, valid)
                self.send(h, self.e, zz, self.e, nxt, valid & (nxt >= 0) & (nxt <= 3))
                self.send(h, self.e, zz, self.firsts[h], self.z, valid)
                self.send(h, self.e, zz, self.seconds[h], self.z, valid)
                self.across(h, self.e, zz, valid)

    def relay_stage(self, k):
        if k == 0 and self.item.skip:
            return
        for zz, valid, _ in self.steps(k):
            for h in (0, 1):
                self.wait(h, self.firsts[h], zz, valid)
                self.send(h, self.firsts[h], zz, self.seconds[h], self.z, valid)
                self.across(h, self.firsts[h], zz, valid)

    def last_stage(self, k):
        if k == 0 and self.item.skip:
            return
        for zz, valid, _ in self.steps(k):
            for h in (0, 1):
                for ee in (self.seconds[h], self.diag):
                    self.wait(h, ee, zz, valid)
                    self.across(h, ee, zz, valid)

    def cross_stage(self):
        if self.item.cross is None:
            return
        for k in (1, 2, 3):
            for zz, valid, _ in self.steps(k):
                @pl.when(valid)
                def _(zz=zz):
                    for ee in range(4):
                        for h in (0, 1):
                            arrived(self.item.cross(zz, ee, h), self.item.cross_recv.at[h, ee * 4 + zz],
                                    (self.dp, self.e, self.z))

    def both_ways(self, h, ee, own=False):
        for sign in (-1, 1):
            nxt = self.z + sign
            self.send(h, ee, self.z, self.e, nxt, (nxt >= 0) & (nxt <= 3), own=own)

    def plane_relay(self):
        for h in (0, 1):
            self.wait(h, self.firsts[h], self.z, None)
            self.send(h, self.firsts[h], self.z, self.seconds[h], self.z, None)

    def line_begin(self, group):
        for h in (0, 1):
            if group == 0:
                self.both_ways(h, self.e, own=True)
                self.both_ways(h, self.firsts[h])
            else:
                for ee in (self.seconds[h], self.diag):
                    self.wait(h, ee, self.z, None)
                    self.both_ways(h, ee)

    def line_stage(self, k, group):
        for zz, valid, sign in self.steps(k):
            nxt = self.z - sign
            for h in (0, 1):
                for ee in ((self.e, self.firsts[h]), (self.seconds[h], self.diag))[group]:
                    self.wait(h, ee, zz, valid)
                    self.send(h, ee, zz, self.e, nxt, valid & (nxt >= 0) & (nxt <= 3))


class Plane:
    def __init__(self, own, all_rows, recv, send, relay, cross):
        self.own, self.all_rows, self.recv = own, all_rows, recv
        self.send, self.relay, self.cross = send, relay, cross
        self.dp, self.e, self.z = place()
        px, py = x_of(self.e), y_of(self.e)
        self.plane = (px, py, x_of(py))
        self.half = all_rows.shape[1] // 2

    def at(self, ref, h):
        return ref.at[pl.ds(h * self.half, self.half)]

    def copy(self, src, slot, h, send_sem, device):
        return pltpu.make_async_remote_copy(
            src_ref=src, dst_ref=self.at(self.all_rows.at[slot], h), send_sem=send_sem,
            recv_sem=self.recv.at[h, slot], device_id=device, device_id_type=MESH_ID)

    def first(self, n, h):
        target = (1 - self.dp, self.e, self.z) if n == 2 else (self.dp, self.plane[n], self.z)
        return self.copy(self.at(self.own, h), self.dp * 4 + self.e, h, self.send.at[n, h], target)

    def on(self, h):
        slot = self.dp * 4 + self.plane[h]
        return self.copy(self.at(self.all_rows.at[slot], h), slot, h, self.relay.at[h],
                         (self.dp, self.plane[1 - h], self.z))

    def over(self, n, h):
        slot = self.dp * 4 + self.plane[n]
        return self.copy(self.at(self.all_rows.at[slot], h), slot, h, self.cross.at[n, h],
                         (1 - self.dp, self.e, self.z))

    def wait(self, h, slot):
        arrived(self.at(self.all_rows.at[slot], h), self.recv.at[h, slot], (self.dp, self.e, self.z))

    def begin(self):
        for n in range(3):
            for h in (0, 1):
                self.first(n, h).start()

    def pass_on(self):
        for h in (0, 1):
            self.wait(h, self.dp * 4 + self.plane[h])
            self.on(h).start()
            self.over(h, h).start()

    def end(self):
        for h in (0, 1):
            self.wait(h, self.dp * 4 + self.plane[1 - h])
            self.over(1 - h, h).start()
        for h in (0, 1):
            self.wait(h, self.dp * 4 + self.plane[2])
            self.over(2, h).start()

    def end_cross(self):
        for ee in range(4):
            for h in (0, 1):
                self.wait(h, (1 - self.dp) * 4 + ee)

    def drain(self):
        for h in (0, 1):
            for n in range(3):
                self.first(n, h).wait_send()
                self.over(n, h).wait_send()
            self.on(h).wait_send()


def mates_of():
    dp, e, z = place()
    return [(lax.rem(dp + d // 4, 2), lax.rem(e + d % 4, 4), z) for d in range(1, 8)]


def columns_of(d, ee):
    return pl.ds(pl.multiple_of(ee * 512 + d * 256, 256), 256)


def as_column(row, count):
    return jnp.broadcast_to(row, (count, row.shape[1])).T


def as_row(column):
    return jnp.broadcast_to(column, (column.shape[0], 128)).T[0:1]


def chosen_experts(route_ids):
    lane = lax.broadcasted_iota(jnp.int32, (route_ids.shape[0], EXTRA), 1)
    found = route_ids[:, 0:1] == lane
    for r in range(1, route_ids.shape[1]):
        found = found | (route_ids[:, r:r + 1] == lane)
    return found


def allowed_keys(live_row):
    rows = live_row.shape[1]
    i = lax.broadcasted_iota(jnp.int32, (rows, rows), 0)
    j = lax.broadcasted_iota(jnp.int32, (rows, rows), 1)
    half = rows // 2
    return ((i < half) == (j < half)) & (j <= i) & (live_row > 0.5)


def front_kernel(
    tok, cot, live, route_ids, cosine, sine, route_in, gains_in, wq, wk, wv, wo, wg, wu, wd,
    q_raw, k_raw, q_low, k_low, v_low, squares, lives, mixed, hidden, ffn_in, router, small_rows, dy,
    rows_all, w_cols, w_out, wide_all, dy_all, wg_far, wu_far, wd_far,
    X, Wc, Wo, R, small, normed, mixed_cols, mixed_own, parts, sent, load_sem, store_sem, x_recv, x_send, x_relay, x_cross,
    recv_w, recv_o, cross_o, recv_a, recv_b, recv_r, recv_small, recv_far, recv_live, recv_sq, recv_mix,
    mate_send, send_sems,
):
    dp, e, z = place()
    px, py = x_of(e), y_of(e)
    me, far = (dp, e, z), (1 - dp, e, z)
    f32, bf = jnp.float32, jnp.bfloat16
    rows, width = tok.shape
    quarter = width // 4
    slot_z = e * 4 + z
    slot_me = dp * 4 + e
    mates = mates_of()
    own_cols = columns_of(dp, e)

    def local(src, dst, sem):
        return pltpu.make_async_copy(src, dst, sem)

    z_rows = pl.ds(pl.multiple_of(z * 512, 512), 512)
    loads = [local(ref.at[:, own_cols], Wc.at[m, z_rows], load_sem.at[m]) for m, ref in enumerate((wq, wk, wv))]
    loads.append(local(wo, Wo.at[z_rows], load_sem.at[3]))
    for load in loads:
        load.start()
    unit = (lax.broadcasted_iota(jnp.int32, (16, 16), 0) == lax.broadcasted_iota(jnp.int32, (16, 16), 1)).astype(bf)
    small[0:16] = times_transposed(unit, route_in[...]).astype(bf)
    small[16:] = gains_in[...]
    dy_live = jnp.where(as_column(live[0:1], rows)[:, :1] > 0.5, cot[...].astype(f32), 0.0)
    dy[...] = dy_live.astype(bf).reshape(dy.shape)
    greet([(dp, e, lax.rem(z + d, 4)) for d in (1, 2, 3)] + mates)
    copies, pool = Copies(), SemPool(send_sems)

    def to_mates(src, dst, recv_at, kind):
        for n, mate in enumerate(mates):
            copies.send(src(mate), dst, mate_send.at[kind, n], recv_at, mate)

    def cols_piece(zz, h):
        return Wc.at[:, pl.ds(pl.multiple_of(zz * 512 + h * 256, 256), 256), :]

    def cols_send(zz, h, sign, when):
        nxt = z + sign
        on = (nxt >= 0) & (nxt <= 3)
        copies.send(cols_piece(zz, h), cols_piece(zz, h), pool.take(), recv_w.at[h, zz], (dp, e, nxt),
                    on if when is None else on & when)

    def cols_stage(k):
        for sign in (-1, 1):
            zz = z + sign * k
            valid = (zz >= 0) & (zz <= 3)
            for h in (0, 1):
                @pl.when(valid)
                def _(zz=zz, h=h):
                    arrived(cols_piece(zz, h), recv_w.at[h, zz], me)
                cols_send(zz, h, -sign, valid)

    def out_piece(d):
        def at(zz, ee, h):
            return Wo.at[pl.ds(pl.multiple_of(zz * 512 + ee * 128 + d * 64 + h * 32, 32), 32), :]
        return at

    out_at = out_piece(dp)
    cuts = (32, 32)
    out_g = Gather(Item(lambda h: out_at(z, e, h), out_at, recv_o, skip=True, cross=out_piece(1 - dp),
                        cross_recv=cross_o), copies, pool)
    dy_a = Gather(Item(lambda h: dy.at[h, 0:cuts[h]], lambda zz, ee, h: dy_all.at[ee * 4 + zz, h, 0:cuts[h]], recv_a),
                  copies, pool)
    dy_b = Gather(Item(lambda h: dy.at[h, cuts[h]:64], lambda zz, ee, h: dy_all.at[ee * 4 + zz, h, cuts[h]:64], recv_b),
                  copies, pool)
    b_all = Gather(Item(lambda h: wide_all.at[slot_z, h], lambda zz, ee, h: wide_all.at[ee * 4 + zz, h], recv_r),
                   copies, pool)
    x_plane = Plane(normed, X, x_recv, x_send, x_relay, x_cross)

    for d in (1, 2, 3):
        copies.send(small, small_rows.at[z], pool.take(), recv_small.at[z], (dp, e, lax.rem(z + d, 4)))
    to_mates(lambda mate: live, lives.at[slot_me], recv_live.at[slot_me], 0)
    small_store = local(small, small_rows.at[z], store_sem.at[0])
    small_store.start()
    dy_store = local(dy, dy_all.at[slot_z], store_sem.at[1])
    dy_store.start()
    for load in loads:
        load.wait()
    for h in (0, 1):
        for sign in (-1, 1):
            cols_send(z, h, sign, None)
    small_store.wait()
    for d in (1, 2, 3):
        zz = lax.rem(z + d, 4)
        arrived(small_rows.at[zz], recv_small.at[zz], me)
    for zz in range(4):
        R[:, zz * quarter:(zz + 1) * quarter] = small_rows[zz]

    def gain(i):
        return R[16 + i:17 + i, :].astype(f32)

    def factor(values):
        return lax.rsqrt(jnp.mean(values * values, axis=1, keepdims=True) + EPSILON)

    x = tok[...].astype(f32)
    normed[...] = (x * factor(x) * gain(0)).astype(bf)
    x_plane.begin()
    x_keep = local(normed, X.at[slot_me], store_sem.at[2])
    x_keep.start()
    lives[slot_me] = live[...]
    dy_a.begin_plane()
    dy_b.begin_plane()
    cols_stage(1)
    out_g.begin_z()
    x_plane.pass_on()
    for i, (src, dst) in enumerate(((wg, wg_far), (wu, wu_far), (wd, wd_far))):
        copies.send(src, dst, pool.take(), recv_far.at[i], far)
    dy_a.relay_stage(0)
    dy_b.plane_relay()
    cols_stage(2)
    x_plane.end()
    out_g.own_stage(1)
    dy_a.begin_z()
    x_plane.end_cross()
    x_keep.wait()
    for n in range(7):
        od, oe, _ = mates[n]
        arrived(lives.at[od * 4 + oe], recv_live.at[od * 4 + oe], me)
    rows_store = local(X, rows_all, store_sem.at[3])
    rows_store.start()
    cols_stage(3)
    cols_store = local(Wc, w_cols, store_sem.at[5])
    cols_store.start()
    out_g.relay_stage(1)

    def project(g, _):
        at = pl.ds(g * 4, 4)
        block = X[at].reshape(4 * rows, width)
        for m, ref in enumerate((q_raw, k_raw)):
            ref[at] = jnp.dot(block, Wc[m], preferred_element_type=f32).reshape(4, rows, 256)
        v_low[at] = jnp.dot(block, Wc[2], preferred_element_type=f32).astype(bf).reshape(4, rows, 256)
        for i in range(4):
            for m, ref in enumerate((q_raw, k_raw)):
                values = ref[g * 4 + i]
                parts[slot_me, m, pl.ds(g * 4 + i, 1), :] = as_row(jnp.sum(values * values, axis=1, keepdims=True))
        return 0

    lax.fori_loop(0, 2, project, 0)
    to_mates(lambda mate: parts.at[slot_me], parts.at[slot_me], recv_sq.at[slot_me], 1)
    out_g.own_stage(2)
    dy_b.line_begin(0)
    for n in range(7):
        od, oe, _ = mates[n]
        arrived(parts.at[od * 4 + oe], recv_sq.at[od * 4 + oe], me)
    squares[...] = (((parts[0] + parts[1]) + (parts[2] + parts[3]))
                    + ((parts[4] + parts[5]) + (parts[6] + parts[7]))) * (1.0 / width)
    cos_t = jnp.concatenate([cosine[...]] * 2, axis=0)
    sin_t = jnp.concatenate([sine[...]] * 2, axis=0)

    def attend(d, _):
        allowed = allowed_keys(lives[d][0:1])
        for m, (raw, low) in enumerate(((q_raw, q_low), (k_raw, k_low))):
            scale = lax.rsqrt(as_column(squares[m, pl.ds(d, 1), :], HDIM) + EPSILON)
            for hh in range(2):
                cc = slice(hh * HDIM, (hh + 1) * HDIM)
                gains = R[18 + m:19 + m, pl.ds(pl.multiple_of(e * 512 + dp * 256 + hh * HDIM, HDIM), HDIM)].astype(f32)
                u = raw[d, :, cc] * scale * gains
                low[d, :, cc] = (u * cos_t + pltpu.roll(u, HDIM // 2, 1) * sin_t).astype(bf)
        for hh in range(2):
            cc = slice(hh * HDIM, (hh + 1) * HDIM)
            scores = times_transposed(q_low[d, :, cc], k_low[d, :, cc]) * (HDIM ** (-0.5))
            probs = softmax_rows(jnp.where(allowed, scores, -1e30))
            mixed_cols[d, :, cc] = jnp.dot(probs.astype(bf), v_low[d, :, cc], preferred_element_type=f32).astype(bf)
        return 0

    lax.fori_loop(0, 4, attend, 0)
    out_g.relay_stage(2)
    out_g.own_stage(3)
    dy_b.line_begin(1)
    lax.fori_loop(4, 8, attend, 0)
    to_mates(lambda mate: mixed_cols.at[mate[0] * 4 + mate[1]], mixed_own.at[:, own_cols], recv_mix.at[slot_me], 2)
    mixed_own[:, own_cols] = mixed_cols[slot_me]
    out_g.last_stage(1)
    out_g.relay_stage(3)
    dy_a.own_stage(1)
    for n in range(7):
        od, oe, _ = mates[n]
        arrived(mixed_own.at[:, columns_of(od, oe)], recv_mix.at[od * 4 + oe], me)
    mixed[...] = mixed_own[...]
    out_g.last_stage(2)
    dy_b.line_stage(1, 0)
    dy_a.relay_stage(1)
    out_g.last_stage(3)
    out_g.cross_stage()
    full_o = local(Wo, w_out, store_sem.at[4])
    full_o.start()

    def out_col(j, _):
        cc = pl.ds(pl.multiple_of(j * 512, 512), 512)
        hidden[:, cc] = tok[:, cc].astype(f32) + jnp.dot(mixed[...], Wo[:, cc], preferred_element_type=f32)
        return 0

    lax.fori_loop(0, 4, out_col, 0)
    h1 = hidden[...]
    b = (h1 * factor(h1) * gain(1)).astype(bf)
    ffn_in[...] = b
    lane = lax.broadcasted_iota(jnp.int32, (rows, EXTRA), 1)
    logits = jnp.where(lane < 16, times_transposed(b, R[...]), -1e30)
    picks = softmax_rows(logits)
    router[...] = picks
    gates = jnp.where(chosen_experts(route_ids[...]), picks, 0.0)
    high = gates.astype(bf).astype(f32)
    extra = high + pltpu.roll(gates - high, 16, 1)
    sent[:, :, :width] = b.reshape(2, rows // 2, width)
    sent[:, :, width:] = extra.astype(bf).reshape(2, rows // 2, EXTRA)
    keep = local(sent, wide_all.at[slot_z], store_sem.at[6])
    keep.start()
    keep.wait()
    b_all.begin_plane()
    b_all.begin_z()
    dy_a.own_stage(2)
    dy_b.line_stage(1, 1)
    dy_a.relay_stage(2)
    b_all.relay_stage(0)
    b_all.own_stage(1)
    dy_a.own_stage(3)
    dy_b.line_stage(2, 0)
    b_all.relay_stage(1)
    b_all.own_stage(2)
    dy_a.relay_stage(3)
    dy_b.line_stage(2, 1)
    b_all.relay_stage(2)
    b_all.own_stage(3)
    b_all.relay_stage(3)
    for group in (0, 1):
        dy_b.line_stage(3, group)
    for k in range(4):
        dy_a.last_stage(k)
    for k in range(4):
        b_all.last_stage(k)
    for i, dst in enumerate((wg_far, wu_far, wd_far)):
        arrived(dst, recv_far.at[i], me)
    copies.drain()
    x_plane.drain()
    for store in (dy_store, full_o, rows_store, cols_store):
        store.wait()


def front(tok, cot, live, route_ids, cosine, sine, route_in, gains_in, *weights):
    bf, f32 = jnp.bfloat16, jnp.float32
    dma = pltpu.SemaphoreType.DMA
    shape = jax.ShapeDtypeStruct
    vmem = pl.BlockSpec(memory_space=pltpu.VMEM)
    rows, width = tok.shape
    wg, wu, wd = weights[4:]
    return pl.pallas_call(
        front_kernel,
        out_shape=(
            shape((8, rows, 256), f32),
            shape((8, rows, 256), f32),
            shape((8, rows, 256), bf),
            shape((8, rows, 256), bf),
            shape((8, rows, 256), bf),
            shape((2, 8, rows), f32),
            shape((8, 8, rows), f32),
            shape((rows, width), bf),
            shape((rows, width), f32),
            shape((rows, width), bf),
            shape((rows, EXTRA), f32),
            shape((4, EXTRA, width // 4), bf),
            shape((2, rows // 2, width), bf),
            shape((8, rows, width), bf),
            shape((3, width, 256), bf),
            shape((width, width), bf),
            shape((16, 2, rows // 2, width + EXTRA), bf),
            shape((16, 2, rows // 2, width), bf),
            shape(wg.shape, bf),
            shape(wu.shape, bf),
            shape(wd.shape, bf),
        ),
        in_specs=[vmem] * 8 + [ANY] * 7,
        out_specs=(vmem,) * 13 + (ANY,) * 8,
        scratch_shapes=[
            pltpu.VMEM((8, rows, width), bf),
            pltpu.VMEM((3, width, 256), bf),
            pltpu.VMEM((width, width), bf),
            pltpu.VMEM((EXTRA, width), bf),
            pltpu.VMEM((EXTRA, width // 4), bf),
            pltpu.VMEM((rows, width), bf),
            pltpu.VMEM((8, rows, 256), bf),
            pltpu.VMEM((rows, width), bf),
            pltpu.VMEM((8, 2, 8, rows), f32),
            pltpu.VMEM((2, rows // 2, width + EXTRA), bf),
            dma((4,)),
            dma((7,)),
            dma((2, 8)),
            dma((3, 2)),
            dma((2,)),
            dma((3, 2)),
            dma((2, 4)),
            dma((2, 16)),
            dma((2, 16)),
            dma((2, 16)),
            dma((2, 16)),
            dma((2, 16)),
            dma((4,)),
            dma((3,)),
            dma((8,)),
            dma((8,)),
            dma((8,)),
            dma((3, 7)),
            dma((330,)),
        ],
        compiler_params=pltpu.CompilerParams(collective_id=0, has_side_effects=True, vmem_limit_bytes=62 * 2**20),
        name="attention_front",
    )(tok, cot, live, route_ids, cosine, sine, route_in, gains_in, *weights)


def times(left, right):
    return jnp.dot(left, right, preferred_element_type=jnp.float32)


def experts_kernel(
    wide, dy, wg, wu, wd, wgf, wuf, wdf,
    res, eg, eu, ed, part, a_buf, b_buf,
    c_buf, WG, WU, WD, rows_in, dy_rows, hidden, saved, acc, stage, addend, turned, column, far_out,
    w_sem, dy_sem, in_sem, part_sem, add_sem, col_sem, fin_sem, out_sem,
    a_sem, b_sem, c_sem, a_send, b_send, c_send, gu_send, gu_sem, dn_send, dn_sem, free_sem,
):
    dp, e, z = place()
    px, py = x_of(e), y_of(e)
    diag = x_of(y_of(e))
    me = (dp, e, z)
    far_core = (1 - dp, e, z)
    f32, bf = jnp.float32, jnp.bfloat16
    width = dy.shape[3]
    half_f = wg.shape[1]
    total_width = part.shape[3]

    def local(src, dst, sem):
        return pltpu.make_async_copy(src, dst, sem)

    def remote(src, dst, send_sem, recv_sem, device):
        return pltpu.make_async_remote_copy(
            src_ref=src, dst_ref=dst, send_sem=send_sem, recv_sem=recv_sem,
            device_id=device, device_id_type=MESH_ID)

    def column_of(c):
        return jnp.where(c == 0, diag, jnp.where(c == 1, py, jnp.where(c == 2, px, e)))

    def zed(i):
        return lax.rem(z + jnp.where(i == 0, 2, jnp.where(i == 1, 1, jnp.where(i == 2, 3, 0))), 4)

    def kind_of(s):
        return jnp.where(s < 2, 0, jnp.where(s < 4, 3, 1 + lax.rem(s, 2)))

    def zed_of(s, i):
        return zed(2 * jnp.where(s < 4, lax.rem(s, 2), (s - 4) // 2) + i)

    def slot_of(s, i):
        return column_of(kind_of(s)) * 4 + zed_of(s, i)

    def rows_load(s, i, buf):
        return local(wide.at[slot_of(s, i)], rows_in.at[buf, i], in_sem.at[buf, i])

    weights = [
        local(src, dst, w_sem.at[n])
        for n, (src, dst) in enumerate((
            (wg, WG.at[0]), (wu, WU.at[0]), (wd, WD.at[0]), (wgf, WG.at[1]), (wuf, WU.at[1]), (wdf, WD.at[1])))
    ]
    for i in range(2):
        rows_load(0, i, 0).start()
    weights[0].start()
    weights[1].start()
    def dy_load(s, i):
        return local(dy.at[slot_of(s, i)], dy_rows.at[slot_of(s, i)], dy_sem.at[s, i])

    for i in range(2):
        dy_load(0, i).start()
    for load in weights[2:]:
        load.start()
    for s in range(1, 8):
        for i in range(2):
            dy_load(s, i).start()
    greet([(dp, e, lax.rem(z + d, 4)) for d in (1, 2, 3)] + [(dp, px, z), (dp, py, z), far_core])

    def part_write(s, i):
        return local(stage.at[lax.rem(s, 2), i], part.at[slot_of(s, i)], part_sem.at[lax.rem(s, 2), i])

    def a_copy(h, g, slot, zz, target):
        return remote(part.at[slot, h], a_buf.at[h, g, zz], a_send.at[h, g, zz], a_sem.at[h, g, zz], (dp, target, z))

    def b_copy(h, slot, zz, target):
        return remote(part.at[slot, h], b_buf.at[h, zz], b_send.at[h, zz], b_sem.at[h, zz], (dp, target, z))

    def send_step(s):
        c = kind_of(s)
        for i in range(2):
            part_write(s, i).wait()
            zz = zed_of(s, i)

            @pl.when(c == 0)
            def _():
                a_copy(0, 0, diag * 4 + zz, zz, py).start()
                a_copy(1, 0, diag * 4 + zz, zz, px).start()

            @pl.when(c == 1)
            def _():
                a_copy(0, 1, py * 4 + zz, zz, py).start()
                b_copy(1, py * 4 + zz, zz, py).start()

            @pl.when(c == 2)
            def _():
                a_copy(1, 1, px * 4 + zz, zz, px).start()
                b_copy(0, px * 4 + zz, zz, px).start()

    def addend_load(s, i):
        h = jnp.where(kind_of(s) == 1, 1, 0)
        zz = zed_of(s, i)
        return local(a_buf.at[h, 0, zz], addend.at[i], add_sem.at[i])

    mine = e * 4 + z
    route_rows = turned
    lane = lax.broadcasted_iota(jnp.int32, (256, EXTRA), 1)
    at_high, at_low = lane == mine, lane == mine + 16

    weights[0].wait()
    weights[1].wait()

    def step(s, _):
        buf = lax.rem(s, 2)

        @pl.when(s + 1 < 8)
        def _():
            for i in range(2):
                rows_load(s + 1, i, 1 - buf).start()
        for i in range(2):
            rows_load(s, i, buf).wait()
            dy_load(s, i).wait()
        slots = [slot_of(s, i) for i in range(2)]
        extra = rows_in[buf, :, :, :, width:].reshape(256, EXTRA).astype(f32)
        gate = jnp.sum(jnp.where(at_high | at_low, extra, 0.0), axis=1, keepdims=True)

        def dy_step():
            return jnp.concatenate([dy_rows[slot].reshape(128, width) for slot in slots], axis=0)

        def put(ref, values, at):
            for i in range(2):
                ref[slots[i], :, pl.ds(pl.multiple_of(at, half_f), half_f)] = values[i * 128:(i + 1) * 128]

        dy_route = (gate * dy_step().astype(f32)).astype(bf)
        route_rows[...] = dy_route
        acc[...] = jnp.zeros_like(acc)

        def half_step(n, _):
            @pl.when((s == 0) & (n == 1))
            def _():
                for load in weights[3:]:
                    load.wait()

            @pl.when((s > 1) & (n == 1))
            def _():
                send_step(s - 1)

            @pl.when((s >= 4) & (n == 1))
            def _():
                for i in range(2):
                    h = jnp.where(kind_of(s) == 1, 1, 0)
                    zz = zed_of(s, i)
                    arrived(a_buf.at[h, 0, zz], a_sem.at[h, 0, zz], me)
                    addend_load(s, i).start()
            x = rows_in[buf, :, :, :, :width].reshape(256, width)
            gate_pre = times(x, WG[n])
            up_value = times(x, WU[n])
            sigmoid_gate = jax.nn.sigmoid(gate_pre)
            activated = gate_pre * sigmoid_gate
            inner = (activated * up_value).astype(bf)
            put(hidden, inner, n * half_f)

            @pl.when((s == 0) & (n == 0))
            def _():
                weights[2].wait()
            d_inner = times_transposed(route_rows[...], WD[n])
            d_gate = (d_inner * up_value * (sigmoid_gate + gate_pre * sigmoid_gate * (1.0 - sigmoid_gate))).astype(bf)
            d_up = (d_inner * activated).astype(bf)
            put(saved, d_gate, 2 * n * half_f)
            put(saved, d_up, (2 * n + 1) * half_f)
            acc[0] += times(inner, WD[n])
            acc[1] += times_transposed(d_gate, WG[n]) + times_transposed(d_up, WU[n])
            return 0

        lax.fori_loop(0, 2, half_step, 0)
        y_low = acc[0].astype(bf).astype(f32)
        d_own = jnp.sum(y_low * dy_step().astype(f32), axis=1, keepdims=True)
        high = d_own.astype(bf).astype(f32)
        tail = jnp.where(at_high, high, jnp.where(at_low, d_own - high, 0.0)).astype(bf)

        def lay(values):
            return values.reshape(2, 2, 64, values.shape[1])

        stage[buf, :, :, :, :width] = lay((gate * y_low).astype(bf))
        stage[buf, :, :, :, width:width + EXTRA] = lay(tail)
        stage[buf, :, :, :, width + EXTRA:] = lay(acc[1].astype(bf))
        for i in range(2):
            dy_rows[slots[i]] = route_rows[i * 128:(i + 1) * 128].reshape(2, 64, width)

        @pl.when(s >= 4)
        def _():
            h = jnp.where(kind_of(s) == 1, 1, 0)
            for i in range(2):
                addend_load(s, i).wait()
                stage[buf, i, h] = (stage[buf, i, h].astype(f32) + addend[i].astype(f32)).astype(bf)
        for i in range(2):
            part_write(s, i).start()

        @pl.when(s == 0)
        def _():
            send_step(s)
        return 0

    lax.fori_loop(0, 8, step, 0)
    pl.semaphore_signal(free_sem, inc=1, device_id=far_core, device_id_type=MESH_ID)
    send_step(7)

    def finish_loads(k):
        zz = zed(k)
        return (local(part.at[e * 4 + zz], stage.at[0, 0], fin_sem.at[0]),
                local(a_buf.at[:, 1, zz], stage.at[0, 1], fin_sem.at[1]),
                local(b_buf.at[:, zz], stage.at[1, 0], fin_sem.at[2]))

    def begin(k):
        zz = zed(k)
        for h in range(2):
            arrived(a_buf.at[h, 1, zz], a_sem.at[h, 1, zz], me)
            arrived(b_buf.at[h, zz], b_sem.at[h, zz], me)
        for load in finish_loads(k):
            load.start()

    def result_write(k):
        return local(stage.at[1, 1], part.at[e * 4 + zed(k)], fin_sem.at[3])

    def c_copy(k):
        zz = zed(k)
        there = (0, 2, 1)[k]
        return remote(part.at[e * 4 + zz], c_buf.at[there], c_send.at[k], c_sem.at[there], (dp, e, zz))

    def close(k):
        for load in finish_loads(k):
            load.wait()
        for h in range(2):
            total = (stage[0, 0, h].astype(f32) + stage[0, 1, h].astype(f32)) + stage[1, 0, h].astype(f32)
            if k < 3:
                stage[1, 1, h] = total.astype(bf)
            else:
                res[h] = total
        if k < 3:
            result_write(k).start()

    def fire(k):
        result_write(k).wait()
        c_copy(k).start()

    def turn_hidden(n):
        turned[...] = hidden[:, :, pl.ds(pl.multiple_of(n * 256, 256), 256)].reshape(2048, 256).T

    def down_block(dst):
        def col(j, _):
            cc = pl.ds(pl.multiple_of(j * 512, 512), 512)
            dst(cc, times(turned[...], dy_rows[:, :, :, cc].reshape(2048, 512)))
            return 0
        lax.fori_loop(0, 4, col, 0)

    def column_load(n):
        return local(wide.at[:, :, :, pl.ds(pl.multiple_of(n * 256, 256), 256)], column.at[lax.rem(n, 2)],
                     col_sem.at[lax.rem(n, 2)])

    def down_send(n):
        return remote(far_out.at[n], WD.at[1, pl.ds(n * 256, 256)], dn_send.at[n], dn_sem.at[n], far_core)

    column_load(0).start()
    for n in range(2):
        turn_hidden(2 + n)

        def to_far(cc, values, n=n):
            far_out[n, :, cc] = values.astype(bf)
        down_block(to_far)
        if n == 0:
            pl.semaphore_wait(free_sem, 1)
        down_send(n).start()

    def row_block(n):
        return pl.ds(pl.multiple_of(n * 256, 256), 256)

    def gu_copy(n, w):
        buf = lax.rem(n, 2)
        return remote(far_out.at[buf, :, w * 512:(w + 1) * 512], WG.at[w, row_block(n)],
                      gu_send.at[buf, w], gu_sem.at[n, w], far_core)

    def gu_out(n, w):
        buf = lax.rem(n, 2)
        return local(acc.at[buf, :, w * 512:(w + 1) * 512], (eg, eu)[w].at[row_block(n)], out_sem.at[buf, w])

    def settle(n):
        buf = lax.rem(n, 2)
        for w in range(2):
            arrived(WG.at[w, row_block(n)], gu_sem.at[n, w], me)
            acc[buf, :, w * 512:(w + 1) * 512] += WG[w, row_block(n)].astype(f32)
            gu_out(n, w).start()

    def gate_up(n, _):
        buf = lax.rem(n, 2)

        @pl.when(n + 1 < 8)
        def _():
            column_load(n + 1).start()
        column_load(n).wait()
        turned[...] = column[buf].reshape(2048, 256).T

        @pl.when(n < 2)
        def _():
            for k in range(2):
                @pl.when(n == k)
                def _(k=k):
                    down_send(k).wait_send()

        @pl.when(n >= 2)
        def _():
            for w in range(2):
                gu_copy(n - 2, w).wait_send()
                gu_out(n - 2, w).wait()

        def far_col(j, _):
            cc = pl.ds(pl.multiple_of(j * 512, 512), 512)
            src = pl.ds(pl.multiple_of(1024 + j * 512, 512), 512)
            far_out[buf, :, cc] = times(turned[...], saved[:, :, src].reshape(2048, 512)).astype(bf)
            return 0

        def near_col(j, _):
            cc = pl.ds(pl.multiple_of(j * 512, 512), 512)
            acc[buf, :, cc] = times(turned[...], saved[:, :, cc].reshape(2048, 512))
            return 0
        lax.fori_loop(0, 2, far_col, 0)
        for w in range(2):
            gu_copy(n, w).start()
        lax.fori_loop(0, 2, near_col, 0)

        @pl.when(n > 0)
        def _():
            settle(n - 1)
        def now(k):
            close(k)
            fire(k)

        for at, act in ((1, lambda: begin(0)), (2, lambda: now(0)), (4, lambda: begin(1)), (5, lambda: now(1))):
            pl.when(n == at)(act)
        return 0

    lax.fori_loop(0, 8, gate_up, 0)
    settle(7)
    for n in (6, 7):
        for w in range(2):
            gu_copy(n, w).wait_send()
            gu_out(n, w).wait()

    def down_out(n):
        return local(acc.at[n], ed.at[pl.ds(n * 256, 256)], out_sem.at[n, 0])

    for n in range(2):
        turn_hidden(n)

        def keep(cc, values, n=n):
            acc[n, :, cc] = values
        down_block(keep)
        arrived(WD.at[1, pl.ds(n * 256, 256)], dn_sem.at[n], me)
        acc[n] += WD[1, pl.ds(n * 256, 256)].astype(f32)
        down_out(n).start()
    begin(2)
    close(2)
    fire(2)
    begin(3)
    close(3)
    for k in range(3):
        arrived(c_buf.at[k], c_sem.at[k], me)
        for h in range(2):
            res[h] += c_buf[k, h].astype(f32)
    for n in range(2):
        down_out(n).wait()
    for k in range(3):
        c_copy(k).wait_send()

    def drain(zz, _):
        a_copy(0, 0, diag * 4 + zz, zz, py).wait_send()
        a_copy(1, 0, diag * 4 + zz, zz, px).wait_send()
        a_copy(0, 1, py * 4 + zz, zz, py).wait_send()
        b_copy(1, py * 4 + zz, zz, py).wait_send()
        a_copy(1, 1, px * 4 + zz, zz, px).wait_send()
        b_copy(0, px * 4 + zz, zz, px).wait_send()
        return 0
    lax.fori_loop(0, 4, drain, 0)


def experts(wide, dy, near, far):
    dma = pltpu.SemaphoreType.DMA
    bf, f32 = jnp.bfloat16, jnp.float32
    wg, wu, wd = near
    width, half_f = wg.shape
    rows = wide.shape[2]
    total_width = 2 * width + EXTRA
    shape = jax.ShapeDtypeStruct
    every = 16 * 2 * rows
    outs = pl.pallas_call(
        experts_kernel,
        out_shape=(
            shape((2, rows, total_width), f32),
            shape((width, half_f), f32),
            shape((width, half_f), f32),
            shape((half_f, width), f32),
            shape((16, 2, rows, total_width), bf),
            shape((2, 2, 4, rows, total_width), bf),
            shape((2, 4, rows, total_width), bf),
        ),
        in_specs=[ANY] * 8,
        out_specs=(pl.BlockSpec(memory_space=pltpu.VMEM),) + (ANY,) * 6,
        scratch_shapes=[
            pltpu.VMEM((3, 2, rows, total_width), bf),
            pltpu.VMEM((2, width, half_f), bf),
            pltpu.VMEM((2, width, half_f), bf),
            pltpu.VMEM((2, half_f, width), bf),
            pltpu.VMEM((2, 2, 2, rows, width + EXTRA), bf),
            pltpu.VMEM((16, 2, rows, width), bf),
            pltpu.VMEM((16, 2 * rows, 2 * half_f), bf),
            pltpu.VMEM((16, 2 * rows, 4 * half_f), bf),
            pltpu.VMEM((2, 256, width), f32),
            pltpu.VMEM((2, 2, 2, rows, total_width), bf),
            pltpu.VMEM((2, rows, total_width), bf),
            pltpu.VMEM((256, every), bf),
            pltpu.VMEM((2, 16, 2, rows, 256), bf),
            pltpu.VMEM((2, 256, width), bf),
            dma((6,)),
            dma((8, 2)),
            dma((2, 2)),
            dma((2, 2)),
            dma((2,)),
            dma((2,)),
            dma((4,)),
            dma((2, 2)),
            dma((2, 2, 4)),
            dma((2, 4)),
            dma((4,)),
            dma((2, 2, 4)),
            dma((2, 4)),
            dma((3,)),
            dma((2, 2)),
            dma((8, 2)),
            dma((2,)),
            dma((2,)),
            pltpu.SemaphoreType.REGULAR,
        ],
        compiler_params=pltpu.CompilerParams(collective_id=2, has_side_effects=True, vmem_limit_bytes=67043328),
        name="owned_expert",
    )(wide, dy, *near, *far)
    return outs[:4]


def back_kernel(
    sums, tok, route_ids, cosine, sine, dy, mixed, q_raw, k_raw, q_low, k_low, v_low, squares, lives, hidden, ffn_in,
    router, small_rows, rows_all, w_cols, w_out,
    mixed_out, grad_tokens, out, small_out,
    Wo, Wc, R, d_hidden, d_heads, DH, d_mix, g_q, g_k, parts, means, X, D, turned, G, own_sum, hop, send_buf, mine,
    far_rows, home_rows, small, s_z, s_all,
    w_sem, load_sem, x_recv, x_send, x_relay, x_cross, d_sem, d_send, h_sem, h_send, q_sem, q_send,
    hop_sem, hop_send, f_sem, f_send, r_sem, r_send, sz_sem, sz_send, sa_sem, sa_send,
    g_sem, g_send, g_pass, g_far, out_sem,
):
    dp, e, z = place()
    px, py = x_of(e), y_of(e)
    diag = x_of(py)
    plane = (px, py, diag)
    me, far = (dp, e, z), (1 - dp, e, z)
    f32, bf = jnp.float32, jnp.bfloat16
    rows, width = tok.shape
    quarter = width // 4
    slot_me = dp * 4 + e
    zs = [lax.rem(z + d, 4) for d in range(4)]
    mates = mates_of()
    own_cols = columns_of(dp, e)

    def local(src, dst, sem):
        return pltpu.make_async_copy(src, dst, sem)

    def remote(src, dst, send_sem, recv_sem, device):
        return pltpu.make_async_remote_copy(
            src_ref=src, dst_ref=dst, send_sem=send_sem, recv_sem=recv_sem,
            device_id=device, device_id_type=MESH_ID)

    load_out = local(w_out, Wo, w_sem.at[0])
    load_cols = local(w_cols, Wc, w_sem.at[1])
    load_rows = local(rows_all, X.at[0], load_sem.at[0])
    load_mixed = local(mixed, X.at[1, slot_me], load_sem.at[1])
    for load in (load_out, load_mixed, load_cols, load_rows):
        load.start()
    greet([(dp, e, zz) for zz in zs[1:]] + mates)
    m_plane = Plane(mixed, X.at[1], x_recv, x_send, x_relay, x_cross)
    m_plane.begin()

    def d_copy(n):
        od, oe, _ = mates[n]
        return remote(d_mix.at[:, columns_of(od, oe)], D.at[3, slot_me], d_send.at[n], d_sem.at[slot_me], mates[n])

    def h_copy(n):
        od, oe, _ = mates[n]
        return remote(d_heads.at[:, columns_of(od, oe)], DH.at[slot_me], h_send.at[n], h_sem.at[slot_me], mates[n])

    def q_copy(n):
        return remote(parts.at[slot_me], parts.at[slot_me], q_send.at[n], q_sem.at[slot_me], mates[n])

    def from_mates(ref, sem):
        for n in range(7):
            od, oe, _ = mates[n]
            arrived(ref.at[od * 4 + oe], sem.at[od * 4 + oe], me)

    def compute(m, i, buf):
        turned[...] = D[m].reshape(8 * rows, 256).T

        def block(zz, _):
            at = pl.ds(pl.multiple_of(zz * 512, 512), 512)
            G[buf, zz] = jnp.dot(turned[...], X[i, :, :, at].reshape(8 * rows, 512), preferred_element_type=f32)
            return 0
        lax.fori_loop(0, 4, block, 0)
        own_sum[m] = G[buf, z]

    middle = (z == 1) | (z == 2)
    lower = z < 2
    targets = (jnp.where(lower, 3, 0), jnp.where(lower, 2, 1), z + 1 - 2 * lax.rem(z, 2))

    def hop_copy(m, j):
        zt = targets[j]
        up = zt > z
        there = jnp.where(zt == z - 1, 4, zt)
        return remote(send_buf.at[m, j], hop.at[m, there], hop_send.at[m, j], hop_sem.at[m, there],
                      (dp, e, jnp.where(up, z + 1, z - 1)))

    def pass_on(m, buf):
        for j in range(3):
            zt = targets[j]

            @pl.when(middle)
            def _():
                arrived(hop.at[m, zt], hop_sem.at[m, zt], me)
                send_buf[m, j] = (G[buf, zt] + hop[m, zt].astype(f32)).astype(bf)

            @pl.when(jnp.logical_not(middle))
            def _():
                send_buf[m, j] = G[buf, zt].astype(bf)
            hop_copy(m, j).start()

    def out_at(m, d, ee, h):
        return out.at[m, pl.ds(h * 256, 256), columns_of(d, ee)]

    def g_copy(m, n, h):
        return remote(mine.at[m, pl.ds(h * 256, 256)], out_at(m, dp, e, h), g_send.at[m, n, h],
                      g_sem.at[m, h, slot_me], far if n == 2 else (dp, plane[n], z))

    def g_relay(m, h):
        ref = out_at(m, dp, plane[h], h)
        return remote(ref, ref, g_pass.at[m, h], g_sem.at[m, h, dp * 4 + plane[h]], (dp, plane[1 - h], z))

    def g_onward(m, n, h):
        ref = out_at(m, dp, plane[n], h)
        return remote(ref, ref, g_far.at[m, n, h], g_sem.at[m, h, dp * 4 + plane[n]], far)

    def wait_g(m, h, d, ee):
        arrived(out_at(m, d, ee, h), g_sem.at[m, h, d * 4 + ee], me)

    def keep(m):
        return local(mine.at[m], out.at[m, :, own_cols], out_sem.at[m])

    def finish(m):
        @pl.when(z > 0)
        def _():
            arrived(hop.at[m, z], hop_sem.at[m, z], me)
            own_sum[m] += hop[m, z].astype(f32)

        @pl.when(z < 3)
        def _():
            arrived(hop.at[m, 4], hop_sem.at[m, 4], me)
            own_sum[m] += hop[m, 4].astype(f32)
        mine[m] = own_sum[m].T.astype(bf)
        for h in (0, 1):
            for n in range(3):
                g_copy(m, n, h).start()
        keep(m).start()

    def relay_out(m):
        for h in (0, 1):
            wait_g(m, h, dp, plane[h])
            g_relay(m, h).start()
            g_onward(m, h, h).start()

    def end_out(m):
        for h in (0, 1):
            wait_g(m, h, dp, plane[1 - h])
            g_onward(m, 1 - h, h).start()
        for h in (0, 1):
            wait_g(m, h, dp, diag)
            g_onward(m, 2, h).start()

    for zz in range(4):
        R[:, zz * quarter:(zz + 1) * quarter] = small_rows[zz]

    def gain(i):
        return R[16 + i:17 + i, :].astype(f32)

    def norm_grad(values, gain_vec, incoming):
        factor = lax.rsqrt(jnp.mean(values * values, axis=1, keepdims=True) + EPSILON)
        unit = values * factor
        weighted = incoming * gain_vec
        back_values = factor * (weighted - unit * jnp.mean(weighted * unit, axis=1, keepdims=True))
        return back_values, jnp.sum(incoming * unit, axis=0, keepdims=True)

    def put_small(at, count, values):
        for zz in range(4):
            small[zz, at:at + count] = values[:, zz * quarter:(zz + 1) * quarter]

    for zz in range(4):
        small[zz] = jnp.zeros(small.shape[1:], f32)
    mixed_out[...] = (hidden[...] + sums[:, :width]).astype(bf)
    extra = sums[:, width:width + EXTRA]
    d_gates = extra + pltpu.roll(extra, EXTRA - 16, 1)
    picks = router[...]
    d_router = jnp.where(chosen_experts(route_ids[...]), d_gates, 0.0)
    d_logits = (picks * (d_router - jnp.sum(picks * d_router, axis=1, keepdims=True))).astype(bf)
    put_small(0, 16, jnp.dot(d_logits.T, ffn_in[...], preferred_element_type=f32)[:16])
    d_ffn = sums[:, width + EXTRA:] + jnp.dot(d_logits, R[...], preferred_element_type=f32)
    back_values, gain_grad = norm_grad(hidden[...], gain(1), d_ffn)
    put_small(17, 1, gain_grad)
    total = dy[...].astype(f32) + back_values
    d_hidden[...] = total
    d_mix[...] = total.astype(bf)
    load_out.wait()

    def heads_back(j, _):
        at = pl.ds(pl.multiple_of(j * 512, 512), 512)
        d_heads[:, at] = times_transposed(d_mix[...], Wo[at, :]).astype(bf)
        return 0

    lax.fori_loop(0, 4, heads_back, 0)
    for n in range(7):
        h_copy(n).start()
    for n in range(7):
        d_copy(n).start()
    DH[slot_me] = d_heads[:, own_cols]
    D[3, slot_me] = d_mix[:, own_cols]
    m_plane.pass_on()
    from_mates(DH, h_sem)

    cos_t = jnp.concatenate([cosine[...]] * 2, axis=0)
    sin_t = jnp.concatenate([sine[...]] * 2, axis=0)
    scale = HDIM ** (-0.5)

    def heads(d, grads):
        allowed = allowed_keys(lives[d][0:1])
        pieces = []
        for hh in range(2):
            cc = slice(hh * HDIM, (hh + 1) * HDIM)
            q, k, v, dh = q_low[d, :, cc], k_low[d, :, cc], v_low[d, :, cc], DH[d, :, cc]
            probs = softmax_rows(jnp.where(allowed, times_transposed(q, k) * scale, -1e30))
            d_probs = times_transposed(dh, v)
            D[2, d, :, cc] = jnp.dot(probs.astype(bf).T, dh, preferred_element_type=f32).astype(bf)
            d_scores = (probs * (d_probs - jnp.sum(probs * d_probs, axis=1, keepdims=True))).astype(bf)
            for z_in in (jnp.dot(d_scores, k, preferred_element_type=f32) * scale,
                         jnp.dot(d_scores.T, q, preferred_element_type=f32) * scale):
                pieces.append(z_in * cos_t - pltpu.roll(z_in, HDIM // 2, 1) * sin_t)
        outs = []
        for m, (raw, ref) in enumerate(((q_raw, g_q), (k_raw, g_k))):
            incoming = jnp.concatenate([pieces[m], pieces[2 + m]], axis=1)
            ref[d] = incoming
            factor = lax.rsqrt(as_column(squares[m, pl.ds(d, 1), :], 256) + EPSILON)
            unit = raw[d] * factor
            gains = R[18 + m:19 + m, own_cols].astype(f32)
            through = incoming * unit
            parts[slot_me, m, pl.ds(d, 1), :] = as_row(jnp.sum(through * gains, axis=1, keepdims=True))
            outs.append(grads[m] + jnp.sum(through, axis=0, keepdims=True))
        return tuple(outs)

    none = jnp.zeros((1, 256), f32)
    gain_grads = lax.fori_loop(0, 8, heads, (none, none))
    for n in range(7):
        q_copy(n).start()
    for m in range(2):
        small[e, 18 + m:19 + m, pl.ds(pl.multiple_of(dp * 256, 256), 256)] = gain_grads[m]
    m_plane.end()
    from_mates(D.at[3], d_sem)
    m_plane.end_cross()
    load_mixed.wait()
    compute(3, 1, 0)
    pass_on(3, 0)
    load_rows.wait()
    compute(2, 0, 1)
    from_mates(parts, q_sem)
    means[...] = (((parts[0] + parts[1]) + (parts[2] + parts[3]))
                  + ((parts[4] + parts[5]) + (parts[6] + parts[7]))) * (1.0 / width)

    def raw_back(d, _):
        for m, (raw, ref) in enumerate(((q_raw, g_q), (k_raw, g_k))):
            factor = lax.rsqrt(as_column(squares[m, pl.ds(d, 1), :], 256) + EPSILON)
            mean = as_column(means[m, pl.ds(d, 1), :], 256)
            gains = R[18 + m:19 + m, own_cols].astype(f32)
            D[m, d] = (factor * (ref[d] * gains - raw[d] * factor * mean)).astype(bf)
        return 0

    lax.fori_loop(0, 8, raw_back, 0)
    pass_on(2, 1)

    load_cols.wait()

    def part_of(d):
        values = times_transposed(D[0, d], Wc[0]) + times_transposed(D[1, d], Wc[1])
        return values + times_transposed(D[2, d], Wc[2])

    def f_copy(ee):
        return remote(Wo.at[pl.ds(ee * rows, rows)], far_rows.at[ee], f_send.at[ee], f_sem.at[ee], far)

    def r_copy(n):
        return remote(home_rows.at[3 + n], home_rows.at[n], r_send.at[n], r_sem.at[n], (dp, plane[n], z))

    for ee in range(4):
        Wo[ee * rows:(ee + 1) * rows] = part_of((1 - dp) * 4 + ee).astype(bf)
        f_copy(ee).start()
    for n in range(3):
        values = part_of(dp * 4 + plane[n])
        arrived(far_rows.at[plane[n]], f_sem.at[plane[n]], me)
        home_rows[3 + n] = (values + far_rows[plane[n]].astype(f32)).astype(bf)
        r_copy(n).start()
    compute(0, 0, 0)
    pass_on(0, 0)
    values = part_of(slot_me)
    arrived(far_rows.at[e], f_sem.at[e], me)
    grad_tokens[...] = values + far_rows[e].astype(f32)
    finish(3)
    compute(1, 0, 1)
    pass_on(1, 1)
    for n in range(3):
        arrived(home_rows.at[n], r_sem.at[n], me)
    back_values, gain_grad = norm_grad(
        tok[...].astype(f32), gain(0),
        (grad_tokens[...] + home_rows[0].astype(f32)) + (home_rows[1].astype(f32) + home_rows[2].astype(f32)))
    put_small(16, 1, gain_grad)
    grad_tokens[...] = d_hidden[...] + back_values

    def sz_copy(d):
        return remote(small.at[zs[d]], s_z.at[z], sz_send.at[d - 1], sz_sem.at[z], (dp, e, zs[d]))

    def sa_copy(d):
        return remote(s_all.at[slot_me], s_all.at[slot_me], sa_send.at[d - 1], sa_sem.at[slot_me], mates[d - 1])

    for d in (1, 2, 3):
        sz_copy(d).start()
    finish(2)
    relay_out(3)
    for d in (1, 2, 3):
        arrived(s_z.at[zs[d]], sz_sem.at[zs[d]], me)
    s_all[slot_me] = (small[z] + s_z[zs[1]]) + (s_z[zs[2]] + s_z[zs[3]])
    for d in range(1, 8):
        sa_copy(d).start()
    finish(0)
    relay_out(2)
    end_out(3)
    finish(1)
    relay_out(0)
    end_out(2)
    from_mates(s_all, sa_sem)
    small_out[...] = (((s_all[0] + s_all[1]) + (s_all[2] + s_all[3]))
                      + ((s_all[4] + s_all[5]) + (s_all[6] + s_all[7])))
    relay_out(1)
    end_out(0)
    end_out(1)
    for m in range(4):
        for h in (0, 1):
            for ee in range(4):
                wait_g(m, h, 1 - dp, ee)
            for n in range(3):
                g_copy(m, n, h).wait_send()
                g_onward(m, n, h).wait_send()
            g_relay(m, h).wait_send()
        keep(m).wait()
        for j in range(3):
            hop_copy(m, j).wait_send()
    m_plane.drain()
    for n in range(7):
        d_copy(n).wait_send()
        h_copy(n).wait_send()
        q_copy(n).wait_send()
        sa_copy(n + 1).wait_send()
    for ee in range(4):
        f_copy(ee).wait_send()
    for n in range(3):
        r_copy(n).wait_send()
        sz_copy(n + 1).wait_send()


def back(*args):
    dma = pltpu.SemaphoreType.DMA
    bf, f32 = jnp.bfloat16, jnp.float32
    shape = jax.ShapeDtypeStruct
    vmem = pl.BlockSpec(memory_space=pltpu.VMEM)
    rows, width = args[1].shape
    small_shape = (4, 24, width // 4)
    return pl.pallas_call(
        back_kernel,
        out_shape=(
            shape((rows, width), bf),
            shape((rows, width), f32),
            shape((4, width // 4, width), bf),
            shape(small_shape[1:], f32),
        ),
        in_specs=[vmem] * 18 + [ANY] * 3,
        out_specs=(vmem, vmem, ANY, vmem),
        scratch_shapes=[
            pltpu.VMEM((width, width), bf),
            pltpu.VMEM((3, width, 256), bf),
            pltpu.VMEM((EXTRA, width), bf),
            pltpu.VMEM((rows, width), f32),
            pltpu.VMEM((rows, width), bf),
            pltpu.VMEM((8, rows, 256), bf),
            pltpu.VMEM((rows, width), bf),
            pltpu.VMEM((8, rows, 256), f32),
            pltpu.VMEM((8, rows, 256), f32),
            pltpu.VMEM((8, 2, 8, rows), f32),
            pltpu.VMEM((2, 8, rows), f32),
            pltpu.VMEM((2, 8, rows, width), bf),
            pltpu.VMEM((4, 8, rows, 256), bf),
            pltpu.VMEM((256, 8 * rows), bf),
            pltpu.VMEM((2, 4, 256, 512), f32),
            pltpu.VMEM((4, 256, 512), f32),
            pltpu.VMEM((4, 5, 256, 512), bf),
            pltpu.VMEM((4, 3, 256, 512), bf),
            pltpu.VMEM((4, 512, 256), bf),
            pltpu.VMEM((4, rows, width), bf),
            pltpu.VMEM((6, rows, width), bf),
            pltpu.VMEM(small_shape, f32),
            pltpu.VMEM(small_shape, f32),
            pltpu.VMEM((8,) + small_shape[1:], f32),
            dma((2,)),
            dma((2,)),
            dma((2, 8)),
            dma((3, 2)),
            dma((2,)),
            dma((3, 2)),
            dma((8,)),
            dma((7,)),
            dma((8,)),
            dma((7,)),
            dma((8,)),
            dma((7,)),
            dma((4, 5)),
            dma((4, 3)),
            dma((4,)),
            dma((4,)),
            dma((3,)),
            dma((3,)),
            dma((4,)),
            dma((3,)),
            dma((8,)),
            dma((7,)),
            dma((4, 2, 8)),
            dma((4, 3, 2)),
            dma((4, 2)),
            dma((4, 3, 2)),
            dma((4,)),
        ],
        compiler_params=pltpu.CompilerParams(collective_id=3, has_side_effects=True, vmem_limit_bytes=63 * 2**20),
        name="attention_back",
    )(*args)


def lay_out_kernel(sums, eg, eu, ed, mixed, grad_in, o_q, o_k, o_v, o_o, o_eg, o_eu, o_ed, o_mixed, o_grad):
    for m, ref in enumerate((o_q, o_k, o_v, o_o)):
        ref[...] = sums[m].astype(jnp.float32)
    for src, dst in ((eg, o_eg), (eu, o_eu), (ed, o_ed), (mixed, o_mixed), (grad_in, o_grad)):
        dst[...] = src[...]


def lay_out(sums, *arrays):
    steps = 8
    f32 = jnp.float32
    wide = (sums.shape[1] // steps, sums.shape[2])

    def rows_spec(array):
        return pl.BlockSpec((array.shape[0] // steps, array.shape[1]), lambda i: (i, 0))

    rows = [rows_spec(a) for a in arrays]
    return pl.pallas_call(
        lay_out_kernel,
        grid=(steps,),
        out_shape=tuple([jax.ShapeDtypeStruct(sums.shape[1:], f32)] * 4
                        + [jax.ShapeDtypeStruct(a.shape, a.dtype) for a in arrays]),
        in_specs=[pl.BlockSpec((4,) + wide, lambda i: (0, i, 0))] + rows,
        out_specs=tuple([pl.BlockSpec(wide, lambda i: (i, 0))] * 4 + rows),
        compiler_params=pltpu.CompilerParams(vmem_limit_bytes=60 * 2**20),
        name="lay_out",
    )(sums, *arrays)


def gathered(
    tokens,
    cotangent,
    lengths,
    routes,
    w_query,
    w_key,
    w_value,
    w_out,
    w_router,
    g_attn,
    g_ffn,
    g_query,
    g_key,
    w_gate,
    w_up,
    w_down,
):
    micro_count, _, seq_len, model_width = tokens.shape
    expert_count = w_router.shape[1]
    f32, bf = jnp.float32, jnp.bfloat16
    places = jnp.arange(seq_len)
    length = lengths[:, 0]
    live = places[None, :] < length[:, None]
    rows = micro_count * seq_len
    gains = jnp.pad(jnp.stack([g_attn, g_ffn, g_query, g_key]), ((0, EXTRA - expert_count - 4), (0, 0)))
    half = HDIM // 2
    angles = np.arange(seq_len)[:, None] * 10000.0 ** (-2.0 * np.arange(half) / HDIM)[None, :]
    cosine_table = np.concatenate([np.cos(angles)] * 2, axis=1).astype(np.float32)
    turned_sine = np.concatenate([-np.sin(angles), np.sin(angles)], axis=1).astype(np.float32)
    live_rows = jnp.broadcast_to(live.astype(f32).reshape(1, rows), (8, rows))
    route_ids = routes[:, 0].reshape(rows, -1)
    tokens_here = tokens[:, 0].reshape(rows, model_width)
    (query_raw, key_raw, query_low, key_low, value_low, squares, lives, mixed_low, hidden_state, ffn_in, router,
     small_rows, dy, rows_all, w_cols, out_full, spread_rows, dy_all, gate_far, up_far, down_far) = front(
        tokens_here, cotangent[:, 0].reshape(rows, model_width), live_rows, route_ids, cosine_table, turned_sine,
        w_router, gains,
        w_query, w_key, w_value, w_out, w_gate[0], w_up[0], w_down[0])
    expert_sums, *expert_grads = experts(
        spread_rows, dy_all, (w_gate[0], w_up[0], w_down[0]), (gate_far, up_far, down_far))
    mixed_out, grad_tokens, sums, small_sums = back(
        expert_sums.reshape(rows, -1), tokens_here, route_ids, cosine_table, turned_sine,
        dy.reshape(rows, model_width), mixed_low, query_raw, key_raw, query_low, key_low, value_low, squares, lives,
        hidden_state, ffn_in, router, small_rows, rows_all, w_cols, out_full)
    *sums, grad_gate, grad_up, grad_down, mixed_out, grad_tokens = lay_out(
        sums, *expert_grads, mixed_out, grad_tokens)
    return (
        mixed_out.reshape(micro_count, 1, seq_len, model_width),
        grad_tokens.reshape(micro_count, 1, seq_len, model_width),
        sums[0],
        sums[1],
        sums[2],
        sums[3],
        small_sums[:expert_count].T,
        small_sums[expert_count],
        small_sums[expert_count + 1],
        small_sums[expert_count + 2],
        small_sums[expert_count + 3],
        grad_gate[None],
        grad_up[None],
        grad_down[None],
    )


def dispatch_rows(buffer):
    return lax.all_to_all(buffer, ("expert", "shard"), split_axis=0, concat_axis=0, tiled=True)


def collect_rows(buffer):
    return lax.all_to_all(buffer, ("expert", "shard"), split_axis=0, concat_axis=0, tiled=True)


def dispatch_grads(buffer):
    return lax.all_to_all(buffer, ("expert", "shard"), split_axis=0, concat_axis=0, tiled=True)


def collect_grads(buffer):
    return lax.all_to_all(buffer, ("expert", "shard"), split_axis=0, concat_axis=0, tiled=True)


def to_experts(arrived, local_experts, capacity):
    sources = arrived.shape[0]
    model_width = arrived.shape[2]
    split_rows = arrived.reshape(sources, local_experts, capacity, model_width)
    return jnp.swapaxes(split_rows, 0, 1).reshape(local_experts, sources * capacity, model_width)


def from_experts(expert_token_rows, owners, capacity):
    local_experts = expert_token_rows.shape[0]
    model_width = expert_token_rows.shape[2]
    split_rows = expert_token_rows.reshape(local_experts, owners, capacity, model_width)
    return jnp.swapaxes(split_rows, 0, 1).reshape(owners, local_experts * capacity, model_width)


def exchanged(
    tokens,
    cotangent,
    lengths,
    routes,
    w_query,
    w_key,
    w_value,
    w_out,
    w_router,
    g_attn,
    g_ffn,
    g_query,
    g_key,
    w_gate,
    w_up,
    w_down,
):
    micro_count = tokens.shape[0]
    seq_len = tokens.shape[2]
    model_width = tokens.shape[3]
    top_count = routes.shape[3]
    expert_count = w_router.shape[1]
    local_experts = w_gate.shape[0]
    owners = expert_count // local_experts
    capacity = min(seq_len, max(2, 2 * seq_len * top_count // expert_count))
    slot_total = expert_count * capacity
    gate_weight_complete, up_weight_complete, down_weight_complete = (
        lax.all_gather(w_gate, "dp", axis=2, tiled=True),
        lax.all_gather(w_up, "dp", axis=2, tiled=True),
        lax.all_gather(w_down, "dp", axis=1, tiled=True),
    )
    cosine_table, sine_table = rope_tables(seq_len, HDIM)
    places = jnp.arange(seq_len)
    slot_ids = jnp.arange(slot_total)
    expert_ids = jnp.arange(expert_count)
    score_scale = HDIM ** (-0.5)
    grad_query = jnp.zeros((model_width, model_width), jnp.float32)
    grad_key = jnp.zeros((model_width, model_width), jnp.float32)
    grad_value = jnp.zeros((model_width, model_width), jnp.float32)
    grad_out = jnp.zeros((model_width, model_width), jnp.float32)
    grad_router = jnp.zeros((model_width, expert_count), jnp.float32)
    grad_gain_attn = jnp.zeros((model_width,), jnp.float32)
    grad_gain_ffn = jnp.zeros((model_width,), jnp.float32)
    grad_gain_query = jnp.zeros((model_width,), jnp.float32)
    grad_gain_key = jnp.zeros((model_width,), jnp.float32)
    grad_gate = jnp.zeros(gate_weight_complete.shape, jnp.float32)
    grad_up = jnp.zeros(up_weight_complete.shape, jnp.float32)
    grad_down = jnp.zeros(down_weight_complete.shape, jnp.float32)
    outs_mixed = []
    outs_grad = []
    for micro_step in range(micro_count):
        layer_set = (
            lax.all_gather(w_query, "shard", axis=0, tiled=True),
            lax.all_gather(w_key, "shard", axis=0, tiled=True),
            lax.all_gather(w_value, "shard", axis=0, tiled=True),
            lax.all_gather(w_out, "shard", axis=0, tiled=True),
            lax.all_gather(w_router, "shard", axis=0, tiled=True),
            lax.all_gather(g_attn, "shard", axis=0, tiled=True),
            lax.all_gather(g_ffn, "shard", axis=0, tiled=True),
            lax.all_gather(g_query, "shard", axis=0, tiled=True),
            lax.all_gather(g_key, "shard", axis=0, tiled=True),
        )
        query_full, key_full, value_full, out_full, route_full = (
            layer_set[0],
            layer_set[1],
            layer_set[2],
            layer_set[3],
            layer_set[4],
        )
        gain_attn = layer_set[5].astype(jnp.float32)
        gain_ffn = layer_set[6].astype(jnp.float32)
        gain_query = layer_set[7].astype(jnp.float32)
        gain_key = layer_set[8].astype(jnp.float32)
        inputs = tokens[micro_step, 0].astype(jnp.float32)
        length = lengths[micro_step, 0]
        route_ids = routes[micro_step, 0]
        normed = rms_norm(inputs, gain_attn).astype(jnp.bfloat16)
        query_raw = matmul(normed, query_full)
        key_raw = matmul(normed, key_full)
        value_raw = matmul(normed, value_full)
        value_low = value_raw.astype(jnp.bfloat16).reshape(seq_len, HEADS, HDIM)
        query_low = rotate(
            rms_norm(query_raw, gain_query).reshape(seq_len, HEADS, HDIM), cosine_table, sine_table
        ).astype(jnp.bfloat16)
        key_low = rotate(
            rms_norm(key_raw, gain_key).reshape(seq_len, HEADS, HDIM), cosine_table, sine_table
        ).astype(jnp.bfloat16)
        allowed = (places[None, :] <= places[:, None]) & (places[None, :] < length)
        scores = (
            jnp.einsum("qhd,khd->hqk", query_low, key_low, preferred_element_type=jnp.float32)
            * score_scale
        )
        attn_probs = softmax_rows(jnp.where(allowed[None], scores, -1e30))
        probs_low = attn_probs.astype(jnp.bfloat16)
        mixed_low = (
            jnp.einsum("hqk,khd->qhd", probs_low, value_low, preferred_element_type=jnp.float32)
            .reshape(seq_len, model_width)
            .astype(jnp.bfloat16)
        )
        attn_part = matmul(mixed_low, out_full)
        hidden_state = inputs + attn_part
        ffn_in = rms_norm(hidden_state, gain_ffn).astype(jnp.bfloat16)
        logits = matmul(ffn_in, route_full)
        router = softmax_rows(logits)
        chosen = route_ids[:, :, None] == expert_ids[None, None, :]
        gate_vals = jnp.sum(jnp.where(chosen, router[:, None, :], 0.0), axis=2)
        flat_chosen = chosen.reshape(seq_len * top_count, expert_count).astype(jnp.int32)
        before = jnp.cumsum(flat_chosen, axis=0) - flat_chosen
        slot_rank = jnp.sum(before * flat_chosen, axis=1)
        target = route_ids.reshape(-1) * capacity + slot_rank
        placing = (slot_ids[:, None] == target[None, :]).astype(jnp.bfloat16)
        token_placing = jnp.sum(placing.reshape(slot_total, seq_len, top_count), axis=2)
        outgoing = matmul(token_placing, ffn_in).astype(jnp.bfloat16)
        arrived = dispatch_rows(outgoing.reshape(owners, local_experts * capacity, model_width))
        expert_token_rows = to_experts(arrived, local_experts, capacity)
        gate_pre = jnp.einsum(
            "qjs,qsy->qjy",
            expert_token_rows,
            gate_weight_complete,
            preferred_element_type=jnp.float32,
        )
        up_value = jnp.einsum(
            "qjs,qsy->qjy",
            expert_token_rows,
            up_weight_complete,
            preferred_element_type=jnp.float32,
        )
        sigmoid_gate = jax.nn.sigmoid(gate_pre)
        activated = gate_pre * sigmoid_gate
        inner_activation = (activated * up_value).astype(jnp.bfloat16)
        expert_out = jnp.einsum(
            "aqc,aco->aqo",
            inner_activation,
            down_weight_complete,
            preferred_element_type=jnp.float32,
        ).astype(jnp.bfloat16)
        returned = collect_rows(from_experts(expert_out, owners, capacity)).reshape(
            slot_total, model_width
        )
        picked = (
            jnp.take(returned, target, axis=0)
            .astype(jnp.float32)
            .reshape(seq_len, top_count, model_width)
        )
        expert_sum = jnp.sum(picked * gate_vals[:, :, None], axis=1)
        outs_mixed.append((hidden_state + expert_sum).astype(jnp.bfloat16))
        live_mask = (places < length).astype(jnp.float32)
        d_output = cotangent[micro_step, 0].astype(jnp.float32) * live_mask[:, None]
        d_gates = jnp.sum(picked * d_output[:, None, :], axis=2)
        d_slots = (
            (gate_vals[:, :, None] * d_output[:, None, :])
            .astype(jnp.bfloat16)
            .reshape(seq_len * top_count, model_width)
        )
        d_outgoing = matmul(placing, d_slots).astype(jnp.bfloat16)
        d_arrived = dispatch_grads(
            d_outgoing.reshape(owners, local_experts * capacity, model_width)
        )
        expert_output_gradient = to_experts(d_arrived, local_experts, capacity)
        d_inner = jnp.einsum(
            "azy,ajy->azj",
            expert_output_gradient,
            down_weight_complete,
            preferred_element_type=jnp.float32,
        )
        grad_down = grad_down + jnp.einsum(
            "qti,qtj->qij",
            inner_activation,
            expert_output_gradient,
            preferred_element_type=jnp.float32,
        )
        gate_preactivation_gradient = (
            d_inner * up_value * (sigmoid_gate + gate_pre * sigmoid_gate * (1.0 - sigmoid_gate))
        ).astype(jnp.bfloat16)
        up_projection_value_gradient = (d_inner * activated).astype(jnp.bfloat16)
        grad_gate = grad_gate + jnp.einsum(
            "hzo,hzg->hog",
            expert_token_rows,
            gate_preactivation_gradient,
            preferred_element_type=jnp.float32,
        )
        grad_up = grad_up + jnp.einsum(
            "hzo,hzg->hog",
            expert_token_rows,
            up_projection_value_gradient,
            preferred_element_type=jnp.float32,
        )
        d_rows = jnp.einsum(
            "ing,itg->int",
            gate_preactivation_gradient,
            gate_weight_complete,
            preferred_element_type=jnp.float32,
        )
        d_rows = (
            d_rows
            + jnp.einsum(
                "ing,itg->int",
                up_projection_value_gradient,
                up_weight_complete,
                preferred_element_type=jnp.float32,
            )
        ).astype(jnp.bfloat16)
        d_returned = collect_grads(from_experts(d_rows, owners, capacity)).reshape(
            slot_total, model_width
        )
        d_ffn_in = jnp.sum(
            jnp.take(d_returned, target, axis=0)
            .astype(jnp.float32)
            .reshape(seq_len, top_count, model_width),
            axis=1,
        )
        d_router = jnp.sum(jnp.where(chosen, d_gates[:, :, None], 0.0), axis=1)
        d_logits = (router * (d_router - jnp.sum(router * d_router, axis=1, keepdims=True))).astype(
            jnp.bfloat16
        )
        grad_router = grad_router + transposed_times(ffn_in, d_logits)
        d_ffn_in = d_ffn_in + times_transposed(d_logits, route_full)
        d_hidden_norm, d_gain_ffn = norm_back(hidden_state, gain_ffn, d_ffn_in)
        grad_gain_ffn = grad_gain_ffn + d_gain_ffn
        d_hidden = d_output + d_hidden_norm
        d_attn_low = d_hidden.astype(jnp.bfloat16)
        grad_out = grad_out + transposed_times(mixed_low, d_attn_low)
        d_mixed_wide = times_transposed(d_attn_low, out_full)
        d_mixed = d_mixed_wide.astype(jnp.bfloat16).reshape(seq_len, HEADS, HDIM)
        d_probs = jnp.einsum("qhd,khd->hqk", d_mixed, value_low, preferred_element_type=jnp.float32)
        d_value = (
            jnp.einsum("hqk,qhd->khd", probs_low, d_mixed, preferred_element_type=jnp.float32)
            .reshape(seq_len, model_width)
            .astype(jnp.bfloat16)
        )
        d_scores = (
            attn_probs * (d_probs - jnp.sum(attn_probs * d_probs, axis=-1, keepdims=True))
        ).astype(jnp.bfloat16)
        d_query = (
            jnp.einsum("hqk,khd->qhd", d_scores, key_low, preferred_element_type=jnp.float32)
            * score_scale
        )
        d_key = (
            jnp.einsum("hqk,qhd->khd", d_scores, query_low, preferred_element_type=jnp.float32)
            * score_scale
        )
        d_query_raw, d_gain_query = norm_back(
            query_raw,
            gain_query,
            rotate_back(d_query, cosine_table, sine_table).reshape(seq_len, model_width),
        )
        d_key_raw, d_gain_key = norm_back(
            key_raw,
            gain_key,
            rotate_back(d_key, cosine_table, sine_table).reshape(seq_len, model_width),
        )
        grad_gain_query = grad_gain_query + d_gain_query
        grad_gain_key = grad_gain_key + d_gain_key
        d_query_low = d_query_raw.astype(jnp.bfloat16)
        d_key_low = d_key_raw.astype(jnp.bfloat16)
        grad_query = grad_query + transposed_times(normed, d_query_low)
        grad_key = grad_key + transposed_times(normed, d_key_low)
        grad_value = grad_value + transposed_times(normed, d_value)
        d_normed = (
            times_transposed(d_query_low, query_full)
            + times_transposed(d_key_low, key_full)
            + times_transposed(d_value, value_full)
        )
        d_input_norm, d_gain_attn = norm_back(inputs, gain_attn, d_normed)
        grad_gain_attn = grad_gain_attn + d_gain_attn
        outs_grad.append(d_hidden + d_input_norm)
    layer_sums = (
        lax.psum_scatter(
            grad_query.astype(jnp.bfloat16), "shard", scatter_dimension=0, tiled=True
        ).astype(jnp.float32),
        lax.psum_scatter(
            grad_key.astype(jnp.bfloat16), "shard", scatter_dimension=0, tiled=True
        ).astype(jnp.float32),
        lax.psum_scatter(
            grad_value.astype(jnp.bfloat16), "shard", scatter_dimension=0, tiled=True
        ).astype(jnp.float32),
        lax.psum_scatter(
            grad_out.astype(jnp.bfloat16), "shard", scatter_dimension=0, tiled=True
        ).astype(jnp.float32),
        lax.psum_scatter(
            grad_router.astype(jnp.bfloat16), "shard", scatter_dimension=0, tiled=True
        ).astype(jnp.float32),
        lax.psum_scatter(
            grad_gain_attn.astype(jnp.bfloat16), "shard", scatter_dimension=0, tiled=True
        ).astype(jnp.float32),
        lax.psum_scatter(
            grad_gain_ffn.astype(jnp.bfloat16), "shard", scatter_dimension=0, tiled=True
        ).astype(jnp.float32),
        lax.psum_scatter(
            grad_gain_query.astype(jnp.bfloat16), "shard", scatter_dimension=0, tiled=True
        ).astype(jnp.float32),
        lax.psum_scatter(
            grad_gain_key.astype(jnp.bfloat16), "shard", scatter_dimension=0, tiled=True
        ).astype(jnp.float32),
    )
    layer_totals = (
        lax.psum(layer_sums[0].astype(jnp.bfloat16), ("dp", "expert")).astype(jnp.float32),
        lax.psum(layer_sums[1].astype(jnp.bfloat16), ("dp", "expert")).astype(jnp.float32),
        lax.psum(layer_sums[2].astype(jnp.bfloat16), ("dp", "expert")).astype(jnp.float32),
        lax.psum(layer_sums[3].astype(jnp.bfloat16), ("dp", "expert")).astype(jnp.float32),
        lax.psum(layer_sums[4].astype(jnp.bfloat16), ("dp", "expert")).astype(jnp.float32),
        lax.psum(layer_sums[5].astype(jnp.bfloat16), ("dp", "expert")).astype(jnp.float32),
        lax.psum(layer_sums[6].astype(jnp.bfloat16), ("dp", "expert")).astype(jnp.float32),
        lax.psum(layer_sums[7].astype(jnp.bfloat16), ("dp", "expert")).astype(jnp.float32),
        lax.psum(layer_sums[8].astype(jnp.bfloat16), ("dp", "expert")).astype(jnp.float32),
    )
    expert_totals = (
        lax.psum_scatter(
            grad_gate.astype(jnp.bfloat16), "dp", scatter_dimension=2, tiled=True
        ).astype(jnp.float32),
        lax.psum_scatter(
            grad_up.astype(jnp.bfloat16), "dp", scatter_dimension=2, tiled=True
        ).astype(jnp.float32),
        lax.psum_scatter(
            grad_down.astype(jnp.bfloat16), "dp", scatter_dimension=1, tiled=True
        ).astype(jnp.float32),
    )
    mixed_out = jnp.stack(outs_mixed)[:, None]
    grad_tokens = jnp.stack(outs_grad)[:, None]
    return (
        mixed_out,
        grad_tokens,
        layer_totals[0],
        layer_totals[1],
        layer_totals[2],
        layer_totals[3],
        layer_totals[4],
        layer_totals[5],
        layer_totals[6],
        layer_totals[7],
        layer_totals[8],
        expert_totals[0],
        expert_totals[1],
        expert_totals[2],
    )


def solution(mesh):
    placed = (
        P(None, ("dp", "expert", "shard"), None, None),
        P(None, ("dp", "expert", "shard"), None, None),
        P(None, ("dp", "expert", "shard")),
        P(None, ("dp", "expert", "shard"), None, None),
        P("shard", None),
        P("shard", None),
        P("shard", None),
        P("shard", None),
        P("shard", None),
        P("shard"),
        P("shard"),
        P("shard"),
        P("shard"),
        P(("expert", "shard"), None, "dp"),
        P(("expert", "shard"), None, "dp"),
        P(("expert", "shard"), "dp", None),
    )
    sizes = (mesh.shape["dp"], mesh.shape["expert"], mesh.shape["shard"])
    return jax.shard_map(
        gathered if sizes == (2, 4, 4) else exchanged,
        mesh=mesh,
        in_specs=placed,
        out_specs=(
            P(None, ("dp", "expert", "shard"), None, None),
            P(None, ("dp", "expert", "shard"), None, None),
            P("shard", None),
            P("shard", None),
            P("shard", None),
            P("shard", None),
            P("shard", None),
            P("shard"),
            P("shard"),
            P("shard"),
            P("shard"),
            P(("expert", "shard"), None, "dp"),
            P(("expert", "shard"), None, "dp"),
            P(("expert", "shard"), "dp", None),
        ),
        check_vma=False,
    )
```
